32 devices in a mesh: parts: 2 (over x), store: 16 (over z, y, core).
Axes of the slice: x: 2, y: 2, z: 4, core: 2. Of those that a mesh axis runs over, the one named last changes fastest.
Arguments:
- store_feats: bfloat16 [131072, 256], P(('parts', 'store')), parts along dimension 0
- requests: int32 [512, 8], P(('parts', 'store')), parts along dimension 0, may hold values from 0 to 4095, as said below
- node_slots: int32 [128, 256], P(('parts', 'store')), parts along dimension 0, may hold values from 0 to 127, as said below
- edges: int32 [128, 1024, 2], P(('parts', 'store')), parts along dimension 0, may hold values from 0 to 255
- pairs: int32 [128, 64, 2], P(('parts', 'store')), parts along dimension 0, may hold values from 0 to 255
- targets: float32 [128, 64], P(('parts', 'store')), parts along dimension 0, may hold values from -6 to 6
- w_qkv: bfloat16 [256, 768], replicated, may hold values from -0.375 to 0.375
- w_o: bfloat16 [256, 256], replicated, may hold values from -0.375 to 0.375
- w_msg: bfloat16 [256, 256], replicated, may hold values from -0.375 to 0.375
- w_up: bfloat16 [256, 512], replicated, may hold values from -0.375 to 0.375
- w_down: bfloat16 [512, 256], replicated, may hold values from -0.25 to 0.25
- w_read: float32 [256], replicated, may hold values from -0.375 to 0.375
Outputs:
- preds: float32 [128, 64], P(('parts', 'store')), parts along dimension 0
- loss: float32 [2], P('parts'), parts along dimension 0
- g_qkv: float32 [512, 768], P(('parts', 'store')), parts along dimension 0
- g_o: float32 [512, 256], P(('parts', 'store')), parts along dimension 0
- g_msg: float32 [512, 256], P(('parts', 'store')), parts along dimension 0
- g_up: float32 [512, 512], P(('parts', 'store')), parts along dimension 0
- g_down: float32 [1024, 256], P(('parts', 'store')), parts along dimension 0
The draws below stay inside these ranges and needn't reach their ends.
There are 2 independent parts, one for each index of `parts`. The reference program is written for one: setup_inputs(seed, part) draws one part's arguments, and reference() takes and returns one part's arrays. A program takes and returns all parts, laid end to end along the dimension named above; an argument that names none is the same for every part. Nothing has to cross between parts.
Inputs may be any that keep to these rules, and one draw needn't show every extreme that they name: Each row of requests starts with 1 to 8 distinct row numbers and holds zeros after them; every device fetches 8 rows from some owner, and some owner serves 8 rows to every device. `node_slots`: A node's slot o * 8 + c always names one of the leading entries c (those before the zero padding; a leading entry may itself be row 0) of the request row of owner o on the subgraph's device.
All inputs are finite; a program needn't handle non-finite values.
Results may differ from the reference program's by a relative error of at most 0.015.
The reference program's roundings to bfloat16 on the way count: a program that leaves them out, or rounds other values in their place, can miss the bound.
Values may be sent and summed in bfloat16 or wider, within the bound.
No kernel may reach another device: no remote copies, remote signals or barrier semaphores. Data moves between devices by JAX's collectives and lax.ppermute only.
A program may use at most 128 MiB of HBM per device.

```python
import jax
import jax.numpy as jnp
from jax import lax

F = 256
FF = 512
S = 256
E = 1024
P_SIZE = 64
SUB_DEV = 4
CAP = 8
ROWS_DEV = 4096
NODES = 65536
SUBS = 64
N_STORE = 16


def request_plan(key):
    k_hot = jax.random.fold_in(key, 101)
    k_raw = jax.random.fold_in(key, 102)
    k_full = jax.random.fold_in(key, 103)
    k_busy = jax.random.fold_in(key, 104)
    k_order = jax.random.fold_in(key, 105)
    hot = jax.random.randint(k_hot, (N_STORE,), 2, 6)
    span = jnp.minimum(CAP, CAP * hot // 4)
    raw = jax.random.randint(k_raw, (N_STORE, N_STORE), 0, 1 << 20)
    counts = 1 + raw % span[None, :]
    owners = jnp.arange(N_STORE, dtype=jnp.int32)
    full_owner = jax.random.randint(k_full, (N_STORE,), 0, N_STORE)
    busy = jax.random.randint(k_busy, (), 0, N_STORE)
    counts = jnp.where(owners[None, :] == full_owner[:, None], CAP, counts)
    counts = jnp.where(owners[None, :] == busy, CAP, counts)
    band = ROWS_DEV // CAP
    slot = jnp.arange(CAP, dtype=jnp.int32)
    jitter = jax.random.randint(k_order, (N_STORE, N_STORE, CAP), 0, band)
    order = (slot[None, None, :] * band + jitter).astype(jnp.int32)
    wanted = jnp.where(slot[None, None, :] < counts[:, :, None], order, 0)
    return (counts, wanted.reshape(N_STORE * N_STORE, CAP).astype(jnp.int32))


def draw_requests(key, part):
    counts, wanted = request_plan(key)
    return wanted


def draw_node_slots(key, part):
    counts, wanted = request_plan(key)
    k_owner = jax.random.fold_in(key, 201)
    k_slot = jax.random.fold_in(key, 202)
    owner = jax.random.randint(k_owner, (N_STORE, SUB_DEV * S), 0, N_STORE)
    limit = jnp.take_along_axis(counts, owner, axis=1)
    pick = jax.random.randint(k_slot, (N_STORE, SUB_DEV * S), 0, limit)
    return (owner * CAP + pick).reshape(N_STORE * SUB_DEV, S).astype(jnp.int32)


def draw_store_feats(key, part):
    k_val = jax.random.fold_in(key, 301)
    values = jnp.clip(jax.random.normal(k_val, (NODES, F), jnp.float32), -6.0, 6.0)
    return values.astype(jnp.bfloat16)


def plant(values, own_key, low, largest):
    longest = values.shape.index(max(values.shape))
    spots = []
    for shift in (0, 1):
        where = [jax.random.randint(jax.random.fold_in(own_key, axis), (), 0, length) for axis, length in enumerate(values.shape)]
        where[longest] = (where[longest] + shift) % values.shape[longest]
        spots.append(tuple(where))
    return values.at[spots[0]].set(low).at[spots[1]].set(largest)


def shard_levels(key, dims, cuts, low, largest):
    def one(position, blocks):
        steps = jax.random.uniform(jax.random.fold_in(jax.random.fold_in(key, 6), position), (blocks,), jnp.float32, low / len(cuts), largest / len(cuts))
        return jnp.repeat(jnp.exp(steps), dims[position] // blocks).reshape((-1,) + (1,) * (len(dims) - position - 1))

    gain = one(*cuts[0])
    for cut in cuts[1:]:
        gain = gain * one(*cut)
    return gain


def gaussian(key, dims, deviation, reach, shards=(), held_as=jnp.bfloat16):
    drawn = deviation * jax.random.normal(key, dims, jnp.float32)
    if shards:
        drawn = drawn * shard_levels(key, dims, shards, -0.22, 0.18)
    return jnp.clip(drawn, -reach, reach).astype(held_as)


def setup_inputs(seed: int = 0, part: int = 0) -> dict:
    seeds = jax.random.split(jax.random.key(seed), 13)
    part_keys = jax.random.split(jax.random.fold_in(seeds[12], part), 13)
    store_feats = draw_store_feats(jax.random.fold_in(jax.random.fold_in(seeds[12], part), 71), part)
    requests = draw_requests(jax.random.fold_in(jax.random.fold_in(seeds[12], part), 71), part)
    node_slots = draw_node_slots(jax.random.fold_in(jax.random.fold_in(seeds[12], part), 71), part)
    edges = plant(jax.random.randint(part_keys[3], (SUBS, E, 2), 0, S), jax.random.fold_in(part_keys[3], 1), 0, S - 1).astype(jnp.int32)
    pairs = plant(jax.random.randint(part_keys[4], (SUBS, P_SIZE, 2), 0, S), jax.random.fold_in(part_keys[4], 1), 0, S - 1).astype(jnp.int32)
    targets = gaussian(part_keys[5], (SUBS, P_SIZE), 1.0, 6.0, ((0, 16),), jnp.float32)
    w_qkv = gaussian(seeds[6], (F, 3 * F), F ** -0.5, 0.375)
    w_o = gaussian(seeds[7], (F, F), F ** -0.5, 0.375)
    w_msg = gaussian(seeds[8], (F, F), F ** -0.5, 0.375)
    w_up = gaussian(seeds[9], (F, FF), F ** -0.5, 0.375)
    w_down = gaussian(seeds[10], (FF, F), FF ** -0.5, 0.25)
    w_read = gaussian(seeds[11], (F,), F ** -0.5, 0.375, (), jnp.float32)
    return {"store_feats": store_feats, "requests": requests, "node_slots": node_slots, "edges": edges, "pairs": pairs, "targets": targets, "w_qkv": w_qkv, "w_o": w_o, "w_msg": w_msg, "w_up": w_up, "w_down": w_down, "w_read": w_read}


def layer_norm(value):
    mean = lax.optimization_barrier(jnp.mean(value, axis=-1, keepdims=True))
    centred = value - mean
    var = lax.optimization_barrier(jnp.mean(centred * centred, axis=-1, keepdims=True))
    return centred * lax.rsqrt(var + 1e-05)

def adjacency(edges, width):
    iota = jnp.arange(width, dtype=jnp.int32)
    src_hot = (edges[:, :, 0][:, :, None] == iota).astype(jnp.bfloat16)
    dst_hot = (edges[:, :, 1][:, :, None] == iota).astype(jnp.bfloat16)
    counts = jnp.einsum('bei,bej->bij', dst_hot, src_hot, preferred_element_type=jnp.float32)
    deg_inv = 1.0 / (1.0 + lax.optimization_barrier(jnp.sum(counts, axis=-1)))
    return (counts.astype(jnp.bfloat16), deg_inv)

def objective_of(x_nodes, adj, deg_inv, pairs, targets, w_read, w_qkv, w_o, w_msg, w_up, w_down):
    batch, width, feats = x_nodes.shape
    heads = 8 if feats % 8 == 0 else 1
    head_dim = feats // heads
    flat = x_nodes.reshape(batch * width, feats)
    qkv = jnp.dot(flat, w_qkv, preferred_element_type=jnp.float32).astype(jnp.bfloat16)
    qkv = qkv.reshape(batch, width, 3, heads, head_dim)
    query, keys, values = (qkv[:, :, 0], qkv[:, :, 1], qkv[:, :, 2])
    scores = jnp.einsum('bqhd,bkhd->bhqk', query, keys, preferred_element_type=jnp.float32) * head_dim ** (-0.5)
    top = lax.optimization_barrier(jnp.max(scores, axis=-1, keepdims=True))
    expo = jnp.exp(scores - top)
    probs = (expo / lax.optimization_barrier(jnp.sum(expo, axis=-1, keepdims=True))).astype(jnp.bfloat16)
    att = jnp.einsum('bhqk,bkhd->bqhd', probs, values, preferred_element_type=jnp.float32).astype(jnp.bfloat16)
    attn_out = jnp.dot(att.reshape(batch * width, feats), w_o, preferred_element_type=jnp.float32)
    xw = jnp.dot(flat, w_msg, preferred_element_type=jnp.float32).astype(jnp.bfloat16).reshape(batch, width, feats)
    agg = (jnp.einsum('bij,bjf->bif', adj, xw, preferred_element_type=jnp.float32) + xw.astype(jnp.float32)) * deg_inv[:, :, None]
    base = flat.astype(jnp.float32)
    hidden_h = (layer_norm(base + jax.nn.relu(agg.reshape(batch * width, feats))) + layer_norm(base + attn_out)).astype(jnp.bfloat16)
    upper = jnp.dot(hidden_h, w_up, preferred_element_type=jnp.float32)
    gated = jax.nn.gelu(upper, approximate=True).astype(jnp.bfloat16)
    mixed = jnp.dot(gated, w_down, preferred_element_type=jnp.float32)
    out = layer_norm(hidden_h.astype(jnp.float32) + mixed).reshape(batch, width, feats)
    left = jnp.take_along_axis(out, pairs[:, :, 0][:, :, None], axis=1)
    right = jnp.take_along_axis(out, pairs[:, :, 1][:, :, None], axis=1)
    preds = lax.optimization_barrier(jnp.sum(left * right * w_read, axis=-1))
    diff = preds - targets
    objective = jnp.sum(diff * diff) / (batch * pairs.shape[1])
    return (objective, preds)

def local_step(x_nodes, edges, pairs, targets, w_read, weights):
    adj, deg_inv = adjacency(edges, x_nodes.shape[1])

    def wrapped(w_qkv, w_o, w_msg, w_up, w_down):
        return objective_of(x_nodes, adj, deg_inv, pairs, targets, w_read, w_qkv, w_o, w_msg, w_up, w_down)
    objective, pullback, preds = jax.vjp(wrapped, *weights, has_aux=True)
    grads = pullback(jnp.ones((), objective.dtype))
    return (objective, preds, grads)

def reference(store_feats, requests, node_slots, edges, pairs, targets, w_qkv, w_o, w_msg, w_up, w_down, w_read):
    weights = (w_qkv, w_o, w_msg, w_up, w_down)
    store3 = store_feats.reshape(N_STORE, ROWS_DEV, F)

    def per_device(device):
        wanted = lax.dynamic_slice_in_dim(requests, (device * N_STORE).astype(jnp.int32), N_STORE, 0)
        fetched = jnp.take_along_axis(store3, wanted[:, :, None], axis=1).reshape(N_STORE * CAP, F)
        start = (device * SUB_DEV).astype(jnp.int32)
        slots = lax.dynamic_slice_in_dim(node_slots, start, SUB_DEV, 0)
        x_nodes = jnp.take(fetched, slots, axis=0)
        objective, preds, grads = local_step(x_nodes, lax.dynamic_slice_in_dim(edges, start, SUB_DEV, 0), lax.dynamic_slice_in_dim(pairs, start, SUB_DEV, 0), lax.dynamic_slice_in_dim(targets, start, SUB_DEV, 0), w_read, weights)
        return (objective, preds, grads)
    objectives, preds, grads = lax.map(per_device, jnp.arange(N_STORE, dtype=jnp.int32))
    totals = tuple((lax.optimization_barrier(jnp.sum(g.astype(jnp.float32), axis=0)) for g in grads))
    loss = (jnp.sum(objectives) / N_STORE).reshape(1)
    return (preds.reshape(SUBS, P_SIZE), loss, totals[0], totals[1], totals[2], totals[3], totals[4])
```

```python
import jax
import jax.numpy as jnp
from jax import lax
from jax.experimental import pallas as pl
from jax.experimental.pallas import tpu as pltpu
from jax.sharding import PartitionSpec as P

HEADS = 8
BF = jnp.bfloat16
F32 = jnp.float32


def _nn(a, b):
    return lax.dot_general(a, b, (((1,), (0,)), ((), ())), preferred_element_type=F32)


def _nt(a, b):
    return lax.dot_general(a, b, (((1,), (1,)), ((), ())), preferred_element_type=F32)


def _tn(a, b):
    return lax.dot_general(a, b, (((0,), (0,)), ((), ())), preferred_element_type=F32)


def _split(v):
    hi = v.astype(BF)
    lo = (v - hi.astype(F32)).astype(BF)
    return hi, lo


def _norm(v):
    c = v - jnp.mean(v, axis=0, keepdims=True)
    r = lax.rsqrt(jnp.mean(c * c, axis=0, keepdims=True) + 1e-05)
    return c * r, r


def _norm_back(d, y, r):
    m1 = jnp.mean(d, axis=0, keepdims=True)
    m2 = jnp.mean(d * y, axis=0, keepdims=True)
    return (d - m1 - y * m2) * r


GELU_C = 0.7978845608028654
GELU_A = 0.044715
LOG2E = 1.4426950408889634


def _step_kernel(
    slots_ref, edges_ref, pairs_ref, targets_ref, fetched_ref,
    wqkv_ref, wo_ref, wmsg_ref, wup_ref, wdown_ref, wread_ref,
    preds_ref, obj_ref, gqkv_ref, go_ref, gmsg_ref, gup_ref, gdown_ref,
    wqmT, woT, wupT, wdownT, fetT, wcol, pf_s, y_s, dy_s, att_s,
    acc_qm, acc_o, acc_up, acc_down,
):
    b = pl.program_id(0)
    subs = pl.num_programs(0)
    feats = wo_ref.shape[0]
    nodes = slots_ref.shape[1]
    rows = fetched_ref.shape[0]
    n_edges = edges_ref.shape[2]
    n_pairs = pairs_ref.shape[2]
    hd = feats // HEADS
    scale = hd ** -0.5
    n_all = subs_static(preds_ref) * n_pairs

    @pl.when(b == 0)
    def _():
        wqmT[0 : 3 * feats, :] = wqkv_ref[...].T
        wqmT[3 * feats : 4 * feats, :] = wmsg_ref[...].T
        woT[...] = wo_ref[...].T
        wupT[...] = wup_ref[...].T
        wdownT[...] = wdown_ref[...].T
        fetT[...] = fetched_ref[...].T
        wcol[...] = jnp.broadcast_to(wread_ref[...], (2 * n_pairs, feats)).T
        acc_qm[...] = jnp.zeros_like(acc_qm)
        acc_o[...] = jnp.zeros_like(acc_o)
        acc_up[...] = jnp.zeros_like(acc_up)
        acc_down[...] = jnp.zeros_like(acc_down)
        obj_ref[...] = jnp.zeros_like(obj_ref)

    slot = slots_ref[pl.ds(b, 1), :]
    pick = (lax.broadcasted_iota(jnp.int32, (rows, nodes), 0) == slot).astype(F32).astype(BF)
    xT = _nn(fetT[...], pick).astype(BF)
    base = xT.astype(F32)
    y_s[...] = _nn(wqmT[...], xT).astype(BF)
    src = edges_ref[0, 0:1, :]
    dst = edges_ref[0, 1:2, :]
    it = lax.broadcasted_iota(jnp.int32, (nodes, n_edges), 0)
    srcT = (it == src).astype(F32).astype(BF)
    dstT = (it == dst).astype(F32).astype(BF)
    cnt = _nt(srcT, dstT)
    deg_inv = 1.0 / (1.0 + jnp.sum(cnt, axis=0, keepdims=True))
    adjT = cnt.astype(BF)
    xw = y_s[3 * feats : 4 * feats, :]
    agg = (_nn(xw, adjT) + xw.astype(F32)) * deg_inv
    for h in range(HEADS):
        qT = y_s[h * hd : (h + 1) * hd, :]
        kT = y_s[feats + h * hd : feats + (h + 1) * hd, :]
        vT = y_s[2 * feats + h * hd : 2 * feats + (h + 1) * hd, :]
        s = _tn(kT, qT)
        e = jnp.exp2((s - jnp.max(s, axis=0, keepdims=True)) * (scale * LOG2E))
        pf = e * (1.0 / jnp.sum(e, axis=0, keepdims=True))
        pf_s[h] = pf
        att_s[h * hd : (h + 1) * hd, :] = _nn(vT, pf.astype(BF)).astype(BF)
    attT = att_s[...]
    n1, r1 = _norm(base + jnp.maximum(agg, 0.0))
    n2, r2 = _norm(base + _nn(woT[...], attT))
    hT = (n1 + n2).astype(BF)
    up = _nn(wupT[...], hT)
    th = jnp.tanh(GELU_C * (up + GELU_A * (up * up * up)))
    half = 0.5 * (1.0 + th)
    gT = (up * half).astype(BF)
    dgelu = half + 0.5 * up * (1.0 - th * th) * (GELU_C * (1.0 + (3.0 * GELU_A) * (up * up)))
    out, r3 = _norm(hT.astype(F32) + _nn(wdownT[...], gT))
    prs = jnp.concatenate([pairs_ref[0, 0:1, :], pairs_ref[0, 1:2, :]], axis=1)
    hot = (lax.broadcasted_iota(jnp.int32, (nodes, 2 * n_pairs), 0) == prs).astype(F32).astype(BF)
    hi, lo = _split(out)
    lr = _nn(hi, hot) + _nn(lo, hot)
    rl = pltpu.roll(lr, n_pairs, 1) * wcol[...]
    preds = jnp.sum(lr * rl, axis=0, keepdims=True)
    tgt = targets_ref[pl.ds(b, 1), :]
    diff = preds - jnp.concatenate([tgt, tgt], axis=1)
    preds_ref[pl.ds(b, 1), :] = preds[:, 0:n_pairs]
    sq = diff[:, 0:n_pairs] * diff[:, 0:n_pairs]
    obj_ref[...] += jnp.broadcast_to(jnp.sum(sq, axis=1, keepdims=True) / n_all, obj_ref.shape)
    dlr = (diff * (2.0 / n_all)) * rl
    hi, lo = _split(dlr)
    dout = _nt(hi, hot) + _nt(lo, hot)
    do = _norm_back(dout, out, r3).astype(BF)
    dg = _nn(wdown_ref[...], do).astype(BF)
    acc_down[...] += _nt(gT, do)
    dup = (dgelu * dg.astype(F32)).astype(BF)
    acc_up[...] += _nt(hT, dup)
    dh = _nn(wup_ref[...], dup).astype(BF)
    dl = (do.astype(F32) + dh.astype(F32)).astype(BF).astype(F32)
    dagg = jnp.where(agg > 0.0, _norm_back(dl, n1, r1), 0.0) * deg_inv
    dagg = dagg.astype(BF)
    dxw = _nt(dagg, adjT).astype(BF)
    dy_s[3 * feats : 4 * feats, :] = (dxw.astype(F32) + dagg.astype(F32)).astype(BF)
    da = _norm_back(dl, n2, r2).astype(BF)
    acc_o[...] += _nt(attT, da)
    datt = _nn(wo_ref[...], da).astype(BF)
    for h in range(HEADS):
        qT = y_s[h * hd : (h + 1) * hd, :]
        kT = y_s[feats + h * hd : feats + (h + 1) * hd, :]
        vT = y_s[2 * feats + h * hd : 2 * feats + (h + 1) * hd, :]
        dh_ = datt[h * hd : (h + 1) * hd, :]
        pf = pf_s[h]
        dp = _tn(vT, dh_).astype(BF).astype(F32)
        dv = _nt(dh_, pf.astype(BF)).astype(BF)
        t = dp * pf
        ds = ((t - pf * jnp.sum(t, axis=0, keepdims=True)) * scale).astype(BF)
        dy_s[h * hd : (h + 1) * hd, :] = _nn(kT, ds).astype(BF)
        dy_s[feats + h * hd : feats + (h + 1) * hd, :] = _nt(qT, ds).astype(BF)
        dy_s[2 * feats + h * hd : 2 * feats + (h + 1) * hd, :] = dv
    acc_qm[...] += _nt(xT, dy_s[...])

    @pl.when(b == subs - 1)
    def _():
        gqkv_ref[...] = acc_qm[:, 0 : 3 * feats].astype(BF)
        gmsg_ref[...] = acc_qm[:, 3 * feats : 4 * feats].astype(BF)
        go_ref[...] = acc_o[...].astype(BF)
        gup_ref[...] = acc_up[...].astype(BF)
        gdown_ref[...] = acc_down[...].astype(BF)


def subs_static(ref):
    return ref.shape[0]


def local_step(fetched, node_slots, edges, pairs, targets, w_qkv, w_o, w_msg, w_up, w_down, w_read):
    subs, nodes = node_slots.shape
    rows, feats = fetched.shape
    hidden = w_up.shape[1]
    n_edges = edges.shape[1]
    n_pairs = pairs.shape[1]

    def whole(shape):
        return pl.BlockSpec(shape, lambda b: (0,) * len(shape))

    return pl.pallas_call(
        _step_kernel,
        grid=(subs,),
        in_specs=[
            whole((subs, nodes)),
            pl.BlockSpec((1, 2, n_edges), lambda b: (b, 0, 0)),
            pl.BlockSpec((1, 2, n_pairs), lambda b: (b, 0, 0)),
            whole((subs, n_pairs)),
            whole((rows, feats)),
            whole((feats, 3 * feats)),
            whole((feats, feats)),
            whole((feats, feats)),
            whole((feats, hidden)),
            whole((hidden, feats)),
            whole((1, feats)),
        ],
        out_specs=[
            whole((subs, n_pairs)),
            whole((8, 128)),
            whole((feats, 3 * feats)),
            whole((feats, feats)),
            whole((feats, feats)),
            whole((feats, hidden)),
            whole((hidden, feats)),
        ],
        out_shape=[
            jax.ShapeDtypeStruct((subs, n_pairs), F32),
            jax.ShapeDtypeStruct((8, 128), F32),
            jax.ShapeDtypeStruct((feats, 3 * feats), BF),
            jax.ShapeDtypeStruct((feats, feats), BF),
            jax.ShapeDtypeStruct((feats, feats), BF),
            jax.ShapeDtypeStruct((feats, hidden), BF),
            jax.ShapeDtypeStruct((hidden, feats), BF),
        ],
        scratch_shapes=[
            pltpu.VMEM((4 * feats, feats), BF),
            pltpu.VMEM((feats, feats), BF),
            pltpu.VMEM((hidden, feats), BF),
            pltpu.VMEM((feats, hidden), BF),
            pltpu.VMEM((feats, rows), BF),
            pltpu.VMEM((feats, 2 * n_pairs), F32),
            pltpu.VMEM((HEADS, nodes, nodes), F32),
            pltpu.VMEM((4 * feats, nodes), BF),
            pltpu.VMEM((4 * feats, nodes), BF),
            pltpu.VMEM((feats, nodes), BF),
            pltpu.VMEM((feats, 4 * feats), F32),
            pltpu.VMEM((feats, feats), F32),
            pltpu.VMEM((feats, hidden), F32),
            pltpu.VMEM((hidden, feats), F32),
        ],
        compiler_params=pltpu.CompilerParams(
            dimension_semantics=("arbitrary",), vmem_limit_bytes=48 << 20
        ),
        name="graph_step",
    )(
        node_slots, edges.transpose(0, 2, 1), pairs.transpose(0, 2, 1), targets, fetched,
        w_qkv, w_o, w_msg, w_up, w_down, w_read.reshape(1, feats),
    )


def _halving(parts, obj, groups):
    idx = lax.axis_index("store")
    bits = groups.bit_length() - 1
    c = jnp.concatenate(parts, axis=2)
    tail = c.shape[1:]
    y = c.reshape((2,) * bits + tail)
    for b in range(bits):
        ax = bits - 1 - b
        bit = (idx >> b) & 1
        perm = [(i, i ^ (1 << b)) for i in range(groups)]
        send = lax.dynamic_slice_in_dim(y, 1 - bit, 1, ax).astype(BF)
        got = lax.ppermute(send, "store", perm)
        obj = obj + lax.ppermute(obj, "store", perm)
        y = lax.dynamic_slice_in_dim(y, bit, 1, ax).astype(F32) + got.astype(F32)
    return y.reshape(tail), obj


def shards(
    store_feats, requests, node_slots, edges, pairs, targets,
    w_qkv, w_o, w_msg, w_up, w_down, w_read,
):
    feats = store_feats.shape[1]
    groups = lax.axis_size("store")
    picked = jnp.take(
        store_feats,
        lax.all_to_all(requests, "store", split_axis=0, concat_axis=0, tiled=True),
        axis=0,
        mode="clip",
    )
    fetched = lax.all_to_all(picked, "store", split_axis=0, concat_axis=0, tiled=True)
    preds, obj, *grads = local_step(
        fetched.reshape(-1, feats), node_slots, edges, pairs, targets,
        w_qkv, w_o, w_msg, w_up, w_down, w_read,
    )
    power = groups & (groups - 1) == 0
    if power and all(g.shape[0] % groups == 0 for g in grads):
        rows = feats // groups
        parts = [g.reshape(groups, -1, g.shape[1]) for g in grads]
        split = []
        for p in parts:
            split += [p[:, i : i + rows] for i in range(0, p.shape[1], rows)]
        total, obj = _halving(split, obj, groups)
        at, shares = 0, []
        for p in parts:
            pieces = []
            for _ in range(0, p.shape[1], rows):
                pieces.append(total[:, at : at + p.shape[2]])
                at += p.shape[2]
            shares.append(pieces[0] if len(pieces) == 1 else jnp.concatenate(pieces, axis=0))
        total_obj = obj[0, 0]
    else:
        shares = [
            lax.psum_scatter(g.astype(F32), "store", scatter_dimension=0, tiled=True)
            for g in grads
        ]
        total_obj = lax.psum(obj[0, 0], "store")
    loss = (total_obj / groups).reshape(1)
    return (preds, loss, *shares)


def solution(mesh):
    rows = P(("parts", "store"), None)
    deep = P(("parts", "store"), None, None)
    in_specs = (rows, rows, rows, deep, deep, rows, P(), P(), P(), P(), P(), P())
    out_specs = (rows, P("parts"), rows, rows, rows, rows, rows)
    return jax.shard_map(shards, mesh=mesh, in_specs=in_specs, out_specs=out_specs, check_vma=False)
```

```python
import jax
import jax.numpy as jnp
from jax import lax
from jax.experimental import pallas as pl
from jax.experimental.pallas import tpu as pltpu
from jax.sharding import PartitionSpec as P

HEADS = 8
BF = jnp.bfloat16
F32 = jnp.float32


def _nn(a, b):
    return lax.dot_general(a, b, (((1,), (0,)), ((), ())), preferred_element_type=F32)


def _nt(a, b):
    return lax.dot_general(a, b, (((1,), (1,)), ((), ())), preferred_element_type=F32)


def _tn(a, b):
    return lax.dot_general(a, b, (((0,), (0,)), ((), ())), preferred_element_type=F32)


def _split(v):
    hi = v.astype(BF)
    lo = (v - hi.astype(F32)).astype(BF)
    return hi, lo


def _norm(v):
    c = v - jnp.mean(v, axis=0, keepdims=True)
    r = lax.rsqrt(jnp.mean(c * c, axis=0, keepdims=True) + 1e-05)
    return c * r, r


def _norm_back(d, y, r):
    m1 = jnp.mean(d, axis=0, keepdims=True)
    m2 = jnp.mean(d * y, axis=0, keepdims=True)
    return (d - m1 - y * m2) * r


GELU_C = 0.7978845608028654
GELU_A = 0.044715
LOG2E = 1.4426950408889634

LANES = 128


def _prep_kernel(
    wqkv_h, wo_h, wmsg_h, wup_h, wdown_h, edges_h, pairs_h, slots_h, wread_h, *refs
):
    results = refs[:9]
    pick, wqmT, adjT, deg, woT, wupT, wdownT, hot, wcol = refs[9:18]
    wqkv, wmsg, wo, wup, wdown, edges, pairs, slots, wread, sems, out_sems = refs[18:]
    moves = [
        (edges_h, edges), (slots_h, slots), (pairs_h, pairs), (wread_h, wread),
        (wqkv_h, wqkv), (wmsg_h, wmsg), (wo_h, wo), (wup_h, wup), (wdown_h, wdown),
    ]
    copies = [pltpu.make_async_copy(s, d, sems.at[i]) for i, (s, d) in enumerate(moves)]
    sends = [
        pltpu.make_async_copy(s, d, out_sems.at[i])
        for i, (s, d) in enumerate(zip(refs[9:18], results))
    ]
    for c in copies:
        c.start()
    feats = wo.shape[0]
    subs, nodes = slots.shape
    rows = pick.shape[0]
    n_edges = edges.shape[2]
    n_pairs = pairs.shape[2]
    for c in copies[:4]:
        c.wait()
    it = lax.broadcasted_iota(jnp.int32, (nodes, n_edges), 0)
    ip = lax.broadcasted_iota(jnp.int32, (nodes, 2 * n_pairs), 0)
    ir = lax.broadcasted_iota(jnp.int32, (rows, nodes), 0)

    @pl.loop(0, subs)
    def _(b):
        e = edges[b]
        srcT = (it == e[0:1, :]).astype(F32).astype(BF)
        dstT = (it == e[1:2, :]).astype(F32).astype(BF)
        cnt = _nt(srcT, dstT)
        deg[pl.ds(b, 1), :] = 1.0 / (1.0 + jnp.sum(cnt, axis=0, keepdims=True))
        adjT[b] = cnt.astype(BF)
        p = pairs[b]
        prs = jnp.concatenate([p[0:1, :], p[1:2, :]], axis=1)
        hot[b] = (ip == prs).astype(F32).astype(BF)
        at = pl.ds(pl.multiple_of(b * nodes, LANES), nodes)
        pick[:, at] = (ir == slots[pl.ds(b, 1), :]).astype(F32).astype(BF)

    wcol[...] = jnp.broadcast_to(wread[...], (2 * n_pairs, feats)).T
    for i in (0, 2, 3, 7, 8):
        sends[i].start()
    for c in copies[4:]:
        c.wait()
    wqmT[0 : 3 * feats, :] = wqkv[...].T
    wqmT[3 * feats : 4 * feats, :] = wmsg[...].T
    sends[1].start()
    woT[...] = wo[...].T
    sends[4].start()
    wupT[...] = wup[...].T
    sends[5].start()
    wdownT[...] = wdown[...].T
    sends[6].start()
    for c in sends:
        c.wait()


def _hbm(*arrays):
    return [pltpu.with_memory_space_constraint(v, pltpu.HBM) for v in arrays]


def _prep(w_qkv, w_o, w_msg, w_up, w_down, edges, pairs, node_slots, w_read, rows):
    feats, hidden = w_up.shape
    subs, nodes = node_slots.shape
    n_edges, n_pairs = edges.shape[1], pairs.shape[1]
    out = [
        ((rows, subs * nodes), BF), ((4 * feats, feats), BF), ((subs, nodes, nodes), BF),
        ((subs, nodes), F32), ((feats, feats), BF), ((hidden, feats), BF), ((feats, hidden), BF),
        ((subs, nodes, 2 * n_pairs), BF), ((feats, 2 * n_pairs), F32),
    ]
    return pl.pallas_call(
        _prep_kernel,
        in_specs=[pl.BlockSpec(memory_space=pltpu.HBM)] * 9,
        out_specs=[pl.BlockSpec(memory_space=pltpu.HBM)] * len(out),
        out_shape=[pltpu.HBM(s, d) for s, d in out],
        scratch_shapes=[pltpu.VMEM(s, d) for s, d in out]
        + [
            pltpu.VMEM((feats, 3 * feats), BF),
            pltpu.VMEM((feats, feats), BF),
            pltpu.VMEM((feats, feats), BF),
            pltpu.VMEM((feats, hidden), BF),
            pltpu.VMEM((hidden, feats), BF),
            pltpu.VMEM((subs, 2, n_edges), jnp.int32),
            pltpu.VMEM((subs, 2, n_pairs), jnp.int32),
            pltpu.VMEM((subs, nodes), jnp.int32),
            pltpu.VMEM((1, feats), F32),
            pltpu.SemaphoreType.DMA((9,)),
            pltpu.SemaphoreType.DMA((9,)),
        ],
        compiler_params=pltpu.CompilerParams(vmem_limit_bytes=24 << 20),
        cost_estimate=pl.CostEstimate(
            flops=2 * subs * nodes * nodes * n_edges, bytes_accessed=8 << 20, transcendentals=0
        ),
        name="prep",
    )(
        *_hbm(
            w_qkv, w_o, w_msg, w_up, w_down, edges.transpose(0, 2, 1),
            pairs.transpose(0, 2, 1), node_slots, w_read.reshape(1, feats),
        )
    )


FWD_GROUP = 1
MID_GROUP = 2
BWD_GROUP = 1


def _over(subs, group, stage):
    if subs % group:
        group = 1
    if group == subs:
        for b in range(subs):
            stage(b)
    else:

        @pl.loop(0, subs // group)
        def _(i):
            for k in range(group):
                stage(i * group + k)


def _step_kernel(packed, *refs):
    fetched_ref = refs[0]
    sources = refs[1:14]
    preds_ref = refs[14]
    outs = refs[15 : 15 + (2 if packed else 6)]
    refs = refs[15 + len(outs) :]
    (
        pick, wqmT, adjT, deg, woT, wupT, wdownT, hot_ref, wcol, targets_ref, wo, wup, wdown,
    ) = refs[:13]
    (
        x_s, y_s, dy_s, att_s, datt_s, h_s, g_s, do_s, dup_s, da_s, pf_s, obj_s, gq_s, gu_s, gd_s,
        sems,
    ) = refs[13:]
    copies = [
        pltpu.make_async_copy(s, d, sems.at[i]) for i, (s, d) in enumerate(zip(sources, refs[:13]))
    ]
    for c in copies:
        c.start()
    feats = wo.shape[0]
    hidden = wup.shape[1]
    subs, nodes = deg.shape
    n_pairs = targets_ref.shape[1]
    n_all = subs * n_pairs
    hd = feats // HEADS
    scale = hd ** -0.5

    def lanes(b):
        if isinstance(b, int):
            return slice(b * nodes, (b + 1) * nodes)
        return pl.ds(pl.multiple_of(b * nodes, LANES), nodes)

    def head(part, h):
        return slice(part * feats + h * hd, part * feats + (h + 1) * hd)

    obj_s[...] = jnp.zeros_like(obj_s)
    fetT = fetched_ref[...].T
    copies[0].wait()
    x_s[...] = _nn(fetT, pick[...]).astype(BF)
    copies[1].wait()
    y_s[...] = _nn(wqmT[...], x_s[...]).astype(BF)

    def attend(b):
        at = lanes(b)
        for h in range(HEADS):
            s = _tn(y_s[head(1, h), at], y_s[head(0, h), at])
            e = jnp.exp2((s - jnp.max(s, axis=0, keepdims=True)) * (scale * LOG2E))
            pf = e * (1.0 / jnp.sum(e, axis=0, keepdims=True))
            pf_s[b, h] = pf
            att_s[head(0, h), at] = _nn(y_s[head(2, h), at], pf.astype(BF)).astype(BF)

    _over(subs, FWD_GROUP, attend)
    for c in copies[2:]:
        c.wait()

    def middle(b):
        at = lanes(b)
        base = x_s[:, at].astype(F32)
        xw = y_s[3 * feats : 4 * feats, at]
        dinv = deg[pl.ds(b, 1), :]
        agg = (_nn(xw, adjT[b]) + xw.astype(F32)) * dinv
        n1, r1 = _norm(base + jnp.maximum(agg, 0.0))
        n2, r2 = _norm(base + _nn(woT[...], att_s[:, at]))
        hT = (n1 + n2).astype(BF)
        h_s[:, at] = hT
        up = _nn(wupT[...], hT)
        sq = up * up
        th = jnp.tanh((GELU_C * up) * (1.0 + GELU_A * sq))
        half = 0.5 + 0.5 * th
        gT = (up * half).astype(BF)
        g_s[:, at] = gT
        dgelu = half + (0.5 * up) * (1.0 - th * th) * (GELU_C + (3.0 * GELU_A * GELU_C) * sq)
        out, r3 = _norm(hT.astype(F32) + _nn(wdownT[...], gT))
        hot = hot_ref[b]
        hi, lo = _split(out)
        lr = _nn(hi, hot) + _nn(lo, hot)
        rl = pltpu.roll(lr, n_pairs, 1) * wcol[...]
        preds = jnp.sum(lr * rl, axis=0, keepdims=True)
        tgt = targets_ref[pl.ds(b, 1), :]
        diff = preds - jnp.concatenate([tgt, tgt], axis=1)
        preds_ref[pl.ds(b, 1), :] = preds[:, 0:n_pairs]
        obj_s[0:1, 0:n_pairs] += diff[:, 0:n_pairs] * diff[:, 0:n_pairs]
        hi, lo = _split((diff * (2.0 / n_all)) * rl)
        do = _norm_back(_nt(hi, hot) + _nt(lo, hot), out, r3).astype(BF)
        do_s[:, at] = do
        dg = _nn(wdown[...], do).astype(BF)
        dup = (dgelu * dg.astype(F32)).astype(BF)
        dup_s[:, at] = dup
        dh = _nn(wup[...], dup).astype(BF)
        dl = (do.astype(F32) + dh.astype(F32)).astype(BF).astype(F32)
        dagg = (jnp.where(agg > 0.0, _norm_back(dl, n1, r1), 0.0) * dinv).astype(BF)
        dxw = _nt(dagg, adjT[b]).astype(BF)
        dy_s[3 * feats : 4 * feats, at] = (dxw.astype(F32) + dagg.astype(F32)).astype(BF)
        da = _norm_back(dl, n2, r2).astype(BF)
        da_s[:, at] = da
        datt_s[:, at] = _nn(wo[...], da).astype(BF)

    _over(subs, MID_GROUP, middle)

    def attend_back(b):
        at = lanes(b)
        for h in range(HEADS):
            d = datt_s[head(0, h), at]
            pf = pf_s[b, h]
            dp = _tn(y_s[head(2, h), at], d).astype(BF).astype(F32)
            dy_s[head(2, h), at] = _nt(d, pf.astype(BF)).astype(BF)
            t = dp * pf
            ds = ((t - pf * jnp.sum(t, axis=0, keepdims=True)) * scale).astype(BF)
            dy_s[head(0, h), at] = _nn(y_s[head(1, h), at], ds).astype(BF)
            dy_s[head(1, h), at] = _nt(y_s[head(0, h), at], ds).astype(BF)

    _over(subs, BWD_GROUP, attend_back)

    gq_s[:, 4 * feats :] = _nt(att_s[...], da_s[...]).astype(BF)
    gu_s[...] = _nt(h_s[...], dup_s[...]).astype(BF)
    gd_s[...] = _nt(g_s[...], do_s[...]).astype(BF)
    gq_s[:, 0 : 4 * feats] = _nt(x_s[...], dy_s[...]).astype(BF)
    obj = jnp.sum(obj_s[0:1, :], axis=1, keepdims=True) / n_all
    if packed:
        keep_ref, send_ref = outs
        slabs, rows, width = keep_ref.shape
        core = lax.axis_index("store") % 2
        obj_block = _spread(obj, rows)
        cut = feats * 5
        for ref, side in ((keep_ref, core), (send_ref, 1 - core)):
            for j in range(slabs):
                d = 2 * j + side
                r = pl.ds(pl.multiple_of(d * rows, rows), rows)
                ref[j, :, 0:cut] = gq_s[r, :]
                ref[j, :, cut : cut + hidden] = gu_s[r, :]
                for i in range(hidden // feats):
                    r = pl.ds(pl.multiple_of(d * (rows * hidden // feats) + i * rows, rows), rows)
                    w = cut + hidden + i * feats
                    ref[j, :, w : w + feats] = gd_s[r, :]
                ref[j, :, width - LANES : width] = obj_block
    else:
        obj_ref, gqkv_ref, go_ref, gmsg_ref, gup_ref, gdown_ref = outs
        obj_ref[...] = jnp.broadcast_to(obj, obj_ref.shape)
        gqkv_ref[...] = gq_s[:, 0 : 3 * feats]
        gmsg_ref[...] = gq_s[:, 3 * feats : 4 * feats]
        go_ref[...] = gq_s[:, 4 * feats :]
        gup_ref[...] = gu_s[...]
        gdown_ref[...] = gd_s[...]


def _spread(value, rows):
    full = jnp.broadcast_to(value, (rows, LANES))
    hi = full.astype(BF).astype(F32)
    mid = (full - hi).astype(BF).astype(F32)
    lo = full - hi - mid
    lane = lax.broadcasted_iota(jnp.int32, (rows, LANES), 1)
    return jnp.where(lane < 32, hi, jnp.where(lane < 64, mid, jnp.where(lane < 96, lo, 0.0))).astype(BF)


def _gather_terms(block):
    return block[0:1, 0:1] + block[0:1, 32:33] + block[0:1, 64:65]


def _pair_kernel(a_ref, b_ref, o_ref):
    slabs, rows, width = o_ref.shape
    o_ref[...] = (a_ref[...].astype(F32) + b_ref[...].astype(F32)).astype(BF)
    blk = a_ref[0, :, width - LANES : width].astype(F32), b_ref[0, :, width - LANES : width].astype(F32)
    obj = _spread(_gather_terms(blk[0]) + _gather_terms(blk[1]), rows)
    for j in range(slabs):
        o_ref[j, :, width - LANES : width] = obj


def _final_kernel(in_ref, loss_ref, gqkv, go, gmsg, gup, gdown):
    slabs, rows, width = in_ref.shape
    total = in_ref[0].astype(F32)
    for j in range(1, slabs):
        total = total + in_ref[j].astype(F32)
    feats = go.shape[1]
    hidden = gup.shape[1]
    gqkv[...] = total[:, 0 : 3 * feats]
    gmsg[...] = total[:, 3 * feats : 4 * feats]
    go[...] = total[:, 4 * feats : 5 * feats]
    gup[...] = total[:, 5 * feats : 5 * feats + hidden]
    for i in range(hidden // feats):
        w = 5 * feats + hidden + i * feats
        gdown[i * rows : (i + 1) * rows, :] = total[:, w : w + feats]
    loss = _gather_terms(total[:, width - LANES : width]) / (2 * slabs)
    loss_ref[0] = jnp.sum(loss)


def _vmem(n):
    return [pl.BlockSpec(memory_space=pltpu.VMEM)] * n


def local_step(prep, fetched, targets, weights, groups):
    feats, hidden = weights[1].shape
    subs, nodes = prep[3].shape
    n_pairs = targets.shape[1]
    total = subs * nodes
    sources = (*prep, targets, *weights)
    rows = feats // groups
    packed = groups % 2 == 0 and feats % groups == 0 and hidden % feats == 0 and rows % 16 == 0
    out = [((subs, n_pairs), F32)]
    if packed:
        slab = (groups // 2, rows, 5 * feats + 2 * hidden // feats * feats + LANES)
        out += [(slab, BF), (slab, BF)]
    else:
        out += [
            ((8, LANES), F32), ((feats, 3 * feats), BF), ((feats, feats), BF), ((feats, feats), BF),
            ((feats, hidden), BF), ((hidden, feats), BF),
        ]
    res = pl.pallas_call(
        lambda *refs: _step_kernel(packed, *refs),
        in_specs=_vmem(1) + [pl.BlockSpec(memory_space=pltpu.HBM)] * len(sources),
        out_specs=_vmem(len(out)),
        out_shape=[jax.ShapeDtypeStruct(s, d) for s, d in out],
        scratch_shapes=[pltpu.VMEM(v.shape, v.dtype) for v in sources]
        + [
            pltpu.VMEM((feats, total), BF),
            pltpu.VMEM((4 * feats, total), BF),
            pltpu.VMEM((4 * feats, total), BF),
            pltpu.VMEM((feats, total), BF),
            pltpu.VMEM((feats, total), BF),
            pltpu.VMEM((feats, total), BF),
            pltpu.VMEM((hidden, total), BF),
            pltpu.VMEM((feats, total), BF),
            pltpu.VMEM((hidden, total), BF),
            pltpu.VMEM((feats, total), BF),
            pltpu.VMEM((subs, HEADS, nodes, nodes), F32),
            pltpu.VMEM((8, LANES), F32),
            pltpu.VMEM((feats, 5 * feats), BF),
            pltpu.VMEM((feats, hidden), BF),
            pltpu.VMEM((hidden, feats), BF),
            pltpu.SemaphoreType.DMA((len(sources),)),
        ],
        compiler_params=pltpu.CompilerParams(vmem_limit_bytes=44 << 20),
        name="graph_step",
    )(fetched, *_hbm(*sources))
    return packed, res


def shards(
    store_feats, requests, node_slots, edges, pairs, targets,
    w_qkv, w_o, w_msg, w_up, w_down, w_read,
):
    feats = store_feats.shape[1]
    hidden = w_up.shape[1]
    groups = lax.axis_size("store")
    picked = jnp.take(
        store_feats,
        lax.all_to_all(requests, "store", split_axis=0, concat_axis=0, tiled=True),
        axis=0,
        mode="clip",
    )
    fetched = lax.all_to_all(picked, "store", split_axis=0, concat_axis=0, tiled=True)
    fetched = fetched.reshape(-1, feats)
    prep = _prep(w_qkv, w_o, w_msg, w_up, w_down, edges, pairs, node_slots, w_read, fetched.shape[0])
    packed, (preds, *terms) = local_step(prep, fetched, targets, (w_o, w_up, w_down), groups)
    if packed:
        keep, send = terms
        rows = keep.shape[1]
        got = lax.ppermute(send, "store", [(i, i ^ 1) for i in range(groups)])
        paired = pl.pallas_call(
            _pair_kernel,
            in_specs=_vmem(2),
            out_specs=pl.BlockSpec(memory_space=pltpu.VMEM),
            out_shape=jax.ShapeDtypeStruct(keep.shape, BF),
            name="pair_sum",
        )(keep, got)
        sides = [[i for i in range(groups) if i % 2 == c] for c in (0, 1)]
        shared = lax.all_to_all(
            paired, "store", split_axis=0, concat_axis=0, tiled=True, axis_index_groups=sides
        )
        loss, *shares = pl.pallas_call(
            _final_kernel,
            in_specs=_vmem(1),
            out_specs=[pl.BlockSpec(memory_space=pltpu.SMEM)] + _vmem(5),
            out_shape=[
                jax.ShapeDtypeStruct((1,), F32),
                jax.ShapeDtypeStruct((rows, 3 * feats), F32),
                jax.ShapeDtypeStruct((rows, feats), F32),
                jax.ShapeDtypeStruct((rows, feats), F32),
                jax.ShapeDtypeStruct((rows, hidden), F32),
                jax.ShapeDtypeStruct((rows * (hidden // feats), feats), F32),
            ],
            name="final_sum",
        )(shared)
    else:
        obj, *grads = terms
        shares = [
            lax.psum_scatter(lax.optimization_barrier(g.astype(F32)), "store", scatter_dimension=0, tiled=True)
            for g in grads
        ]
        loss = (lax.psum(obj[0, 0], "store") / groups).reshape(1)
    return (preds, loss, *shares)


def solution(mesh):
    rows = P(("parts", "store"), None)
    deep = P(("parts", "store"), None, None)
    in_specs = (rows, rows, rows, deep, deep, rows, P(), P(), P(), P(), P(), P())
    out_specs = (rows, P("parts"), rows, rows, rows, rows, rows)
    return jax.shard_map(shards, mesh=mesh, in_specs=in_specs, out_specs=out_specs, check_vma=False)
```

```python
import jax
import jax.numpy as jnp
from jax import lax
from jax.experimental import pallas as pl
from jax.experimental.pallas import tpu as pltpu
from jax.sharding import PartitionSpec as P

HEADS = 8
BF = jnp.bfloat16
F32 = jnp.float32


def _nn(a, b):
    return lax.dot_general(a, b, (((1,), (0,)), ((), ())), preferred_element_type=F32)


def _nt(a, b):
    return lax.dot_general(a, b, (((1,), (1,)), ((), ())), preferred_element_type=F32)


def _tn(a, b):
    return lax.dot_general(a, b, (((0,), (0,)), ((), ())), preferred_element_type=F32)


def _split(v):
    hi = v.astype(BF)
    lo = (v - hi.astype(F32)).astype(BF)
    return hi, lo


def _norm(v):
    c = v - jnp.mean(v, axis=0, keepdims=True)
    r = lax.rsqrt(jnp.mean(c * c, axis=0, keepdims=True) + 1e-05)
    return c * r, r


def _norm_back(d, y, r):
    m1 = jnp.mean(d, axis=0, keepdims=True)
    m2 = jnp.mean(d * y, axis=0, keepdims=True)
    return (d - m1 - y * m2) * r


GELU_C = 0.7978845608028654
GELU_A = 0.044715
LOG2E = 1.4426950408889634

LANES = 128


def _prep_kernel(
    wqkv_h, wo_h, wmsg_h, wup_h, wdown_h, edges_h, pairs_h, slots_h, wread_h, *refs
):
    results = refs[:9]
    pick, wqmT, adjT, deg, woT, wupT, wdownT, hot, wcol = refs[9:18]
    wqkv, wmsg, wo, wup, wdown, edges, pairs, slots, wread, sems, out_sems = refs[18:]
    moves = [
        (edges_h, edges), (slots_h, slots), (pairs_h, pairs), (wread_h, wread),
        (wqkv_h, wqkv), (wmsg_h, wmsg), (wo_h, wo), (wup_h, wup), (wdown_h, wdown),
    ]
    copies = [pltpu.make_async_copy(s, d, sems.at[i]) for i, (s, d) in enumerate(moves)]
    sends = [
        pltpu.make_async_copy(s, d, out_sems.at[i])
        for i, (s, d) in enumerate(zip(refs[9:18], results))
    ]
    for c in copies:
        c.start()
    feats = wo.shape[0]
    subs, nodes = slots.shape
    rows = pick.shape[0]
    n_edges = edges.shape[2]
    n_pairs = pairs.shape[2]
    for c in copies[:4]:
        c.wait()
    it = lax.broadcasted_iota(jnp.int32, (nodes, n_edges), 0)
    ip = lax.broadcasted_iota(jnp.int32, (nodes, 2 * n_pairs), 0)
    ir = lax.broadcasted_iota(jnp.int32, (rows, nodes), 0)

    @pl.loop(0, subs)
    def _(b):
        e = edges[b]
        srcT = (it == e[0:1, :]).astype(F32).astype(BF)
        dstT = (it == e[1:2, :]).astype(F32).astype(BF)
        cnt = _nt(srcT, dstT)
        deg[pl.ds(b, 1), :] = 1.0 / (1.0 + jnp.sum(cnt, axis=0, keepdims=True))
        adjT[b] = cnt.astype(BF)
        p = pairs[b]
        prs = jnp.concatenate([p[0:1, :], p[1:2, :]], axis=1)
        hot[b] = (ip == prs).astype(F32).astype(BF)
        at = pl.ds(pl.multiple_of(b * nodes, LANES), nodes)
        pick[:, at] = (ir == slots[pl.ds(b, 1), :]).astype(F32).astype(BF)

    wcol[...] = jnp.broadcast_to(wread[...], (2 * n_pairs, feats)).T
    for i in (0, 2, 3, 7, 8):
        sends[i].start()
    for c in copies[4:]:
        c.wait()
    wqmT[0 : 3 * feats, :] = wqkv[...].T
    wqmT[3 * feats : 4 * feats, :] = wmsg[...].T
    sends[1].start()
    woT[...] = wo[...].T
    sends[4].start()
    wupT[...] = wup[...].T
    sends[5].start()
    wdownT[...] = wdown[...].T
    sends[6].start()
    for c in sends:
        c.wait()


def _hbm(*arrays):
    return [pltpu.with_memory_space_constraint(v, pltpu.HBM) for v in arrays]


def _prep(w_qkv, w_o, w_msg, w_up, w_down, edges, pairs, node_slots, w_read, rows):
    feats, hidden = w_up.shape
    subs, nodes = node_slots.shape
    n_edges, n_pairs = edges.shape[1], pairs.shape[1]
    out = [
        ((rows, subs * nodes), BF), ((4 * feats, feats), BF), ((subs, nodes, nodes), BF),
        ((subs, nodes), F32), ((feats, feats), BF), ((hidden, feats), BF), ((feats, hidden), BF),
        ((subs, nodes, 2 * n_pairs), BF), ((feats, 2 * n_pairs), F32),
    ]
    return pl.pallas_call(
        _prep_kernel,
        in_specs=[pl.BlockSpec(memory_space=pltpu.HBM)] * 9,
        out_specs=[pl.BlockSpec(memory_space=pltpu.HBM)] * len(out),
        out_shape=[pltpu.HBM(s, d) for s, d in out],
        scratch_shapes=[pltpu.VMEM(s, d) for s, d in out]
        + [
            pltpu.VMEM((feats, 3 * feats), BF),
            pltpu.VMEM((feats, feats), BF),
            pltpu.VMEM((feats, feats), BF),
            pltpu.VMEM((feats, hidden), BF),
            pltpu.VMEM((hidden, feats), BF),
            pltpu.VMEM((subs, 2, n_edges), jnp.int32),
            pltpu.VMEM((subs, 2, n_pairs), jnp.int32),
            pltpu.VMEM((subs, nodes), jnp.int32),
            pltpu.VMEM((1, feats), F32),
            pltpu.SemaphoreType.DMA((9,)),
            pltpu.SemaphoreType.DMA((9,)),
        ],
        compiler_params=pltpu.CompilerParams(vmem_limit_bytes=24 << 20),
        cost_estimate=pl.CostEstimate(
            flops=2 * subs * nodes * nodes * n_edges, bytes_accessed=8 << 20, transcendentals=0
        ),
        name="prep",
    )(
        *_hbm(
            w_qkv, w_o, w_msg, w_up, w_down, edges.transpose(0, 2, 1),
            pairs.transpose(0, 2, 1), node_slots, w_read.reshape(1, feats),
        )
    )


FWD_GROUP = 1
BWD_GROUP = 1


def _over(subs, group, stage):
    if subs % group:
        group = 1
    if group == subs:
        for b in range(subs):
            stage(b)
    else:

        @pl.loop(0, subs // group)
        def _(i):
            for k in range(group):
                stage(i * group + k)


def _step_kernel(packed, *refs):
    fetched_ref = refs[0]
    sources = refs[1:14]
    preds_ref = refs[14]
    outs = refs[15 : 15 + (2 if packed else 6)]
    refs = refs[15 + len(outs) :]
    (
        pick, wqmT, adjT, deg, woT, wupT, wdownT, hot_ref, wcol, targets_ref, wo, wup, wdown,
    ) = refs[:13]
    (
        x_s, y_s, dy_s, att_s, datt_s, h_s, g_s, do_s, dup_s, da_s, pf_s, p_s, ds_s, obj_s, gq_s, gu_s, gd_s,
        agg_s, n1_s, n2_s, up_s, out_s, dout_s, hi_s, lo_s, r1_s, r2_s, r3_s,
        sems,
    ) = refs[13:]
    copies = [
        pltpu.make_async_copy(s, d, sems.at[i]) for i, (s, d) in enumerate(zip(sources, refs[:13]))
    ]
    for c in copies:
        c.start()
    feats = wo.shape[0]
    hidden = wup.shape[1]
    subs, nodes = deg.shape
    n_pairs = targets_ref.shape[1]
    n_all = subs * n_pairs
    hd = feats // HEADS
    scale = hd ** -0.5

    def lanes(b):
        if isinstance(b, int):
            return slice(b * nodes, (b + 1) * nodes)
        return pl.ds(pl.multiple_of(b * nodes, LANES), nodes)

    def head(part, h):
        return slice(part * feats + h * hd, part * feats + (h + 1) * hd)

    obj_s[...] = jnp.zeros_like(obj_s)
    fetT = fetched_ref[...].T
    copies[0].wait()
    x_s[...] = _nn(fetT, pick[...]).astype(BF)
    copies[1].wait()
    y_s[...] = _nn(wqmT[...], x_s[...]).astype(BF)

    def attend(b):
        at = lanes(b)
        for h in range(HEADS):
            pf_s[b, h] = _tn(y_s[head(1, h), at], y_s[head(0, h), at])
        for h in range(HEADS):
            s = pf_s[b, h]
            e = jnp.exp2((s - jnp.max(s, axis=0, keepdims=True)) * (scale * LOG2E))
            pf = e * (1.0 / jnp.sum(e, axis=0, keepdims=True))
            pf_s[b, h] = pf
            p_s[h] = pf.astype(BF)
        for h in range(HEADS):
            att_s[head(0, h), at] = _nn(y_s[head(2, h), at], p_s[h]).astype(BF)

    _over(subs, FWD_GROUP, attend)
    for c in copies[2:]:
        c.wait()

    total = subs * nodes
    blocks = [slice(b * nodes, (b + 1) * nodes) for b in range(subs)]
    cuts = [slice(c, c + LANES) for c in range(0, total, LANES)]
    msg = slice(3 * feats, 4 * feats)
    for b, at in enumerate(blocks):
        agg_s[:, at] = _nn(y_s[msg, at], adjT[b])
        n2_s[:, at] = _nn(woT[...], att_s[:, at])
    for c in cuts:
        b, w = c.start // nodes, c.start % nodes
        base = x_s[:, c].astype(F32)
        agg = (agg_s[:, c] + y_s[msg, c].astype(F32)) * deg[b : b + 1, w : w + LANES]
        agg_s[:, c] = agg
        n1, r1_s[0:1, c] = _norm(base + jnp.maximum(agg, 0.0))
        n2, r2_s[0:1, c] = _norm(base + n2_s[:, c])
        n1_s[:, c] = n1
        n2_s[:, c] = n2
        h_s[:, c] = (n1 + n2).astype(BF)
    for at in blocks:
        up_s[:, at] = _nn(wupT[...], h_s[:, at])
    for c in cuts:
        up = up_s[:, c]
        sq = up * up
        th = jnp.tanh((GELU_C * up) * (1.0 + GELU_A * sq))
        half = 0.5 + 0.5 * th
        g_s[:, c] = (up * half).astype(BF)
        up_s[:, c] = half + (0.5 * up) * (1.0 - th * th) * (GELU_C + (3.0 * GELU_A * GELU_C) * sq)
    for at in blocks:
        out_s[:, at] = _nn(wdownT[...], g_s[:, at])
    for c in cuts:
        out, r3_s[0:1, c] = _norm(h_s[:, c].astype(F32) + out_s[:, c])
        out_s[:, c] = out
        hi_s[:, c], lo_s[:, c] = _split(out)
    for b, at in enumerate(blocks):
        hot = hot_ref[b]
        lr = _nn(hi_s[:, at], hot) + _nn(lo_s[:, at], hot)
        rl = pltpu.roll(lr, n_pairs, 1) * wcol[...]
        preds = jnp.sum(lr * rl, axis=0, keepdims=True)
        tgt = targets_ref[b : b + 1, :]
        diff = preds - jnp.concatenate([tgt, tgt], axis=1)
        preds_ref[b : b + 1, :] = preds[:, 0:n_pairs]
        obj_s[0:1, 0:n_pairs] += diff[:, 0:n_pairs] * diff[:, 0:n_pairs]
        hi, lo = _split((diff * (2.0 / n_all)) * rl)
        dout_s[:, at] = _nt(hi, hot) + _nt(lo, hot)
    for c in cuts:
        do_s[:, c] = _norm_back(dout_s[:, c], out_s[:, c], r3_s[0:1, c]).astype(BF)
    for at in blocks:
        dup_s[:, at] = _nn(wdown[...], do_s[:, at]).astype(BF)
    for c in cuts:
        dup_s[:, c] = (up_s[:, c] * dup_s[:, c].astype(F32)).astype(BF)
    for at in blocks:
        da_s[:, at] = _nn(wup[...], dup_s[:, at]).astype(BF)
    for c in cuts:
        b, w = c.start // nodes, c.start % nodes
        dl = (do_s[:, c].astype(F32) + da_s[:, c].astype(F32)).astype(BF).astype(F32)
        d1 = _norm_back(dl, n1_s[:, c], r1_s[0:1, c])
        d1 = jnp.where(agg_s[:, c] > 0.0, d1, 0.0) * deg[b : b + 1, w : w + LANES]
        hi_s[:, c] = d1.astype(BF)
        da_s[:, c] = _norm_back(dl, n2_s[:, c], r2_s[0:1, c]).astype(BF)
    for b, at in enumerate(blocks):
        datt_s[:, at] = _nn(wo[...], da_s[:, at]).astype(BF)
        dagg = hi_s[:, at]
        dxw = _nt(dagg, adjT[b]).astype(BF)
        dy_s[msg, at] = (dxw.astype(F32) + dagg.astype(F32)).astype(BF)

    def attend_back(b):
        at = lanes(b)
        for h in range(HEADS):
            ds_s[h] = _tn(y_s[head(2, h), at], datt_s[head(0, h), at]).astype(BF)
        for h in range(HEADS):
            for c in range(0, nodes, LANES):
                cut = slice(c, c + LANES)
                pf = pf_s[b, h, :, cut]
                t = ds_s[h, :, cut].astype(F32) * pf
                ds = (t - pf * jnp.sum(t, axis=0, keepdims=True)) * scale
                ds_s[h, :, cut] = ds.astype(BF)
                p_s[h, :, cut] = pf.astype(BF)
        for h in range(HEADS):
            dy_s[head(2, h), at] = _nt(datt_s[head(0, h), at], p_s[h]).astype(BF)
            dy_s[head(0, h), at] = _nn(y_s[head(1, h), at], ds_s[h]).astype(BF)
            dy_s[head(1, h), at] = _nt(y_s[head(0, h), at], ds_s[h]).astype(BF)

    _over(subs, BWD_GROUP, attend_back)

    gq_s[:, 4 * feats :] = _nt(att_s[...], da_s[...]).astype(BF)
    gu_s[...] = _nt(h_s[...], dup_s[...]).astype(BF)
    gd_s[...] = _nt(g_s[...], do_s[...]).astype(BF)
    gq_s[:, 0 : 4 * feats] = _nt(x_s[...], dy_s[...]).astype(BF)
    obj = jnp.sum(obj_s[0:1, :], axis=1, keepdims=True) / n_all
    if packed:
        keep_ref, send_ref = outs
        slabs, rows, width = keep_ref.shape
        core = lax.axis_index("store") % 2
        obj_block = _spread(obj, rows)
        cut = feats * 5
        for ref, side in ((keep_ref, core), (send_ref, 1 - core)):
            for j in range(slabs):
                d = 2 * j + side
                r = pl.ds(pl.multiple_of(d * rows, rows), rows)
                ref[j, :, 0:cut] = gq_s[r, :]
                ref[j, :, cut : cut + hidden] = gu_s[r, :]
                for i in range(hidden // feats):
                    r = pl.ds(pl.multiple_of(d * (rows * hidden // feats) + i * rows, rows), rows)
                    w = cut + hidden + i * feats
                    ref[j, :, w : w + feats] = gd_s[r, :]
                ref[j, :, width - LANES : width] = obj_block
    else:
        obj_ref, gqkv_ref, go_ref, gmsg_ref, gup_ref, gdown_ref = outs
        obj_ref[...] = jnp.broadcast_to(obj, obj_ref.shape)
        gqkv_ref[...] = gq_s[:, 0 : 3 * feats]
        gmsg_ref[...] = gq_s[:, 3 * feats : 4 * feats]
        go_ref[...] = gq_s[:, 4 * feats :]
        gup_ref[...] = gu_s[...]
        gdown_ref[...] = gd_s[...]


def _spread(value, rows):
    full = jnp.broadcast_to(value, (rows, LANES))
    hi = full.astype(BF).astype(F32)
    mid = (full - hi).astype(BF).astype(F32)
    lo = full - hi - mid
    lane = lax.broadcasted_iota(jnp.int32, (rows, LANES), 1)
    return jnp.where(lane < 32, hi, jnp.where(lane < 64, mid, jnp.where(lane < 96, lo, 0.0))).astype(BF)


def _gather_terms(block):
    return block[0:1, 0:1] + block[0:1, 32:33] + block[0:1, 64:65]


def _pair_kernel(a_ref, b_ref, o_ref):
    slabs, rows, width = o_ref.shape
    o_ref[...] = (a_ref[...].astype(F32) + b_ref[...].astype(F32)).astype(BF)
    blk = a_ref[0, :, width - LANES : width].astype(F32), b_ref[0, :, width - LANES : width].astype(F32)
    obj = _spread(_gather_terms(blk[0]) + _gather_terms(blk[1]), rows)
    for j in range(slabs):
        o_ref[j, :, width - LANES : width] = obj


def _final_kernel(in_ref, loss_ref, gqkv, go, gmsg, gup, gdown):
    slabs, rows, width = in_ref.shape
    total = in_ref[0].astype(F32)
    for j in range(1, slabs):
        total = total + in_ref[j].astype(F32)
    feats = go.shape[1]
    hidden = gup.shape[1]
    gqkv[...] = total[:, 0 : 3 * feats]
    gmsg[...] = total[:, 3 * feats : 4 * feats]
    go[...] = total[:, 4 * feats : 5 * feats]
    gup[...] = total[:, 5 * feats : 5 * feats + hidden]
    for i in range(hidden // feats):
        w = 5 * feats + hidden + i * feats
        gdown[i * rows : (i + 1) * rows, :] = total[:, w : w + feats]
    loss = _gather_terms(total[:, width - LANES : width]) / (2 * slabs)
    loss_ref[0] = jnp.sum(loss)


def _vmem(n):
    return [pl.BlockSpec(memory_space=pltpu.VMEM)] * n


def local_step(prep, fetched, targets, weights, groups):
    feats, hidden = weights[1].shape
    subs, nodes = prep[3].shape
    n_pairs = targets.shape[1]
    total = subs * nodes
    sources = (*prep, targets, *weights)
    rows = feats // groups
    packed = groups % 2 == 0 and feats % groups == 0 and hidden % feats == 0 and rows % 16 == 0
    out = [((subs, n_pairs), F32)]
    if packed:
        slab = (groups // 2, rows, 5 * feats + 2 * hidden // feats * feats + LANES)
        out += [(slab, BF), (slab, BF)]
    else:
        out += [
            ((8, LANES), F32), ((feats, 3 * feats), BF), ((feats, feats), BF), ((feats, feats), BF),
            ((feats, hidden), BF), ((hidden, feats), BF),
        ]
    res = pl.pallas_call(
        lambda *refs: _step_kernel(packed, *refs),
        in_specs=_vmem(1) + [pl.BlockSpec(memory_space=pltpu.HBM)] * len(sources),
        out_specs=_vmem(len(out)),
        out_shape=[jax.ShapeDtypeStruct(s, d) for s, d in out],
        scratch_shapes=[pltpu.VMEM(v.shape, v.dtype) for v in sources]
        + [
            pltpu.VMEM((feats, total), BF),
            pltpu.VMEM((4 * feats, total), BF),
            pltpu.VMEM((4 * feats, total), BF),
            pltpu.VMEM((feats, total), BF),
            pltpu.VMEM((feats, total), BF),
            pltpu.VMEM((feats, total), BF),
            pltpu.VMEM((hidden, total), BF),
            pltpu.VMEM((feats, total), BF),
            pltpu.VMEM((hidden, total), BF),
            pltpu.VMEM((feats, total), BF),
            pltpu.VMEM((subs, HEADS, nodes, nodes), F32),
            pltpu.VMEM((HEADS, nodes, nodes), BF),
            pltpu.VMEM((HEADS, nodes, nodes), BF),
            pltpu.VMEM((8, LANES), F32),
            pltpu.VMEM((feats, 5 * feats), BF),
            pltpu.VMEM((feats, hidden), BF),
            pltpu.VMEM((hidden, feats), BF),
            pltpu.VMEM((feats, total), F32),
            pltpu.VMEM((feats, total), F32),
            pltpu.VMEM((feats, total), F32),
            pltpu.VMEM((hidden, total), F32),
            pltpu.VMEM((feats, total), F32),
            pltpu.VMEM((feats, total), F32),
            pltpu.VMEM((feats, total), BF),
            pltpu.VMEM((feats, total), BF),
            pltpu.VMEM((8, total), F32),
            pltpu.VMEM((8, total), F32),
            pltpu.VMEM((8, total), F32),
            pltpu.SemaphoreType.DMA((len(sources),)),
        ],
        compiler_params=pltpu.CompilerParams(vmem_limit_bytes=44 << 20),
        name="graph_step",
    )(fetched, *_hbm(*sources))
    return packed, res


def shards(
    store_feats, requests, node_slots, edges, pairs, targets,
    w_qkv, w_o, w_msg, w_up, w_down, w_read,
):
    feats = store_feats.shape[1]
    hidden = w_up.shape[1]
    groups = lax.axis_size("store")
    picked = jnp.take(
        store_feats,
        lax.all_to_all(requests, "store", split_axis=0, concat_axis=0, tiled=True),
        axis=0,
        mode="clip",
    )
    fetched = lax.all_to_all(picked, "store", split_axis=0, concat_axis=0, tiled=True)
    fetched = fetched.reshape(-1, feats)
    prep = _prep(w_qkv, w_o, w_msg, w_up, w_down, edges, pairs, node_slots, w_read, fetched.shape[0])
    packed, (preds, *terms) = local_step(prep, fetched, targets, (w_o, w_up, w_down), groups)
    if packed:
        keep, send = terms
        rows = keep.shape[1]
        got = lax.ppermute(send, "store", [(i, i ^ 1) for i in range(groups)])
        paired = pl.pallas_call(
            _pair_kernel,
            in_specs=_vmem(2),
            out_specs=pl.BlockSpec(memory_space=pltpu.VMEM),
            out_shape=jax.ShapeDtypeStruct(keep.shape, BF),
            compiler_params=pltpu.CompilerParams(vmem_limit_bytes=8 << 20),
            name="pair_sum",
        )(keep, got)
        sides = [[i for i in range(groups) if i % 2 == c] for c in (0, 1)]
        shared = lax.all_to_all(
            paired, "store", split_axis=0, concat_axis=0, tiled=True, axis_index_groups=sides
        )
        loss, *shares = pl.pallas_call(
            _final_kernel,
            in_specs=_vmem(1),
            out_specs=[pl.BlockSpec(memory_space=pltpu.SMEM)] + _vmem(5),
            out_shape=[
                jax.ShapeDtypeStruct((1,), F32),
                jax.ShapeDtypeStruct((rows, 3 * feats), F32),
                jax.ShapeDtypeStruct((rows, feats), F32),
                jax.ShapeDtypeStruct((rows, feats), F32),
                jax.ShapeDtypeStruct((rows, hidden), F32),
                jax.ShapeDtypeStruct((rows * (hidden // feats), feats), F32),
            ],
            compiler_params=pltpu.CompilerParams(vmem_limit_bytes=8 << 20),
            name="final_sum",
        )(shared)
    else:
        obj, *grads = terms
        shares = [
            lax.psum_scatter(lax.optimization_barrier(g.astype(F32)), "store", scatter_dimension=0, tiled=True)
            for g in grads
        ]
        loss = (lax.psum(obj[0, 0], "store") / groups).reshape(1)
    return (preds, loss, *shares)


def solution(mesh):
    rows = P(("parts", "store"), None)
    deep = P(("parts", "store"), None, None)
    in_specs = (rows, rows, rows, deep, deep, rows, P(), P(), P(), P(), P(), P())
    out_specs = (rows, P("parts"), rows, rows, rows, rows, rows)
    return jax.shard_map(shards, mesh=mesh, in_specs=in_specs, out_specs=out_specs, check_vma=False)
```

```python
import jax
import jax.numpy as jnp
from jax import lax
from jax.experimental import pallas as pl
from jax.experimental.pallas import tpu as pltpu
from jax.sharding import PartitionSpec as P

HEADS = 8
BF = jnp.bfloat16
F32 = jnp.float32


def _nn(a, b):
    return lax.dot_general(a, b, (((1,), (0,)), ((), ())), preferred_element_type=F32)


def _nt(a, b):
    return lax.dot_general(a, b, (((1,), (1,)), ((), ())), preferred_element_type=F32)


def _tn(a, b):
    return lax.dot_general(a, b, (((0,), (0,)), ((), ())), preferred_element_type=F32)


def _split(v):
    hi = v.astype(BF)
    lo = (v - hi.astype(F32)).astype(BF)
    return hi, lo


def _norm(v):
    c = v - jnp.mean(v, axis=0, keepdims=True)
    r = lax.rsqrt(jnp.mean(c * c, axis=0, keepdims=True) + 1e-05)
    return c * r, r


def _norm_back(d, y, r):
    m1 = jnp.mean(d, axis=0, keepdims=True)
    m2 = jnp.mean(d * y, axis=0, keepdims=True)
    return (d - m1 - y * m2) * r


GELU_C = 0.7978845608028654
GELU_A = 0.044715
LOG2E = 1.4426950408889634

LANES = 128


def _prep_kernel(
    wqkv_h, wo_h, wmsg_h, wup_h, wdown_h, edges_h, pairs_h, slots_h, wread_h, *refs
):
    results = refs[:9]
    pick, wqmT, adjT, deg, woT, wupT, wdownT, hot, wcol = refs[9:18]
    wqkv, wmsg, wo, wup, wdown, edges, pairs, slots, wread, sems, out_sems = refs[18:]
    moves = [
        (edges_h, edges), (slots_h, slots), (pairs_h, pairs), (wread_h, wread),
        (wqkv_h, wqkv), (wmsg_h, wmsg), (wo_h, wo), (wup_h, wup), (wdown_h, wdown),
    ]
    copies = [pltpu.make_async_copy(s, d, sems.at[i]) for i, (s, d) in enumerate(moves)]
    sends = [
        pltpu.make_async_copy(s, d, out_sems.at[i])
        for i, (s, d) in enumerate(zip(refs[9:18], results))
    ]
    for c in copies:
        c.start()
    feats = wo.shape[0]
    subs, nodes = slots.shape
    rows = pick.shape[0]
    n_edges = edges.shape[2]
    n_pairs = pairs.shape[2]
    for c in copies[:4]:
        c.wait()
    it = lax.broadcasted_iota(jnp.int32, (nodes, n_edges), 0)
    ip = lax.broadcasted_iota(jnp.int32, (nodes, 2 * n_pairs), 0)
    ir = lax.broadcasted_iota(jnp.int32, (rows, nodes), 0)

    @pl.loop(0, subs)
    def _(b):
        e = edges[b]
        srcT = (it == e[0:1, :]).astype(F32).astype(BF)
        dstT = (it == e[1:2, :]).astype(F32).astype(BF)
        cnt = _nt(srcT, dstT)
        deg[pl.ds(b, 1), :] = 1.0 / (1.0 + jnp.sum(cnt, axis=0, keepdims=True))
        adjT[b] = cnt.astype(BF)
        p = pairs[b]
        prs = jnp.concatenate([p[0:1, :], p[1:2, :]], axis=1)
        hot[b] = (ip == prs).astype(F32).astype(BF)
        at = pl.ds(pl.multiple_of(b * nodes, LANES), nodes)
        pick[:, at] = (ir == slots[pl.ds(b, 1), :]).astype(F32).astype(BF)

    wcol[...] = jnp.broadcast_to(wread[...], (2 * n_pairs, feats)).T
    for i in (0, 2, 3, 7, 8):
        sends[i].start()
    for c in copies[4:]:
        c.wait()
    wqmT[0 : 3 * feats, :] = wqkv[...].T
    wqmT[3 * feats : 4 * feats, :] = wmsg[...].T
    sends[1].start()
    woT[...] = wo[...].T
    sends[4].start()
    wupT[...] = wup[...].T
    sends[5].start()
    wdownT[...] = wdown[...].T
    sends[6].start()
    for c in sends:
        c.wait()


def _hbm(*arrays):
    return [pltpu.with_memory_space_constraint(v, pltpu.HBM) for v in arrays]


def _prep(w_qkv, w_o, w_msg, w_up, w_down, edges, pairs, node_slots, w_read, rows):
    feats, hidden = w_up.shape
    subs, nodes = node_slots.shape
    n_edges, n_pairs = edges.shape[1], pairs.shape[1]
    out = [
        ((rows, subs * nodes), BF), ((4 * feats, feats), BF), ((subs, nodes, nodes), BF),
        ((subs, nodes), F32), ((feats, feats), BF), ((hidden, feats), BF), ((feats, hidden), BF),
        ((subs, nodes, 2 * n_pairs), BF), ((feats, 2 * n_pairs), F32),
    ]
    return pl.pallas_call(
        _prep_kernel,
        in_specs=[pl.BlockSpec(memory_space=pltpu.HBM)] * 9,
        out_specs=[pl.BlockSpec(memory_space=pltpu.HBM)] * len(out),
        out_shape=[pltpu.HBM(s, d) for s, d in out],
        scratch_shapes=[pltpu.VMEM(s, d) for s, d in out]
        + [
            pltpu.VMEM((feats, 3 * feats), BF),
            pltpu.VMEM((feats, feats), BF),
            pltpu.VMEM((feats, feats), BF),
            pltpu.VMEM((feats, hidden), BF),
            pltpu.VMEM((hidden, feats), BF),
            pltpu.VMEM((subs, 2, n_edges), jnp.int32),
            pltpu.VMEM((subs, 2, n_pairs), jnp.int32),
            pltpu.VMEM((subs, nodes), jnp.int32),
            pltpu.VMEM((1, feats), F32),
            pltpu.SemaphoreType.DMA((9,)),
            pltpu.SemaphoreType.DMA((9,)),
        ],
        compiler_params=pltpu.CompilerParams(vmem_limit_bytes=24 << 20),
        cost_estimate=pl.CostEstimate(
            flops=2 * subs * nodes * nodes * n_edges, bytes_accessed=8 << 20, transcendentals=0
        ),
        name="prep",
    )(
        *_hbm(
            w_qkv, w_o, w_msg, w_up, w_down, edges.transpose(0, 2, 1),
            pairs.transpose(0, 2, 1), node_slots, w_read.reshape(1, feats),
        )
    )


FWD_GROUP = 4
BWD_GROUP = 4


FWD_SKEW = 0
MID_SKEW = 0
BWD_SKEW = 0


def _wave(items, skew, stages):
    for step in range(len(stages) + skew * (items - 1) if skew else len(stages)):
        for i in range(items):
            s = step - skew * i
            if 0 <= s < len(stages):
                stages[s](i)


def _over(subs, group, stage):
    if subs % group:
        group = 1
    if group == subs:
        for b in range(subs):
            stage(b)
    else:

        @pl.loop(0, subs // group)
        def _(i):
            for k in range(group):
                stage(i * group + k)


def _step_kernel(packed, *refs):
    fetched_ref = refs[0]
    sources = refs[1:14]
    preds_ref = refs[14]
    outs = refs[15 : 15 + (2 if packed else 6)]
    refs = refs[15 + len(outs) :]
    (
        pick, wqmT, adjT, deg, woT, wupT, wdownT, hot_ref, wcol, targets_ref, wo, wup, wdown,
    ) = refs[:13]
    (
        x_s, y_s, dy_s, att_s, datt_s, h_s, g_s, do_s, dup_s, da_s, pf_s, p_s, ds_s, obj_s, gq_s, gu_s, gd_s,
        agg_s, n1_s, n2_s, up_s, out_s, dout_s, hi_s, lo_s, r1_s, r2_s, r3_s,
        sems,
    ) = refs[13:]
    copies = [
        pltpu.make_async_copy(s, d, sems.at[i]) for i, (s, d) in enumerate(zip(sources, refs[:13]))
    ]
    for c in copies:
        c.start()
    feats = wo.shape[0]
    hidden = wup.shape[1]
    subs, nodes = deg.shape
    n_pairs = targets_ref.shape[1]
    n_all = subs * n_pairs
    hd = feats // HEADS
    scale = hd ** -0.5

    def lanes(b):
        if isinstance(b, int):
            return slice(b * nodes, (b + 1) * nodes)
        return pl.ds(pl.multiple_of(b * nodes, LANES), nodes)

    def head(part, h):
        return slice(part * feats + h * hd, part * feats + (h + 1) * hd)

    obj_s[...] = jnp.zeros_like(obj_s)
    fetT = fetched_ref[...].T
    copies[0].wait()
    x_s[...] = _nn(fetT, pick[...]).astype(BF)
    copies[1].wait()
    y_s[...] = _nn(wqmT[...], x_s[...]).astype(BF)

    def attend(b):
        at = lanes(b)
        def score(h):
            pf_s[b, h] = _tn(y_s[head(1, h), at], y_s[head(0, h), at])

        def soften(h):
            s = pf_s[b, h]
            e = jnp.exp2((s - jnp.max(s, axis=0, keepdims=True)) * (scale * LOG2E))
            pf = e * (1.0 / jnp.sum(e, axis=0, keepdims=True))
            pf_s[b, h] = pf
            p_s[b, h] = pf.astype(BF)

        def blend(h):
            att_s[head(0, h), at] = _nn(y_s[head(2, h), at], p_s[b, h]).astype(BF)

        _wave(HEADS, FWD_SKEW, (score, soften, blend))

    _over(subs, FWD_GROUP, attend)
    for c in copies[2:]:
        c.wait()

    total = subs * nodes
    msg = slice(3 * feats, 4 * feats)

    def block(b):
        return slice(b * nodes, (b + 1) * nodes)

    def cuts(b):
        return [block(b)]

    def branches(b):
        at = block(b)
        agg_s[:, at] = _nn(y_s[msg, at], adjT[b])
        n2_s[:, at] = _nn(woT[...], att_s[:, at])

    def branch_norms(b):
        for c in cuts(b):
            w = c.start % nodes
            base = x_s[:, c].astype(F32)
            agg = (agg_s[:, c] + y_s[msg, c].astype(F32)) * deg[b : b + 1, w : w + nodes]
            agg_s[:, c] = agg
            n1, r1_s[0:1, c] = _norm(base + jnp.maximum(agg, 0.0))
            n2, r2_s[0:1, c] = _norm(base + n2_s[:, c])
            n1_s[:, c] = n1
            n2_s[:, c] = n2
            h_s[:, c] = (n1 + n2).astype(BF)

    def raise_up(b):
        up_s[:, block(b)] = _nn(wupT[...], h_s[:, block(b)])

    def gate(b):
        for c in cuts(b):
            up = up_s[:, c]
            sq = up * up
            th = jnp.tanh((GELU_C * up) * (1.0 + GELU_A * sq))
            half = 0.5 + 0.5 * th
            g_s[:, c] = (up * half).astype(BF)
            slope = (1.0 - th * th) * (GELU_C + (3.0 * GELU_A * GELU_C) * sq)
            up_s[:, c] = half + (0.5 * up) * slope

    def lower_down(b):
        out_s[:, block(b)] = _nn(wdownT[...], g_s[:, block(b)])

    def out_norm(b):
        for c in cuts(b):
            out, r3_s[0:1, c] = _norm(h_s[:, c].astype(F32) + out_s[:, c])
            out_s[:, c] = out
            hi_s[:, c], lo_s[:, c] = _split(out)

    def readout(b):
        hot = hot_ref[b]
        at = block(b)
        lr = _nn(hi_s[:, at], hot) + _nn(lo_s[:, at], hot)
        rl = pltpu.roll(lr, n_pairs, 1) * wcol[...]
        preds = jnp.sum(lr * rl, axis=0, keepdims=True)
        tgt = targets_ref[b : b + 1, :]
        diff = preds - jnp.concatenate([tgt, tgt], axis=1)
        preds_ref[b : b + 1, :] = preds[:, 0:n_pairs]
        obj_s[0:1, 0:n_pairs] += diff[:, 0:n_pairs] * diff[:, 0:n_pairs]
        hi, lo = _split((diff * (2.0 / n_all)) * rl)
        dout_s[:, at] = _nt(hi, hot) + _nt(lo, hot)

    def out_back(b):
        for c in cuts(b):
            do_s[:, c] = _norm_back(dout_s[:, c], out_s[:, c], r3_s[0:1, c]).astype(BF)

    def down_back(b):
        dup_s[:, block(b)] = _nn(wdown[...], do_s[:, block(b)]).astype(BF)

    def gate_back(b):
        for c in cuts(b):
            dup_s[:, c] = (up_s[:, c] * dup_s[:, c].astype(F32)).astype(BF)

    def up_back(b):
        da_s[:, block(b)] = _nn(wup[...], dup_s[:, block(b)]).astype(BF)

    def norms_back(b):
        for c in cuts(b):
            w = c.start % nodes
            dl = (do_s[:, c].astype(F32) + da_s[:, c].astype(F32)).astype(BF).astype(F32)
            d1 = _norm_back(dl, n1_s[:, c], r1_s[0:1, c])
            d1 = jnp.where(agg_s[:, c] > 0.0, d1, 0.0) * deg[b : b + 1, w : w + nodes]
            hi_s[:, c] = d1.astype(BF)
            da_s[:, c] = _norm_back(dl, n2_s[:, c], r2_s[0:1, c]).astype(BF)

    def branches_back(b):
        at = block(b)
        datt_s[:, at] = _nn(wo[...], da_s[:, at]).astype(BF)
        dagg = hi_s[:, at]
        dxw = _nt(dagg, adjT[b]).astype(BF)
        dy_s[msg, at] = (dxw.astype(F32) + dagg.astype(F32)).astype(BF)

    stages = (
        branches, branch_norms, raise_up, gate, lower_down, out_norm, readout, out_back,
        down_back, gate_back, up_back, norms_back, branches_back,
    )
    _wave(subs, MID_SKEW, stages)

    def attend_back(b):
        at = lanes(b)
        def score(h):
            ds_s[h] = _tn(y_s[head(2, h), at], datt_s[head(0, h), at]).astype(BF)

        def soften(h):
            pf = pf_s[b, h]
            t = ds_s[h].astype(F32) * pf
            ds_s[h] = ((t - pf * jnp.sum(t, axis=0, keepdims=True)) * scale).astype(BF)

        def blend(h):
            dy_s[head(2, h), at] = _nt(datt_s[head(0, h), at], p_s[b, h]).astype(BF)
            dy_s[head(0, h), at] = _nn(y_s[head(1, h), at], ds_s[h]).astype(BF)
            dy_s[head(1, h), at] = _nt(y_s[head(0, h), at], ds_s[h]).astype(BF)

        _wave(HEADS, BWD_SKEW, (score, soften, blend))

    _over(subs, BWD_GROUP, attend_back)

    gq_s[:, 4 * feats :] = _nt(att_s[...], da_s[...]).astype(BF)
    gu_s[...] = _nt(h_s[...], dup_s[...]).astype(BF)
    gd_s[...] = _nt(g_s[...], do_s[...]).astype(BF)
    gq_s[:, 0 : 4 * feats] = _nt(x_s[...], dy_s[...]).astype(BF)
    obj = jnp.sum(obj_s[0:1, :], axis=1, keepdims=True) / n_all
    if packed:
        keep_ref, send_ref = outs
        slabs, rows, width = keep_ref.shape
        core = lax.axis_index("store") % 2
        obj_block = _spread(obj, rows)
        cut = feats * 5
        for ref, side in ((keep_ref, core), (send_ref, 1 - core)):
            for j in range(slabs):
                d = 2 * j + side
                r = pl.ds(pl.multiple_of(d * rows, rows), rows)
                ref[j, :, 0:cut] = gq_s[r, :]
                ref[j, :, cut : cut + hidden] = gu_s[r, :]
                for i in range(hidden // feats):
                    r = pl.ds(pl.multiple_of(d * (rows * hidden // feats) + i * rows, rows), rows)
                    w = cut + hidden + i * feats
                    ref[j, :, w : w + feats] = gd_s[r, :]
                ref[j, :, width - LANES : width] = obj_block
    else:
        obj_ref, gqkv_ref, go_ref, gmsg_ref, gup_ref, gdown_ref = outs
        obj_ref[...] = jnp.broadcast_to(obj, obj_ref.shape)
        gqkv_ref[...] = gq_s[:, 0 : 3 * feats]
        gmsg_ref[...] = gq_s[:, 3 * feats : 4 * feats]
        go_ref[...] = gq_s[:, 4 * feats :]
        gup_ref[...] = gu_s[...]
        gdown_ref[...] = gd_s[...]


def _spread(value, rows):
    full = jnp.broadcast_to(value, (rows, LANES))
    hi = full.astype(BF).astype(F32)
    mid = (full - hi).astype(BF).astype(F32)
    lo = full - hi - mid
    lane = lax.broadcasted_iota(jnp.int32, (rows, LANES), 1)
    return jnp.where(lane < 32, hi, jnp.where(lane < 64, mid, jnp.where(lane < 96, lo, 0.0))).astype(BF)


def _gather_terms(block):
    return block[0:1, 0:1] + block[0:1, 32:33] + block[0:1, 64:65]


def _pair_kernel(a_ref, b_ref, o_ref):
    slabs, rows, width = o_ref.shape
    o_ref[...] = (a_ref[...].astype(F32) + b_ref[...].astype(F32)).astype(BF)
    blk = a_ref[0, :, width - LANES : width].astype(F32), b_ref[0, :, width - LANES : width].astype(F32)
    obj = _spread(_gather_terms(blk[0]) + _gather_terms(blk[1]), rows)
    for j in range(slabs):
        o_ref[j, :, width - LANES : width] = obj


def _final_kernel(in_ref, loss_ref, gqkv, go, gmsg, gup, gdown):
    slabs, rows, width = in_ref.shape
    total = in_ref[0].astype(F32)
    for j in range(1, slabs):
        total = total + in_ref[j].astype(F32)
    feats = go.shape[1]
    hidden = gup.shape[1]
    gqkv[...] = total[:, 0 : 3 * feats]
    gmsg[...] = total[:, 3 * feats : 4 * feats]
    go[...] = total[:, 4 * feats : 5 * feats]
    gup[...] = total[:, 5 * feats : 5 * feats + hidden]
    for i in range(hidden // feats):
        w = 5 * feats + hidden + i * feats
        gdown[i * rows : (i + 1) * rows, :] = total[:, w : w + feats]
    loss = _gather_terms(total[:, width - LANES : width]) / (2 * slabs)
    loss_ref[0] = jnp.sum(loss)


def _vmem(n):
    return [pl.BlockSpec(memory_space=pltpu.VMEM)] * n


def local_step(prep, fetched, targets, weights, groups):
    feats, hidden = weights[1].shape
    subs, nodes = prep[3].shape
    n_pairs = targets.shape[1]
    total = subs * nodes
    sources = (*prep, targets, *weights)
    rows = feats // groups
    packed = groups % 2 == 0 and feats % groups == 0 and hidden % feats == 0 and rows % 16 == 0
    out = [((subs, n_pairs), F32)]
    if packed:
        slab = (groups // 2, rows, 5 * feats + 2 * hidden // feats * feats + LANES)
        out += [(slab, BF), (slab, BF)]
    else:
        out += [
            ((8, LANES), F32), ((feats, 3 * feats), BF), ((feats, feats), BF), ((feats, feats), BF),
            ((feats, hidden), BF), ((hidden, feats), BF),
        ]
    res = pl.pallas_call(
        lambda *refs: _step_kernel(packed, *refs),
        in_specs=_vmem(1) + [pl.BlockSpec(memory_space=pltpu.HBM)] * len(sources),
        out_specs=_vmem(len(out)),
        out_shape=[jax.ShapeDtypeStruct(s, d) for s, d in out],
        scratch_shapes=[pltpu.VMEM(v.shape, v.dtype) for v in sources]
        + [
            pltpu.VMEM((feats, total), BF),
            pltpu.VMEM((4 * feats, total), BF),
            pltpu.VMEM((4 * feats, total), BF),
            pltpu.VMEM((feats, total), BF),
            pltpu.VMEM((feats, total), BF),
            pltpu.VMEM((feats, total), BF),
            pltpu.VMEM((hidden, total), BF),
            pltpu.VMEM((feats, total), BF),
            pltpu.VMEM((hidden, total), BF),
            pltpu.VMEM((feats, total), BF),
            pltpu.VMEM((subs, HEADS, nodes, nodes), F32),
            pltpu.VMEM((subs, HEADS, nodes, nodes), BF),
            pltpu.VMEM((HEADS, nodes, nodes), BF),
            pltpu.VMEM((8, LANES), F32),
            pltpu.VMEM((feats, 5 * feats), BF),
            pltpu.VMEM((feats, hidden), BF),
            pltpu.VMEM((hidden, feats), BF),
            pltpu.VMEM((feats, total), F32),
            pltpu.VMEM((feats, total), F32),
            pltpu.VMEM((feats, total), F32),
            pltpu.VMEM((hidden, total), F32),
            pltpu.VMEM((feats, total), F32),
            pltpu.VMEM((feats, total), F32),
            pltpu.VMEM((feats, total), BF),
            pltpu.VMEM((feats, total), BF),
            pltpu.VMEM((8, total), F32),
            pltpu.VMEM((8, total), F32),
            pltpu.VMEM((8, total), F32),
            pltpu.SemaphoreType.DMA((len(sources),)),
        ],
        compiler_params=pltpu.CompilerParams(vmem_limit_bytes=44 << 20),
        name="graph_step",
    )(fetched, *_hbm(*sources))
    return packed, res


def shards(
    store_feats, requests, node_slots, edges, pairs, targets,
    w_qkv, w_o, w_msg, w_up, w_down, w_read,
):
    feats = store_feats.shape[1]
    hidden = w_up.shape[1]
    groups = lax.axis_size("store")
    picked = jnp.take(
        store_feats,
        lax.all_to_all(requests, "store", split_axis=0, concat_axis=0, tiled=True),
        axis=0,
        mode="clip",
    )
    fetched = lax.all_to_all(picked, "store", split_axis=0, concat_axis=0, tiled=True)
    fetched = fetched.reshape(-1, feats)
    prep = _prep(w_qkv, w_o, w_msg, w_up, w_down, edges, pairs, node_slots, w_read, fetched.shape[0])
    packed, (preds, *terms) = local_step(prep, fetched, targets, (w_o, w_up, w_down), groups)
    if packed:
        keep, send = terms
        rows = keep.shape[1]
        got = lax.ppermute(send, "store", [(i, i ^ 1) for i in range(groups)])
        paired = pl.pallas_call(
            _pair_kernel,
            in_specs=_vmem(2),
            out_specs=pl.BlockSpec(memory_space=pltpu.VMEM),
            out_shape=jax.ShapeDtypeStruct(keep.shape, BF),
            compiler_params=pltpu.CompilerParams(vmem_limit_bytes=8 << 20),
            name="pair_sum",
        )(keep, got)
        sides = [[i for i in range(groups) if i % 2 == c] for c in (0, 1)]
        shared = lax.all_to_all(
            paired, "store", split_axis=0, concat_axis=0, tiled=True, axis_index_groups=sides
        )
        loss, *shares = pl.pallas_call(
            _final_kernel,
            in_specs=_vmem(1),
            out_specs=[pl.BlockSpec(memory_space=pltpu.SMEM)] + _vmem(5),
            out_shape=[
                jax.ShapeDtypeStruct((1,), F32),
                jax.ShapeDtypeStruct((rows, 3 * feats), F32),
                jax.ShapeDtypeStruct((rows, feats), F32),
                jax.ShapeDtypeStruct((rows, feats), F32),
                jax.ShapeDtypeStruct((rows, hidden), F32),
                jax.ShapeDtypeStruct((rows * (hidden // feats), feats), F32),
            ],
            compiler_params=pltpu.CompilerParams(vmem_limit_bytes=8 << 20),
            name="final_sum",
        )(shared)
    else:
        obj, *grads = terms
        shares = [
            lax.psum_scatter(lax.optimization_barrier(g.astype(F32)), "store", scatter_dimension=0, tiled=True)
            for g in grads
        ]
        loss = (lax.psum(obj[0, 0], "store") / groups).reshape(1)
    return (preds, loss, *shares)


def solution(mesh):
    rows = P(("parts", "store"), None)
    deep = P(("parts", "store"), None, None)
    in_specs = (rows, rows, rows, deep, deep, rows, P(), P(), P(), P(), P(), P())
    out_specs = (rows, P("parts"), rows, rows, rows, rows, rows)
    return jax.shard_map(shards, mesh=mesh, in_specs=in_specs, out_specs=out_specs, check_vma=False)
```

```python
import jax
import jax.numpy as jnp
from jax import lax
from jax.experimental import pallas as pl
from jax.experimental.pallas import tpu as pltpu
from jax.sharding import PartitionSpec as P

HEADS = 8
BF = jnp.bfloat16
F32 = jnp.float32


def _nn(a, b):
    return lax.dot_general(a, b, (((1,), (0,)), ((), ())), preferred_element_type=F32)


def _nt(a, b):
    return lax.dot_general(a, b, (((1,), (1,)), ((), ())), preferred_element_type=F32)


def _tn(a, b):
    return lax.dot_general(a, b, (((0,), (0,)), ((), ())), preferred_element_type=F32)


def _split(v):
    hi = v.astype(BF)
    lo = (v - hi.astype(F32)).astype(BF)
    return hi, lo


def _norm(v):
    c = v - jnp.mean(v, axis=0, keepdims=True)
    r = lax.rsqrt(jnp.mean(c * c, axis=0, keepdims=True) + 1e-05)
    return c * r, r


def _norm_back(d, y, r):
    m1 = jnp.mean(d, axis=0, keepdims=True)
    m2 = jnp.mean(d * y, axis=0, keepdims=True)
    return (d - m1 - y * m2) * r


GELU_C = 0.7978845608028654
GELU_A = 0.044715
LOG2E = 1.4426950408889634

LANES = 128


def _serve_kernel(wanted, store, out, column):
    peers, _, cap = wanted.shape
    diagonal = lax.broadcasted_iota(jnp.int32, (cap, cap), 0) == lax.broadcasted_iota(
        jnp.int32, (cap, cap), 1
    )
    for o in range(peers):
        row = jnp.where(diagonal, wanted[o], 0)
        column[o * cap : (o + 1) * cap, :] = jnp.sum(row, axis=1, keepdims=True)
    rows = store.shape[0]
    step = rows // 4 if rows % 512 == 0 else rows
    lane = lax.broadcasted_iota(jnp.int32, (out.shape[0], step), 1)
    total = jnp.zeros(out.shape, F32)
    for at in range(0, rows, step):
        hot = (lane == column[...] - at).astype(F32).astype(BF)
        total = total + _nn(hot, store[at : at + step, :])
    out[...] = total.astype(out.dtype)


def _prep_kernel(
    wqkv_h, wo_h, wmsg_h, wup_h, wdown_h, edges_h, pairs_h, slots_h, wread_h, store_h, *refs
):
    pick, wqmT = refs[:2]
    results = refs[2:9]
    store = refs[9]
    adjT, deg, woT, wupT, wdownT, hot, wcol = refs[10:17]
    wqkv, wmsg, wo, wup, wdown, edges, pairs, slots, wread, sems, out_sems = refs[17:]
    moves = [
        (edges_h, edges), (slots_h, slots), (pairs_h, pairs), (wread_h, wread),
        (wqkv_h, wqkv), (wmsg_h, wmsg), (wo_h, wo), (wup_h, wup), (wdown_h, wdown),
        (store_h, store),
    ]
    copies = [pltpu.make_async_copy(s, d, sems.at[i]) for i, (s, d) in enumerate(moves)]
    sends = [
        pltpu.make_async_copy(s, d, out_sems.at[i])
        for i, (s, d) in enumerate(zip(refs[10:17], results))
    ]
    for c in copies:
        c.start()
    feats = wo.shape[0]
    subs, nodes = slots.shape
    rows = pick.shape[0]
    n_edges = edges.shape[2]
    n_pairs = pairs.shape[2]
    for c in copies[:4]:
        c.wait()
    it = lax.broadcasted_iota(jnp.int32, (nodes, n_edges), 0)
    ip = lax.broadcasted_iota(jnp.int32, (nodes, 2 * n_pairs), 0)
    ir = lax.broadcasted_iota(jnp.int32, (rows, nodes), 0)

    @pl.loop(0, subs)
    def _(b):
        e = edges[b]
        srcT = (it == e[0:1, :]).astype(F32).astype(BF)
        dstT = (it == e[1:2, :]).astype(F32).astype(BF)
        cnt = _nt(srcT, dstT)
        deg[pl.ds(b, 1), :] = 1.0 / (1.0 + jnp.sum(cnt, axis=0, keepdims=True))
        adjT[b] = cnt.astype(BF)
        p = pairs[b]
        prs = jnp.concatenate([p[0:1, :], p[1:2, :]], axis=1)
        hot[b] = (ip == prs).astype(F32).astype(BF)
        at = pl.ds(pl.multiple_of(b * nodes, LANES), nodes)
        pick[:, at] = (ir == slots[pl.ds(b, 1), :]).astype(F32).astype(BF)

    wcol[...] = jnp.broadcast_to(wread[...], (2 * n_pairs, feats)).T
    for i in (0, 1, 5, 6):
        sends[i].start()
    for c in copies[4:9]:
        c.wait()
    wqmT[0 : 3 * feats, :] = wqkv[...].T
    wqmT[3 * feats : 4 * feats, :] = wmsg[...].T
    woT[...] = wo[...].T
    sends[2].start()
    wupT[...] = wup[...].T
    sends[3].start()
    wdownT[...] = wdown[...].T
    sends[4].start()
    for c in sends:
        c.wait()
    copies[9].wait()


def _hbm(*arrays):
    return [pltpu.with_memory_space_constraint(v, pltpu.HBM) for v in arrays]


def _prep(w_qkv, w_o, w_msg, w_up, w_down, edges, pairs, node_slots, w_read, store, rows):
    feats, hidden = w_up.shape
    subs, nodes = node_slots.shape
    n_edges, n_pairs = edges.shape[1], pairs.shape[1]
    out = [
        ((rows, subs * nodes), BF), ((4 * feats, feats), BF), ((subs, nodes, nodes), BF),
        ((subs, nodes), F32), ((feats, feats), BF), ((hidden, feats), BF), ((feats, hidden), BF),
        ((subs, nodes, 2 * n_pairs), BF), ((feats, 2 * n_pairs), F32),
    ]
    return pl.pallas_call(
        _prep_kernel,
        in_specs=[pl.BlockSpec(memory_space=pltpu.HBM)] * 10,
        out_specs=_vmem(2) + [pl.BlockSpec(memory_space=pltpu.HBM)] * 7 + _vmem(1),
        out_shape=[pltpu.VMEM(s, d) for s, d in out[:2]]
        + [pltpu.HBM(s, d) for s, d in out[2:]]
        + [pltpu.VMEM(store.shape, store.dtype)],
        scratch_shapes=[pltpu.VMEM(s, d) for s, d in out[2:]]
        + [
            pltpu.VMEM((feats, 3 * feats), BF),
            pltpu.VMEM((feats, feats), BF),
            pltpu.VMEM((feats, feats), BF),
            pltpu.VMEM((feats, hidden), BF),
            pltpu.VMEM((hidden, feats), BF),
            pltpu.VMEM((subs, 2, n_edges), jnp.int32),
            pltpu.VMEM((subs, 2, n_pairs), jnp.int32),
            pltpu.VMEM((subs, nodes), jnp.int32),
            pltpu.VMEM((1, feats), F32),
            pltpu.SemaphoreType.DMA((10,)),
            pltpu.SemaphoreType.DMA((7,)),
        ],
        compiler_params=pltpu.CompilerParams(vmem_limit_bytes=24 << 20),
        cost_estimate=pl.CostEstimate(
            flops=2 * subs * nodes * nodes * n_edges, bytes_accessed=8 << 20, transcendentals=0
        ),
        name="prep",
    )(
        *_hbm(
            w_qkv, w_o, w_msg, w_up, w_down, edges.transpose(0, 2, 1),
            pairs.transpose(0, 2, 1), node_slots, w_read.reshape(1, feats), store,
        )
    )


FWD_GROUP = 4
BWD_GROUP = 4


FWD_SKEW = 0
MID_SKEW = 0
BWD_SKEW = 0


def _wave(items, skew, stages):
    for step in range(len(stages) + skew * (items - 1) if skew else len(stages)):
        for i in range(items):
            s = step - skew * i
            if 0 <= s < len(stages):
                stages[s](i)


def _over(subs, group, stage):
    if subs % group:
        group = 1
    if group == subs:
        for b in range(subs):
            stage(b)
    else:

        @pl.loop(0, subs // group)
        def _(i):
            for k in range(group):
                stage(i * group + k)


def _step_kernel(packed, *refs):
    fetched_ref, pick, wqmT = refs[:3]
    sources = refs[3:14]
    preds_ref = refs[14]
    outs = refs[15 : 15 + (2 if packed else 6)]
    refs = refs[15 + len(outs) :]
    adjT, deg, woT, wupT, wdownT, hot_ref, wcol, targets_ref, wo, wup, wdown = refs[:11]
    (
        x_s, y_s, dy_s, att_s, datt_s, h_s, g_s, do_s, dup_s, da_s, pf_s, p_s, ds_s, obj_s, gq_s, gu_s, gd_s,
        agg_s, n1_s, n2_s, up_s, out_s, dout_s, hi_s, lo_s, r1_s, r2_s, r3_s,
        sems,
    ) = refs[11:]
    copies = [
        pltpu.make_async_copy(s, d, sems.at[i]) for i, (s, d) in enumerate(zip(sources, refs[:11]))
    ]
    for c in copies:
        c.start()
    feats = wo.shape[0]
    hidden = wup.shape[1]
    subs, nodes = deg.shape
    n_pairs = targets_ref.shape[1]
    n_all = subs * n_pairs
    hd = feats // HEADS
    scale = hd ** -0.5

    def lanes(b):
        if isinstance(b, int):
            return slice(b * nodes, (b + 1) * nodes)
        return pl.ds(pl.multiple_of(b * nodes, LANES), nodes)

    def head(part, h):
        return slice(part * feats + h * hd, part * feats + (h + 1) * hd)

    obj_s[...] = jnp.zeros_like(obj_s)
    x_s[...] = _nn(fetched_ref[...].T, pick[...]).astype(BF)
    y_s[...] = _nn(wqmT[...], x_s[...]).astype(BF)

    def attend(b):
        at = lanes(b)
        def score(h):
            pf_s[b, h] = _tn(y_s[head(1, h), at], y_s[head(0, h), at])

        def soften(h):
            s = pf_s[b, h]
            e = jnp.exp2((s - jnp.max(s, axis=0, keepdims=True)) * (scale * LOG2E))
            pf = e * (1.0 / jnp.sum(e, axis=0, keepdims=True))
            pf_s[b, h] = pf
            p_s[b, h] = pf.astype(BF)

        def blend(h):
            att_s[head(0, h), at] = _nn(y_s[head(2, h), at], p_s[b, h]).astype(BF)

        _wave(HEADS, FWD_SKEW, (score, soften, blend))

    _over(subs, FWD_GROUP, attend)
    for c in copies:
        c.wait()

    total = subs * nodes
    msg = slice(3 * feats, 4 * feats)

    def block(b):
        return slice(b * nodes, (b + 1) * nodes)

    def cuts(b):
        return [block(b)]

    def branches(b):
        at = block(b)
        agg_s[:, at] = _nn(y_s[msg, at], adjT[b])
        n2_s[:, at] = _nn(woT[...], att_s[:, at])

    def branch_norms(b):
        for c in cuts(b):
            w = c.start % nodes
            base = x_s[:, c].astype(F32)
            agg = (agg_s[:, c] + y_s[msg, c].astype(F32)) * deg[b : b + 1, w : w + nodes]
            agg_s[:, c] = agg
            n1, r1_s[0:1, c] = _norm(base + jnp.maximum(agg, 0.0))
            n2, r2_s[0:1, c] = _norm(base + n2_s[:, c])
            n1_s[:, c] = n1
            n2_s[:, c] = n2
            h_s[:, c] = (n1 + n2).astype(BF)

    def raise_up(b):
        up_s[:, block(b)] = _nn(wupT[...], h_s[:, block(b)])

    def gate(b):
        for c in cuts(b):
            up = up_s[:, c]
            sq = up * up
            th = jnp.tanh((GELU_C * up) * (1.0 + GELU_A * sq))
            half = 0.5 + 0.5 * th
            g_s[:, c] = (up * half).astype(BF)
            slope = (1.0 - th * th) * (GELU_C + (3.0 * GELU_A * GELU_C) * sq)
            up_s[:, c] = half + (0.5 * up) * slope

    def lower_down(b):
        out_s[:, block(b)] = _nn(wdownT[...], g_s[:, block(b)])

    def out_norm(b):
        for c in cuts(b):
            out, r3_s[0:1, c] = _norm(h_s[:, c].astype(F32) + out_s[:, c])
            out_s[:, c] = out
            hi_s[:, c], lo_s[:, c] = _split(out)

    def readout(b):
        hot = hot_ref[b]
        at = block(b)
        lr = _nn(hi_s[:, at], hot) + _nn(lo_s[:, at], hot)
        rl = pltpu.roll(lr, n_pairs, 1) * wcol[...]
        preds = jnp.sum(lr * rl, axis=0, keepdims=True)
        tgt = targets_ref[b : b + 1, :]
        diff = preds - jnp.concatenate([tgt, tgt], axis=1)
        preds_ref[b : b + 1, :] = preds[:, 0:n_pairs]
        obj_s[0:1, 0:n_pairs] += diff[:, 0:n_pairs] * diff[:, 0:n_pairs]
        hi, lo = _split((diff * (2.0 / n_all)) * rl)
        dout_s[:, at] = _nt(hi, hot) + _nt(lo, hot)

    def out_back(b):
        for c in cuts(b):
            do_s[:, c] = _norm_back(dout_s[:, c], out_s[:, c], r3_s[0:1, c]).astype(BF)

    def down_back(b):
        dup_s[:, block(b)] = _nn(wdown[...], do_s[:, block(b)]).astype(BF)

    def gate_back(b):
        for c in cuts(b):
            dup_s[:, c] = (up_s[:, c] * dup_s[:, c].astype(F32)).astype(BF)

    def up_back(b):
        da_s[:, block(b)] = _nn(wup[...], dup_s[:, block(b)]).astype(BF)

    def norms_back(b):
        for c in cuts(b):
            w = c.start % nodes
            dl = (do_s[:, c].astype(F32) + da_s[:, c].astype(F32)).astype(BF).astype(F32)
            d1 = _norm_back(dl, n1_s[:, c], r1_s[0:1, c])
            d1 = jnp.where(agg_s[:, c] > 0.0, d1, 0.0) * deg[b : b + 1, w : w + nodes]
            hi_s[:, c] = d1.astype(BF)
            da_s[:, c] = _norm_back(dl, n2_s[:, c], r2_s[0:1, c]).astype(BF)

    def branches_back(b):
        at = block(b)
        datt_s[:, at] = _nn(wo[...], da_s[:, at]).astype(BF)
        dagg = hi_s[:, at]
        dxw = _nt(dagg, adjT[b]).astype(BF)
        dy_s[msg, at] = (dxw.astype(F32) + dagg.astype(F32)).astype(BF)

    stages = (
        branches, branch_norms, raise_up, gate, lower_down, out_norm, readout, out_back,
        down_back, gate_back, up_back, norms_back, branches_back,
    )
    _wave(subs, MID_SKEW, stages)

    def attend_back(b):
        at = lanes(b)
        def score(h):
            ds_s[h] = _tn(y_s[head(2, h), at], datt_s[head(0, h), at]).astype(BF)

        def soften(h):
            pf = pf_s[b, h]
            t = ds_s[h].astype(F32) * pf
            ds_s[h] = ((t - pf * jnp.sum(t, axis=0, keepdims=True)) * scale).astype(BF)

        def blend(h):
            dy_s[head(2, h), at] = _nt(datt_s[head(0, h), at], p_s[b, h]).astype(BF)
            dy_s[head(0, h), at] = _nn(y_s[head(1, h), at], ds_s[h]).astype(BF)
            dy_s[head(1, h), at] = _nt(y_s[head(0, h), at], ds_s[h]).astype(BF)

        _wave(HEADS, BWD_SKEW, (score, soften, blend))

    _over(subs, BWD_GROUP, attend_back)

    gq_s[:, 4 * feats :] = _nt(att_s[...], da_s[...]).astype(BF)
    gu_s[...] = _nt(h_s[...], dup_s[...]).astype(BF)
    gd_s[...] = _nt(g_s[...], do_s[...]).astype(BF)
    gq_s[:, 0 : 4 * feats] = _nt(x_s[...], dy_s[...]).astype(BF)
    obj = jnp.sum(obj_s[0:1, :], axis=1, keepdims=True) / n_all
    if packed:
        keep_ref, send_ref = outs
        slabs = keep_ref.shape[0]
        rows = feats // (2 * slabs)
        core = lax.axis_index("store") % 2
        obj_block = _spread(obj, TAIL)
        per = hidden // feats
        for ref, side in ((keep_ref, core), (send_ref, 1 - core)):
            for j in range(slabs):
                d = 2 * j + side
                r = pl.ds(pl.multiple_of(d * rows, rows), rows)
                pieces = [gq_s[r, c : c + LANES] for c in range(0, 5 * feats, LANES)]
                pieces += [gu_s[r, c : c + LANES] for c in range(0, hidden, LANES)]
                for i in range(per):
                    r = pl.ds(pl.multiple_of(d * (rows * per) + i * rows, rows), rows)
                    pieces += [gd_s[r, c : c + LANES] for c in range(0, feats, LANES)]
                for i, piece in enumerate(pieces):
                    ref[j, i * rows : (i + 1) * rows, :] = piece
                ref[j, len(pieces) * rows :, :] = obj_block
    else:
        obj_ref, gqkv_ref, go_ref, gmsg_ref, gup_ref, gdown_ref = outs
        obj_ref[...] = jnp.broadcast_to(obj, obj_ref.shape)
        gqkv_ref[...] = gq_s[:, 0 : 3 * feats]
        gmsg_ref[...] = gq_s[:, 3 * feats : 4 * feats]
        go_ref[...] = gq_s[:, 4 * feats :]
        gup_ref[...] = gu_s[...]
        gdown_ref[...] = gd_s[...]


def _spread(value, rows):
    full = jnp.broadcast_to(value, (rows, LANES))
    hi = full.astype(BF).astype(F32)
    mid = (full - hi).astype(BF).astype(F32)
    lo = full - hi - mid
    lane = lax.broadcasted_iota(jnp.int32, (rows, LANES), 1)
    return jnp.where(lane < 32, hi, jnp.where(lane < 64, mid, jnp.where(lane < 96, lo, 0.0))).astype(BF)


def _gather_terms(block):
    return block[0:1, 0:1] + block[0:1, 32:33] + block[0:1, 64:65]


TAIL = 8


def _pair_kernel(a_ref, b_ref, o_ref):
    slabs, rows, _ = o_ref.shape
    o_ref[...] = (a_ref[...].astype(F32) + b_ref[...].astype(F32)).astype(BF)
    a = a_ref[0, rows - TAIL :, :].astype(F32)
    b = b_ref[0, rows - TAIL :, :].astype(F32)
    obj = _spread(_gather_terms(a) + _gather_terms(b), TAIL)
    for j in range(slabs):
        o_ref[j, rows - TAIL :, :] = obj


def _final_kernel(in_ref, loss_ref, gqkv, go, gmsg, gup, gdown):
    slabs, height, _ = in_ref.shape
    total = in_ref[0].astype(F32)
    for j in range(1, slabs):
        total = total + in_ref[j].astype(F32)
    rows, feats = go.shape
    hidden = gup.shape[1]
    places = [(gqkv, 0, c) for c in range(0, 3 * feats, LANES)]
    places += [(gmsg, 0, c) for c in range(0, feats, LANES)]
    places += [(go, 0, c) for c in range(0, feats, LANES)]
    places += [(gup, 0, c) for c in range(0, hidden, LANES)]
    for i in range(hidden // feats):
        places += [(gdown, i * rows, c) for c in range(0, feats, LANES)]
    for i, (ref, r, c) in enumerate(places):
        ref[r : r + rows, c : c + LANES] = total[i * rows : (i + 1) * rows, :]
    loss_ref[0] = jnp.sum(_gather_terms(total[height - TAIL :, :]) / (2 * slabs))


def _vmem(n):
    return [pl.BlockSpec(memory_space=pltpu.VMEM)] * n


def local_step(prep, fetched, targets, weights, groups):
    feats, hidden = weights[1].shape
    subs, nodes = prep[3].shape
    n_pairs = targets.shape[1]
    total = subs * nodes
    sources = (*prep[2:], targets, *weights)
    rows = feats // groups
    packed = groups % 2 == 0 and feats % groups == 0 and hidden % feats == 0 and rows % 16 == 0
    packed = packed and feats % LANES == 0
    out = [((subs, n_pairs), F32)]
    if packed:
        slab = (groups // 2, rows * (5 * feats + 2 * hidden) // LANES + TAIL, LANES)
        out += [(slab, BF), (slab, BF)]
    else:
        out += [
            ((8, LANES), F32), ((feats, 3 * feats), BF), ((feats, feats), BF), ((feats, feats), BF),
            ((feats, hidden), BF), ((hidden, feats), BF),
        ]
    res = pl.pallas_call(
        lambda *refs: _step_kernel(packed, *refs),
        in_specs=_vmem(3) + [pl.BlockSpec(memory_space=pltpu.HBM)] * len(sources),
        out_specs=_vmem(len(out)),
        out_shape=[jax.ShapeDtypeStruct(s, d) for s, d in out],
        scratch_shapes=[pltpu.VMEM(v.shape, v.dtype) for v in sources]
        + [
            pltpu.VMEM((feats, total), BF),
            pltpu.VMEM((4 * feats, total), BF),
            pltpu.VMEM((4 * feats, total), BF),
            pltpu.VMEM((feats, total), BF),
            pltpu.VMEM((feats, total), BF),
            pltpu.VMEM((feats, total), BF),
            pltpu.VMEM((hidden, total), BF),
            pltpu.VMEM((feats, total), BF),
            pltpu.VMEM((hidden, total), BF),
            pltpu.VMEM((feats, total), BF),
            pltpu.VMEM((subs, HEADS, nodes, nodes), F32),
            pltpu.VMEM((subs, HEADS, nodes, nodes), BF),
            pltpu.VMEM((HEADS, nodes, nodes), BF),
            pltpu.VMEM((8, LANES), F32),
            pltpu.VMEM((feats, 5 * feats), BF),
            pltpu.VMEM((feats, hidden), BF),
            pltpu.VMEM((hidden, feats), BF),
            pltpu.VMEM((feats, total), F32),
            pltpu.VMEM((feats, total), F32),
            pltpu.VMEM((feats, total), F32),
            pltpu.VMEM((hidden, total), F32),
            pltpu.VMEM((feats, total), F32),
            pltpu.VMEM((feats, total), F32),
            pltpu.VMEM((feats, total), BF),
            pltpu.VMEM((feats, total), BF),
            pltpu.VMEM((8, total), F32),
            pltpu.VMEM((8, total), F32),
            pltpu.VMEM((8, total), F32),
            pltpu.SemaphoreType.DMA((len(sources),)),
        ],
        compiler_params=pltpu.CompilerParams(vmem_limit_bytes=40 << 20),
        name="graph_step",
    )(fetched, *prep[:2], *_hbm(*sources))
    return packed, res


def shards(
    store_feats, requests, node_slots, edges, pairs, targets,
    w_qkv, w_o, w_msg, w_up, w_down, w_read,
):
    feats = store_feats.shape[1]
    hidden = w_up.shape[1]
    groups = lax.axis_size("store")
    wanted = lax.all_to_all(
        requests.reshape(groups, 1, -1), "store", split_axis=0, concat_axis=0, tiled=True
    )
    *prep, store = _prep(
        w_qkv, w_o, w_msg, w_up, w_down, edges, pairs, node_slots, w_read, store_feats,
        wanted.size,
    )
    picked = pl.pallas_call(
        _serve_kernel,
        in_specs=_vmem(2),
        out_specs=pl.BlockSpec(memory_space=pltpu.VMEM),
        out_shape=jax.ShapeDtypeStruct((wanted.size, feats), store_feats.dtype),
        scratch_shapes=[pltpu.VMEM((wanted.size, 1), jnp.int32)],
        compiler_params=pltpu.CompilerParams(vmem_limit_bytes=16 << 20),
        name="serve",
    )(wanted, store)
    picked = picked.reshape(groups, -1, feats)
    fetched = lax.all_to_all(picked, "store", split_axis=0, concat_axis=0, tiled=True)
    fetched = fetched.reshape(-1, feats)
    packed, (preds, *terms) = local_step(prep, fetched, targets, (w_o, w_up, w_down), groups)
    if packed:
        keep, send = terms
        rows = feats // groups
        got = lax.ppermute(send, "store", [(i, i ^ 1) for i in range(groups)])
        paired = pl.pallas_call(
            _pair_kernel,
            in_specs=_vmem(2),
            out_specs=pl.BlockSpec(memory_space=pltpu.VMEM),
            out_shape=jax.ShapeDtypeStruct(keep.shape, BF),
            compiler_params=pltpu.CompilerParams(vmem_limit_bytes=8 << 20),
            name="pair_sum",
        )(keep, got)
        sides = [[i for i in range(groups) if i % 2 == c] for c in (0, 1)]
        shared = lax.all_to_all(
            paired, "store", split_axis=0, concat_axis=0, tiled=True, axis_index_groups=sides
        )
        loss, *shares = pl.pallas_call(
            _final_kernel,
            in_specs=_vmem(1),
            out_specs=[pl.BlockSpec(memory_space=pltpu.SMEM)] + _vmem(5),
            out_shape=[
                jax.ShapeDtypeStruct((1,), F32),
                jax.ShapeDtypeStruct((rows, 3 * feats), F32),
                jax.ShapeDtypeStruct((rows, feats), F32),
                jax.ShapeDtypeStruct((rows, feats), F32),
                jax.ShapeDtypeStruct((rows, hidden), F32),
                jax.ShapeDtypeStruct((rows * (hidden // feats), feats), F32),
            ],
            compiler_params=pltpu.CompilerParams(vmem_limit_bytes=8 << 20),
            name="final_sum",
        )(shared)
    else:
        obj, *grads = terms
        shares = [
            lax.psum_scatter(lax.optimization_barrier(g.astype(F32)), "store", scatter_dimension=0, tiled=True)
            for g in grads
        ]
        loss = (lax.psum(obj[0, 0], "store") / groups).reshape(1)
    return (preds, loss, *shares)


def solution(mesh):
    rows = P(("parts", "store"), None)
    deep = P(("parts", "store"), None, None)
    in_specs = (rows, rows, rows, deep, deep, rows, P(), P(), P(), P(), P(), P())
    out_specs = (rows, P("parts"), rows, rows, rows, rows, rows)
    return jax.shard_map(shards, mesh=mesh, in_specs=in_specs, out_specs=out_specs, check_vma=False)
```

```python
import jax
import jax.numpy as jnp
from jax import lax
from jax.experimental import pallas as pl
from jax.experimental.pallas import tpu as pltpu
from jax.sharding import PartitionSpec as P

HEADS = 8
BF = jnp.bfloat16
F32 = jnp.float32


def _nn(a, b):
    return lax.dot_general(a, b, (((1,), (0,)), ((), ())), preferred_element_type=F32)


def _nt(a, b):
    return lax.dot_general(a, b, (((1,), (1,)), ((), ())), preferred_element_type=F32)


def _tn(a, b):
    return lax.dot_general(a, b, (((0,), (0,)), ((), ())), preferred_element_type=F32)


def _split(v):
    hi = v.astype(BF)
    lo = (v - hi.astype(F32)).astype(BF)
    return hi, lo


def _norm(v):
    c = v - jnp.mean(v, axis=0, keepdims=True)
    r = lax.rsqrt(jnp.mean(c * c, axis=0, keepdims=True) + 1e-05)
    return c * r, r


def _norm_back(d, y, r):
    m1 = jnp.mean(d, axis=0, keepdims=True)
    m2 = jnp.mean(d * y, axis=0, keepdims=True)
    return (d - m1 - y * m2) * r


GELU_C = 0.7978845608028654
GELU_A = 0.044715
LOG2E = 1.4426950408889634

LANES = 128


def _serve_kernel(wanted, store, out, column):
    peers, _, cap = wanted.shape
    diagonal = lax.broadcasted_iota(jnp.int32, (cap, cap), 0) == lax.broadcasted_iota(
        jnp.int32, (cap, cap), 1
    )
    for o in range(peers):
        row = jnp.where(diagonal, wanted[o], 0)
        column[o * cap : (o + 1) * cap, :] = jnp.sum(row, axis=1, keepdims=True)
    rows = store.shape[0]
    step = rows // 4 if rows % 512 == 0 else rows
    lane = lax.broadcasted_iota(jnp.int32, (out.shape[0], step), 1)
    total = jnp.zeros(out.shape, F32)
    for at in range(0, rows, step):
        hot = (lane == column[...] - at).astype(F32).astype(BF)
        total = total + _nn(hot, store[at : at + step, :])
    out[...] = total.astype(out.dtype)


def _prep_kernel(
    wqkv_h, wo_h, wmsg_h, wup_h, wdown_h, edges_h, pairs_h, slots_h, wread_h, store_h, *refs
):
    pick, wqmT = refs[:2]
    results = refs[2:9]
    store = refs[9]
    adjT, deg, woT, wupT, wdownT, hot, wcol = refs[10:17]
    wqkv, wmsg, wo, wup, wdown, edges, pairs, slots, wread, sems, out_sems = refs[17:]
    moves = [
        (edges_h, edges), (slots_h, slots), (pairs_h, pairs), (wread_h, wread),
        (wqkv_h, wqkv), (wmsg_h, wmsg), (wo_h, wo), (wup_h, wup), (wdown_h, wdown),
        (store_h, store),
    ]
    copies = [pltpu.make_async_copy(s, d, sems.at[i]) for i, (s, d) in enumerate(moves)]
    sends = [
        pltpu.make_async_copy(s, d, out_sems.at[i])
        for i, (s, d) in enumerate(zip(refs[10:17], results))
    ]
    for c in copies:
        c.start()
    feats = wo.shape[0]
    subs, nodes = slots.shape
    rows = pick.shape[0]
    n_edges = edges.shape[2]
    n_pairs = pairs.shape[2]
    for c in copies[:4]:
        c.wait()
    it = lax.broadcasted_iota(jnp.int32, (nodes, n_edges), 0)
    ip = lax.broadcasted_iota(jnp.int32, (nodes, 2 * n_pairs), 0)
    ir = lax.broadcasted_iota(jnp.int32, (rows, nodes), 0)

    @pl.loop(0, subs)
    def _(b):
        e = edges[b]
        srcT = (it == e[0:1, :]).astype(F32).astype(BF)
        dstT = (it == e[1:2, :]).astype(F32).astype(BF)
        cnt = _nt(srcT, dstT)
        deg[pl.ds(b, 1), :] = 1.0 / (1.0 + jnp.sum(cnt, axis=0, keepdims=True))
        adjT[b] = cnt.astype(BF)
        p = pairs[b]
        prs = jnp.concatenate([p[0:1, :], p[1:2, :]], axis=1)
        hot[b] = (ip == prs).astype(F32).astype(BF)
        at = pl.ds(pl.multiple_of(b * nodes, LANES), nodes)
        pick[:, at] = (ir == slots[pl.ds(b, 1), :]).astype(F32).astype(BF)

    wcol[...] = jnp.broadcast_to(wread[...], (2 * n_pairs, feats)).T
    for i in (0, 1, 5, 6):
        sends[i].start()
    for c in copies[4:9]:
        c.wait()
    wqmT[0 : 3 * feats, :] = wqkv[...].T
    wqmT[3 * feats : 4 * feats, :] = wmsg[...].T
    woT[...] = wo[...].T
    sends[2].start()
    wupT[...] = wup[...].T
    sends[3].start()
    wdownT[...] = wdown[...].T
    sends[4].start()
    for c in sends:
        c.wait()
    copies[9].wait()


def _hbm(*arrays):
    return [pltpu.with_memory_space_constraint(v, pltpu.HBM) for v in arrays]


def _prep(w_qkv, w_o, w_msg, w_up, w_down, edges, pairs, node_slots, w_read, store, rows):
    feats, hidden = w_up.shape
    subs, nodes = node_slots.shape
    n_edges, n_pairs = edges.shape[1], pairs.shape[1]
    out = [
        ((rows, subs * nodes), BF), ((4 * feats, feats), BF), ((subs, nodes, nodes), BF),
        ((subs, nodes), F32), ((feats, feats), BF), ((hidden, feats), BF), ((feats, hidden), BF),
        ((subs, nodes, 2 * n_pairs), BF), ((feats, 2 * n_pairs), F32),
    ]
    return pl.pallas_call(
        _prep_kernel,
        in_specs=[pl.BlockSpec(memory_space=pltpu.HBM)] * 10,
        out_specs=_vmem(2) + [pl.BlockSpec(memory_space=pltpu.HBM)] * 7 + _vmem(1),
        out_shape=[pltpu.VMEM(s, d) for s, d in out[:2]]
        + [pltpu.HBM(s, d) for s, d in out[2:]]
        + [pltpu.VMEM(store.shape, store.dtype)],
        scratch_shapes=[pltpu.VMEM(s, d) for s, d in out[2:]]
        + [
            pltpu.VMEM((feats, 3 * feats), BF),
            pltpu.VMEM((feats, feats), BF),
            pltpu.VMEM((feats, feats), BF),
            pltpu.VMEM((feats, hidden), BF),
            pltpu.VMEM((hidden, feats), BF),
            pltpu.VMEM((subs, 2, n_edges), jnp.int32),
            pltpu.VMEM((subs, 2, n_pairs), jnp.int32),
            pltpu.VMEM((subs, nodes), jnp.int32),
            pltpu.VMEM((1, feats), F32),
            pltpu.SemaphoreType.DMA((10,)),
            pltpu.SemaphoreType.DMA((7,)),
        ],
        compiler_params=pltpu.CompilerParams(vmem_limit_bytes=24 << 20),
        cost_estimate=pl.CostEstimate(
            flops=2 * subs * nodes * nodes * n_edges, bytes_accessed=8 << 20, transcendentals=0
        ),
        name="prep",
    )(
        *_hbm(
            w_qkv, w_o, w_msg, w_up, w_down, edges.transpose(0, 2, 1),
            pairs.transpose(0, 2, 1), node_slots, w_read.reshape(1, feats), store,
        )
    )


FWD_GROUP = 4
BWD_GROUP = 4


FWD_SKEW = 0
MID_SKEW = 0
BWD_SKEW = 0


def _wave(items, skew, stages):
    for step in range(len(stages) + skew * (items - 1) if skew else len(stages)):
        for i in range(items):
            s = step - skew * i
            if 0 <= s < len(stages):
                stages[s](i)


def _over(subs, group, stage):
    if subs % group:
        group = 1
    if group == subs:
        for b in range(subs):
            stage(b)
    else:

        @pl.loop(0, subs // group)
        def _(i):
            for k in range(group):
                stage(i * group + k)


def _step_kernel(packed, *refs):
    fetched_ref, pick, wqmT = refs[:3]
    sources = refs[3:14]
    preds_ref = refs[14]
    outs = refs[15 : 15 + (2 if packed else 6)]
    refs = refs[15 + len(outs) :]
    adjT, deg, woT, wupT, wdownT, hot_ref, wcol, targets_ref, wo, wup, wdown = refs[:11]
    (
        x_s, y_s, dy_s, att_s, datt_s, h_s, g_s, do_s, dup_s, da_s, pf_s, p_s, ds_s, obj_s, gq_s, gu_s, gd_s,
        agg_s, n1_s, n2_s, up_s, out_s, dout_s, hi_s, lo_s, r1_s, r2_s, r3_s,
        sems,
    ) = refs[11:]
    copies = [
        pltpu.make_async_copy(s, d, sems.at[i]) for i, (s, d) in enumerate(zip(sources, refs[:11]))
    ]
    for c in copies:
        c.start()
    feats = wo.shape[0]
    hidden = wup.shape[1]
    subs, nodes = deg.shape
    n_pairs = targets_ref.shape[1]
    n_all = subs * n_pairs
    hd = feats // HEADS
    scale = hd ** -0.5

    def lanes(b):
        if isinstance(b, int):
            return slice(b * nodes, (b + 1) * nodes)
        return pl.ds(pl.multiple_of(b * nodes, LANES), nodes)

    def head(part, h):
        return slice(part * feats + h * hd, part * feats + (h + 1) * hd)

    obj_s[...] = jnp.zeros_like(obj_s)
    x_s[...] = _nn(fetched_ref[...].T, pick[...]).astype(BF)
    y_s[...] = _nn(wqmT[...], x_s[...]).astype(BF)

    def attend(b):
        at = lanes(b)
        def score(h):
            pf_s[b, h] = _tn(y_s[head(1, h), at], y_s[head(0, h), at])

        def soften(h):
            s = pf_s[b, h]
            e = jnp.exp2((s - jnp.max(s, axis=0, keepdims=True)) * (scale * LOG2E))
            pf = e * (1.0 / jnp.sum(e, axis=0, keepdims=True))
            pf_s[b, h] = pf
            p_s[b, h] = pf.astype(BF)

        def blend(h):
            att_s[head(0, h), at] = _nn(y_s[head(2, h), at], p_s[b, h]).astype(BF)

        _wave(HEADS, FWD_SKEW, (score, soften, blend))

    _over(subs, FWD_GROUP, attend)
    for c in copies:
        c.wait()

    total = subs * nodes
    msg = slice(3 * feats, 4 * feats)

    def block(b):
        return slice(b * nodes, (b + 1) * nodes)

    def cuts(b):
        return [block(b)]

    def branches(b):
        at = block(b)
        agg_s[:, at] = _nn(y_s[msg, at], adjT[b])
        n2_s[:, at] = _nn(woT[...], att_s[:, at])

    def branch_norms(b):
        for c in cuts(b):
            w = c.start % nodes
            base = x_s[:, c].astype(F32)
            agg = (agg_s[:, c] + y_s[msg, c].astype(F32)) * deg[b : b + 1, w : w + nodes]
            agg_s[:, c] = agg
            n1, r1_s[0:1, c] = _norm(base + jnp.maximum(agg, 0.0))
            n2, r2_s[0:1, c] = _norm(base + n2_s[:, c])
            n1_s[:, c] = n1
            n2_s[:, c] = n2
            h_s[:, c] = (n1 + n2).astype(BF)

    def raise_up(b):
        up_s[:, block(b)] = _nn(wupT[...], h_s[:, block(b)])

    def gate(b):
        for c in cuts(b):
            up = up_s[:, c]
            sq = up * up
            th = jnp.tanh((GELU_C * up) * (1.0 + GELU_A * sq))
            half = 0.5 + 0.5 * th
            g_s[:, c] = (up * half).astype(BF)
            slope = (1.0 - th * th) * (GELU_C + (3.0 * GELU_A * GELU_C) * sq)
            up_s[:, c] = half + (0.5 * up) * slope

    def lower_down(b):
        out_s[:, block(b)] = _nn(wdownT[...], g_s[:, block(b)])

    def out_norm(b):
        for c in cuts(b):
            out, r3_s[0:1, c] = _norm(h_s[:, c].astype(F32) + out_s[:, c])
            out_s[:, c] = out
            hi_s[:, c], lo_s[:, c] = _split(out)

    def readout(b):
        hot = hot_ref[b]
        at = block(b)
        lr = _nn(hi_s[:, at], hot) + _nn(lo_s[:, at], hot)
        rl = pltpu.roll(lr, n_pairs, 1) * wcol[...]
        preds = jnp.sum(lr * rl, axis=0, keepdims=True)
        tgt = targets_ref[b : b + 1, :]
        diff = preds - jnp.concatenate([tgt, tgt], axis=1)
        preds_ref[b : b + 1, :] = preds[:, 0:n_pairs]
        obj_s[0:1, 0:n_pairs] += diff[:, 0:n_pairs] * diff[:, 0:n_pairs]
        hi, lo = _split((diff * (2.0 / n_all)) * rl)
        dout_s[:, at] = _nt(hi, hot) + _nt(lo, hot)

    def out_back(b):
        for c in cuts(b):
            do_s[:, c] = _norm_back(dout_s[:, c], out_s[:, c], r3_s[0:1, c]).astype(BF)

    def down_back(b):
        dup_s[:, block(b)] = _nn(wdown[...], do_s[:, block(b)]).astype(BF)

    def gate_back(b):
        for c in cuts(b):
            dup_s[:, c] = (up_s[:, c] * dup_s[:, c].astype(F32)).astype(BF)

    def up_back(b):
        da_s[:, block(b)] = _nn(wup[...], dup_s[:, block(b)]).astype(BF)

    def norms_back(b):
        for c in cuts(b):
            w = c.start % nodes
            dl = (do_s[:, c].astype(F32) + da_s[:, c].astype(F32)).astype(BF).astype(F32)
            d1 = _norm_back(dl, n1_s[:, c], r1_s[0:1, c])
            d1 = jnp.where(agg_s[:, c] > 0.0, d1, 0.0) * deg[b : b + 1, w : w + nodes]
            hi_s[:, c] = d1.astype(BF)
            da_s[:, c] = _norm_back(dl, n2_s[:, c], r2_s[0:1, c]).astype(BF)

    def branches_back(b):
        at = block(b)
        datt_s[:, at] = _nn(wo[...], da_s[:, at]).astype(BF)
        dagg = hi_s[:, at]
        dxw = _nt(dagg, adjT[b]).astype(BF)
        dy_s[msg, at] = (dxw.astype(F32) + dagg.astype(F32)).astype(BF)

    stages = (
        branches, branch_norms, raise_up, gate, lower_down, out_norm, readout, out_back,
        down_back, gate_back, up_back, norms_back, branches_back,
    )
    _wave(subs, MID_SKEW, stages)

    def attend_back(b):
        at = lanes(b)
        def score(h):
            ds_s[h] = _tn(y_s[head(2, h), at], datt_s[head(0, h), at]).astype(BF)

        def soften(h):
            pf = pf_s[b, h]
            t = ds_s[h].astype(F32) * pf
            ds_s[h] = ((t - pf * jnp.sum(t, axis=0, keepdims=True)) * scale).astype(BF)

        def blend(h):
            dy_s[head(2, h), at] = _nt(datt_s[head(0, h), at], p_s[b, h]).astype(BF)
            dy_s[head(0, h), at] = _nn(y_s[head(1, h), at], ds_s[h]).astype(BF)
            dy_s[head(1, h), at] = _nt(y_s[head(0, h), at], ds_s[h]).astype(BF)

        _wave(HEADS, BWD_SKEW, (score, soften, blend))

    _over(subs, BWD_GROUP, attend_back)

    gq_s[:, 4 * feats :] = _nt(att_s[...], da_s[...]).astype(BF)
    gu_s[...] = _nt(h_s[...], dup_s[...]).astype(BF)
    gd_s[...] = _nt(g_s[...], do_s[...]).astype(BF)
    gq_s[:, 0 : 4 * feats] = _nt(x_s[...], dy_s[...]).astype(BF)
    obj = jnp.sum(obj_s[0:1, :], axis=1, keepdims=True) / n_all
    if packed:
        keep_ref, send_ref = outs
        slabs = keep_ref.shape[0]
        rows = feats // (2 * slabs)
        core = lax.axis_index("store") % 2
        obj_block = _spread(obj, TAIL)
        per = hidden // feats
        for ref, side in ((keep_ref, core), (send_ref, 1 - core)):
            for j in range(slabs):
                d = 2 * j + side
                r = pl.ds(pl.multiple_of(d * rows, rows), rows)
                pieces = [gq_s[r, c : c + LANES] for c in range(0, 5 * feats, LANES)]
                pieces += [gu_s[r, c : c + LANES] for c in range(0, hidden, LANES)]
                for i in range(per):
                    r = pl.ds(pl.multiple_of(d * (rows * per) + i * rows, rows), rows)
                    pieces += [gd_s[r, c : c + LANES] for c in range(0, feats, LANES)]
                for i, piece in enumerate(pieces):
                    ref[j, i * rows : (i + 1) * rows, :] = piece
                ref[j, len(pieces) * rows :, :] = obj_block
    else:
        obj_ref, gqkv_ref, go_ref, gmsg_ref, gup_ref, gdown_ref = outs
        obj_ref[...] = jnp.broadcast_to(obj, obj_ref.shape)
        gqkv_ref[...] = gq_s[:, 0 : 3 * feats]
        gmsg_ref[...] = gq_s[:, 3 * feats : 4 * feats]
        go_ref[...] = gq_s[:, 4 * feats :]
        gup_ref[...] = gu_s[...]
        gdown_ref[...] = gd_s[...]


def _weights(rows):
    shape = (rows, LANES)
    at = lax.broadcasted_iota(jnp.int32, shape, 0) * LANES + lax.broadcasted_iota(jnp.int32, shape, 1)
    return 1.0 + at.astype(F32) / (rows * LANES)


def _spread(value, rows):
    return (value * _weights(rows)).astype(BF)


def _gather_terms(block):
    w = _weights(block.shape[0])
    return jnp.sum(block * w) / jnp.sum(w * w)


TAIL = 8


def _pair_kernel(a_ref, b_ref, first_ref, second_ref):
    cut = first_ref.shape[1]
    first_ref[...] = a_ref[:, :cut, :].astype(F32) + b_ref[:, :cut, :].astype(F32)
    second_ref[...] = a_ref[:, cut:, :].astype(F32) + b_ref[:, cut:, :].astype(F32)


def _halving(halves, groups):
    idx = lax.axis_index("store")
    bits = groups.bit_length() - 2
    orders = [list(range(1, bits + 1)) for _ in halves]
    if bits > 1:
        orders[1][:2] = [2, 1]
    halves = [h.reshape((2,) * bits + h.shape[1:]) for h in halves]
    for step in range(bits):
        kept, got = [], []
        for h, order in zip(halves, orders):
            axis = bits - order[step]
            bit = (idx >> order[step]) & 1
            perm = [(i, i ^ (1 << order[step])) for i in range(groups)]
            send = lax.dynamic_slice_in_dim(h, 1 - bit, 1, axis).astype(BF)
            got.append(lax.ppermute(send, "store", perm))
            kept.append(lax.dynamic_slice_in_dim(h, bit, 1, axis))
        halves = [k + g.astype(F32) for k, g in zip(kept, got)]
    return [h.reshape(h.shape[-2:]) for h in halves]


def _final_kernel(groups, first_ref, second_ref, loss_ref, gqkv, go, gmsg, gup, gdown):
    total = jnp.concatenate([first_ref[...], second_ref[...]], axis=0)
    height = total.shape[0]
    rows, feats = go.shape
    hidden = gup.shape[1]
    places = [(gqkv, 0, c) for c in range(0, 3 * feats, LANES)]
    places += [(gmsg, 0, c) for c in range(0, feats, LANES)]
    places += [(go, 0, c) for c in range(0, feats, LANES)]
    places += [(gup, 0, c) for c in range(0, hidden, LANES)]
    for i in range(hidden // feats):
        places += [(gdown, i * rows, c) for c in range(0, feats, LANES)]
    for i, (ref, r, c) in enumerate(places):
        ref[r : r + rows, c : c + LANES] = total[i * rows : (i + 1) * rows, :]
    loss_ref[0] = _gather_terms(total[height - TAIL :, :]) / groups


def _vmem(n):
    return [pl.BlockSpec(memory_space=pltpu.VMEM)] * n


def local_step(prep, fetched, targets, weights, groups):
    feats, hidden = weights[1].shape
    subs, nodes = prep[3].shape
    n_pairs = targets.shape[1]
    total = subs * nodes
    sources = (*prep[2:], targets, *weights)
    rows = feats // groups
    packed = groups % 2 == 0 and feats % groups == 0 and hidden % feats == 0 and rows % 16 == 0
    packed = packed and feats % LANES == 0 and groups & (groups - 1) == 0
    out = [((subs, n_pairs), F32)]
    if packed:
        slab = (groups // 2, rows * (5 * feats + 2 * hidden) // LANES + TAIL, LANES)
        out += [(slab, BF), (slab, BF)]
    else:
        out += [
            ((8, LANES), F32), ((feats, 3 * feats), BF), ((feats, feats), BF), ((feats, feats), BF),
            ((feats, hidden), BF), ((hidden, feats), BF),
        ]
    res = pl.pallas_call(
        lambda *refs: _step_kernel(packed, *refs),
        in_specs=_vmem(3) + [pl.BlockSpec(memory_space=pltpu.HBM)] * len(sources),
        out_specs=_vmem(len(out)),
        out_shape=[jax.ShapeDtypeStruct(s, d) for s, d in out],
        scratch_shapes=[pltpu.VMEM(v.shape, v.dtype) for v in sources]
        + [
            pltpu.VMEM((feats, total), BF),
            pltpu.VMEM((4 * feats, total), BF),
            pltpu.VMEM((4 * feats, total), BF),
            pltpu.VMEM((feats, total), BF),
            pltpu.VMEM((feats, total), BF),
            pltpu.VMEM((feats, total), BF),
            pltpu.VMEM((hidden, total), BF),
            pltpu.VMEM((feats, total), BF),
            pltpu.VMEM((hidden, total), BF),
            pltpu.VMEM((feats, total), BF),
            pltpu.VMEM((subs, HEADS, nodes, nodes), F32),
            pltpu.VMEM((subs, HEADS, nodes, nodes), BF),
            pltpu.VMEM((HEADS, nodes, nodes), BF),
            pltpu.VMEM((8, LANES), F32),
            pltpu.VMEM((feats, 5 * feats), BF),
            pltpu.VMEM((feats, hidden), BF),
            pltpu.VMEM((hidden, feats), BF),
            pltpu.VMEM((feats, total), F32),
            pltpu.VMEM((feats, total), F32),
            pltpu.VMEM((feats, total), F32),
            pltpu.VMEM((hidden, total), F32),
            pltpu.VMEM((feats, total), F32),
            pltpu.VMEM((feats, total), F32),
            pltpu.VMEM((feats, total), BF),
            pltpu.VMEM((feats, total), BF),
            pltpu.VMEM((8, total), F32),
            pltpu.VMEM((8, total), F32),
            pltpu.VMEM((8, total), F32),
            pltpu.SemaphoreType.DMA((len(sources),)),
        ],
        compiler_params=pltpu.CompilerParams(vmem_limit_bytes=40 << 20),
        name="graph_step",
    )(fetched, *prep[:2], *_hbm(*sources))
    return packed, res


def shards(
    store_feats, requests, node_slots, edges, pairs, targets,
    w_qkv, w_o, w_msg, w_up, w_down, w_read,
):
    feats = store_feats.shape[1]
    hidden = w_up.shape[1]
    groups = lax.axis_size("store")
    wanted = lax.all_to_all(
        requests.reshape(groups, 1, -1), "store", split_axis=0, concat_axis=0, tiled=True
    )
    *prep, store = _prep(
        w_qkv, w_o, w_msg, w_up, w_down, edges, pairs, node_slots, w_read, store_feats,
        wanted.size,
    )
    picked = pl.pallas_call(
        _serve_kernel,
        in_specs=_vmem(2),
        out_specs=pl.BlockSpec(memory_space=pltpu.VMEM),
        out_shape=jax.ShapeDtypeStruct((wanted.size, feats), store_feats.dtype),
        scratch_shapes=[pltpu.VMEM((wanted.size, 1), jnp.int32)],
        compiler_params=pltpu.CompilerParams(vmem_limit_bytes=16 << 20),
        name="serve",
    )(wanted, store)
    picked = picked.reshape(groups, -1, feats)
    fetched = lax.all_to_all(picked, "store", split_axis=0, concat_axis=0, tiled=True)
    fetched = fetched.reshape(-1, feats)
    packed, (preds, *terms) = local_step(prep, fetched, targets, (w_o, w_up, w_down), groups)
    if packed:
        keep, send = terms
        rows = feats // groups
        got = lax.ppermute(send, "store", [(i, i ^ 1) for i in range(groups)])
        height = keep.shape[1]
        cut = height // 2 // 16 * 16
        paired = pl.pallas_call(
            _pair_kernel,
            in_specs=_vmem(2),
            out_specs=_vmem(2),
            out_shape=[
                jax.ShapeDtypeStruct((keep.shape[0], h, LANES), F32) for h in (cut, height - cut)
            ],
            compiler_params=pltpu.CompilerParams(vmem_limit_bytes=8 << 20),
            name="pair_sum",
        )(keep, got)
        shared = _halving(list(paired), groups)
        loss, *shares = pl.pallas_call(
            lambda *refs: _final_kernel(groups, *refs),
            in_specs=_vmem(2),
            out_specs=[pl.BlockSpec(memory_space=pltpu.SMEM)] + _vmem(5),
            out_shape=[
                jax.ShapeDtypeStruct((1,), F32),
                jax.ShapeDtypeStruct((rows, 3 * feats), F32),
                jax.ShapeDtypeStruct((rows, feats), F32),
                jax.ShapeDtypeStruct((rows, feats), F32),
                jax.ShapeDtypeStruct((rows, hidden), F32),
                jax.ShapeDtypeStruct((rows * (hidden // feats), feats), F32),
            ],
            compiler_params=pltpu.CompilerParams(vmem_limit_bytes=8 << 20),
            name="final_sum",
        )(*shared)
    else:
        obj, *grads = terms
        shares = [
            lax.psum_scatter(lax.optimization_barrier(g.astype(F32)), "store", scatter_dimension=0, tiled=True)
            for g in grads
        ]
        loss = (lax.psum(obj[0, 0], "store") / groups).reshape(1)
    return (preds, loss, *shares)


def solution(mesh):
    rows = P(("parts", "store"), None)
    deep = P(("parts", "store"), None, None)
    in_specs = (rows, rows, rows, deep, deep, rows, P(), P(), P(), P(), P(), P())
    out_specs = (rows, P("parts"), rows, rows, rows, rows, rows)
    return jax.shard_map(shards, mesh=mesh, in_specs=in_specs, out_specs=out_specs, check_vma=False)
```

```python
import jax
import jax.numpy as jnp
from jax import lax
from jax.experimental import pallas as pl
from jax.experimental.pallas import tpu as pltpu
from jax.sharding import PartitionSpec as P

HEADS = 8
BF = jnp.bfloat16
F32 = jnp.float32


def _nn(a, b):
    return lax.dot_general(a, b, (((1,), (0,)), ((), ())), preferred_element_type=F32)


def _nt(a, b):
    return lax.dot_general(a, b, (((1,), (1,)), ((), ())), preferred_element_type=F32)


def _tn(a, b):
    return lax.dot_general(a, b, (((0,), (0,)), ((), ())), preferred_element_type=F32)


def _split(v):
    hi = v.astype(BF)
    lo = (v - hi.astype(F32)).astype(BF)
    return hi, lo


def _norm(v):
    c = v - jnp.mean(v, axis=0, keepdims=True)
    r = lax.rsqrt(jnp.mean(c * c, axis=0, keepdims=True) + 1e-05)
    return c * r, r


def _norm_back(d, y, r):
    m1 = jnp.mean(d, axis=0, keepdims=True)
    m2 = jnp.mean(d * y, axis=0, keepdims=True)
    return (d - m1 - y * m2) * r


GELU_C = 0.7978845608028654
GELU_A = 0.044715
LOG2E = 1.4426950408889634

LANES = 128


def _serve_kernel(wanted, store, out, column):
    peers, _, cap = wanted.shape
    diagonal = lax.broadcasted_iota(jnp.int32, (cap, cap), 0) == lax.broadcasted_iota(
        jnp.int32, (cap, cap), 1
    )
    for o in range(peers):
        row = jnp.where(diagonal, wanted[o], 0)
        column[o * cap : (o + 1) * cap, :] = jnp.sum(row, axis=1, keepdims=True)
    rows = store.shape[0]
    step = rows // 4 if rows % 512 == 0 else rows
    lane = lax.broadcasted_iota(jnp.int32, (out.shape[0], step), 1)
    total = jnp.zeros(out.shape, F32)
    for at in range(0, rows, step):
        hot = (lane == column[...] - at).astype(F32).astype(BF)
        total = total + _nn(hot, store[at : at + step, :])
    out[...] = total.astype(out.dtype)


def _prep_kernel(
    wqkv_h, wo_h, wmsg_h, wup_h, wdown_h, edges_h, pairs_h, slots_h, wread_h, store_h, *refs
):
    pick, wqmT = refs[:2]
    results = refs[2:9]
    store = refs[9]
    adjT, deg, woT, wupT, wdownT, hot, wcol = refs[10:17]
    wqkv, wmsg, wo, wup, wdown, edges, pairs, slots, wread, sems, out_sems = refs[17:]
    moves = [
        (edges_h, edges), (slots_h, slots), (pairs_h, pairs), (wread_h, wread),
        (wqkv_h, wqkv), (wmsg_h, wmsg), (wo_h, wo), (wup_h, wup), (wdown_h, wdown),
        (store_h, store),
    ]
    copies = [pltpu.make_async_copy(s, d, sems.at[i]) for i, (s, d) in enumerate(moves)]
    sends = [
        pltpu.make_async_copy(s, d, out_sems.at[i])
        for i, (s, d) in enumerate(zip(refs[10:17], results))
    ]
    for c in copies:
        c.start()
    feats = wo.shape[0]
    subs, nodes = slots.shape
    rows = pick.shape[0]
    n_edges = edges.shape[2]
    n_pairs = pairs.shape[2]
    for c in copies[:4]:
        c.wait()
    it = lax.broadcasted_iota(jnp.int32, (nodes, n_edges), 0)
    ip = lax.broadcasted_iota(jnp.int32, (nodes, 2 * n_pairs), 0)
    ir = lax.broadcasted_iota(jnp.int32, (rows, nodes), 0)

    @pl.loop(0, subs)
    def _(b):
        e = edges[b]
        srcT = (it == e[0:1, :]).astype(F32).astype(BF)
        dstT = (it == e[1:2, :]).astype(F32).astype(BF)
        cnt = _nt(srcT, dstT)
        deg[pl.ds(b, 1), :] = 1.0 / (1.0 + jnp.sum(cnt, axis=0, keepdims=True))
        adjT[b] = cnt.astype(BF)
        p = pairs[b]
        prs = jnp.concatenate([p[0:1, :], p[1:2, :]], axis=1)
        hot[b] = (ip == prs).astype(F32).astype(BF)
        at = pl.ds(pl.multiple_of(b * nodes, LANES), nodes)
        pick[:, at] = (ir == slots[pl.ds(b, 1), :]).astype(F32).astype(BF)

    wcol[...] = jnp.broadcast_to(wread[...], (2 * n_pairs, feats)).T
    for i in (0, 1, 5, 6):
        sends[i].start()
    for c in copies[4:9]:
        c.wait()
    wqmT[0 : 3 * feats, :] = wqkv[...].T
    wqmT[3 * feats : 4 * feats, :] = wmsg[...].T
    woT[...] = wo[...].T
    sends[2].start()
    wupT[...] = wup[...].T
    sends[3].start()
    wdownT[...] = wdown[...].T
    sends[4].start()
    for c in sends:
        c.wait()
    copies[9].wait()


def _hbm(*arrays):
    return [pltpu.with_memory_space_constraint(v, pltpu.HBM) for v in arrays]


def _prep(w_qkv, w_o, w_msg, w_up, w_down, edges, pairs, node_slots, w_read, store, rows):
    feats, hidden = w_up.shape
    subs, nodes = node_slots.shape
    n_edges, n_pairs = edges.shape[1], pairs.shape[1]
    out = [
        ((rows, subs * nodes), BF), ((4 * feats, feats), BF), ((subs, nodes, nodes), BF),
        ((subs, nodes), F32), ((feats, feats), BF), ((hidden, feats), BF), ((feats, hidden), BF),
        ((subs, nodes, 2 * n_pairs), BF), ((feats, 2 * n_pairs), F32),
    ]
    return pl.pallas_call(
        _prep_kernel,
        in_specs=[pl.BlockSpec(memory_space=pltpu.HBM)] * 10,
        out_specs=_vmem(2) + [pl.BlockSpec(memory_space=pltpu.HBM)] * 7 + _vmem(1),
        out_shape=[pltpu.VMEM(s, d) for s, d in out[:2]]
        + [pltpu.HBM(s, d) for s, d in out[2:]]
        + [pltpu.VMEM(store.shape, store.dtype)],
        scratch_shapes=[pltpu.VMEM(s, d) for s, d in out[2:]]
        + [
            pltpu.VMEM((feats, 3 * feats), BF),
            pltpu.VMEM((feats, feats), BF),
            pltpu.VMEM((feats, feats), BF),
            pltpu.VMEM((feats, hidden), BF),
            pltpu.VMEM((hidden, feats), BF),
            pltpu.VMEM((subs, 2, n_edges), jnp.int32),
            pltpu.VMEM((subs, 2, n_pairs), jnp.int32),
            pltpu.VMEM((subs, nodes), jnp.int32),
            pltpu.VMEM((1, feats), F32),
            pltpu.SemaphoreType.DMA((10,)),
            pltpu.SemaphoreType.DMA((7,)),
        ],
        compiler_params=pltpu.CompilerParams(vmem_limit_bytes=24 << 20),
        cost_estimate=pl.CostEstimate(
            flops=2 * subs * nodes * nodes * n_edges, bytes_accessed=8 << 20, transcendentals=0
        ),
        name="prep",
    )(
        *_hbm(
            w_qkv, w_o, w_msg, w_up, w_down, edges.transpose(0, 2, 1),
            pairs.transpose(0, 2, 1), node_slots, w_read.reshape(1, feats), store,
        )
    )


FWD_GROUP = 4
BWD_GROUP = 4


FWD_SKEW = 0
MID_SKEW = 0
BWD_SKEW = 0


def _wave(items, skew, stages):
    for step in range(len(stages) + skew * (items - 1) if skew else len(stages)):
        for i in range(items):
            s = step - skew * i
            if 0 <= s < len(stages):
                stages[s](i)


def _over(subs, group, stage):
    if subs % group:
        group = 1
    if group == subs:
        for b in range(subs):
            stage(b)
    else:

        @pl.loop(0, subs // group)
        def _(i):
            for k in range(group):
                stage(i * group + k)


def _step_kernel(packed, *refs):
    fetched_ref, pick, wqmT = refs[:3]
    sources = refs[3:14]
    preds_ref = refs[14]
    outs = refs[15 : 15 + (4 if packed else 6)]
    refs = refs[15 + len(outs) :]
    adjT, deg, woT, wupT, wdownT, hot_ref, wcol, targets_ref, wo, wup, wdown = refs[:11]
    (
        x_s, y_s, dy_s, att_s, datt_s, h_s, g_s, do_s, dup_s, da_s, pf_s, p_s, ds_s, obj_s, gq_s, gu_s, gd_s,
        agg_s, n1_s, n2_s, up_s, out_s, dout_s, hi_s, lo_s, r1_s, r2_s, r3_s,
        sems,
    ) = refs[11:]
    copies = [
        pltpu.make_async_copy(s, d, sems.at[i]) for i, (s, d) in enumerate(zip(sources, refs[:11]))
    ]
    for c in copies:
        c.start()
    feats = wo.shape[0]
    hidden = wup.shape[1]
    subs, nodes = deg.shape
    n_pairs = targets_ref.shape[1]
    n_all = subs * n_pairs
    hd = feats // HEADS
    scale = hd ** -0.5

    def lanes(b):
        if isinstance(b, int):
            return slice(b * nodes, (b + 1) * nodes)
        return pl.ds(pl.multiple_of(b * nodes, LANES), nodes)

    def head(part, h):
        return slice(part * feats + h * hd, part * feats + (h + 1) * hd)

    obj_s[...] = jnp.zeros_like(obj_s)
    x_s[...] = _nn(fetched_ref[...].T, pick[...]).astype(BF)
    y_s[...] = _nn(wqmT[...], x_s[...]).astype(BF)

    def attend(b):
        at = lanes(b)
        def score(h):
            pf_s[b, h] = _tn(y_s[head(1, h), at], y_s[head(0, h), at])

        def soften(h):
            s = pf_s[b, h]
            e = jnp.exp2((s - jnp.max(s, axis=0, keepdims=True)) * (scale * LOG2E))
            pf = e * (1.0 / jnp.sum(e, axis=0, keepdims=True))
            pf_s[b, h] = pf
            p_s[b, h] = pf.astype(BF)

        def blend(h):
            att_s[head(0, h), at] = _nn(y_s[head(2, h), at], p_s[b, h]).astype(BF)

        _wave(HEADS, FWD_SKEW, (score, soften, blend))

    _over(subs, FWD_GROUP, attend)
    for c in copies:
        c.wait()

    total = subs * nodes
    msg = slice(3 * feats, 4 * feats)

    def block(b):
        return slice(b * nodes, (b + 1) * nodes)

    def cuts(b):
        return [block(b)]

    def branches(b):
        at = block(b)
        agg_s[:, at] = _nn(y_s[msg, at], adjT[b])
        n2_s[:, at] = _nn(woT[...], att_s[:, at])

    def branch_norms(b):
        for c in cuts(b):
            w = c.start % nodes
            base = x_s[:, c].astype(F32)
            agg = (agg_s[:, c] + y_s[msg, c].astype(F32)) * deg[b : b + 1, w : w + nodes]
            agg_s[:, c] = agg
            n1, r1_s[0:1, c] = _norm(base + jnp.maximum(agg, 0.0))
            n2, r2_s[0:1, c] = _norm(base + n2_s[:, c])
            n1_s[:, c] = n1
            n2_s[:, c] = n2
            h_s[:, c] = (n1 + n2).astype(BF)

    def raise_up(b):
        up_s[:, block(b)] = _nn(wupT[...], h_s[:, block(b)])

    def gate(b):
        for c in cuts(b):
            up = up_s[:, c]
            sq = up * up
            th = jnp.tanh((GELU_C * up) * (1.0 + GELU_A * sq))
            half = 0.5 + 0.5 * th
            g_s[:, c] = (up * half).astype(BF)
            slope = (1.0 - th * th) * (GELU_C + (3.0 * GELU_A * GELU_C) * sq)
            up_s[:, c] = half + (0.5 * up) * slope

    def lower_down(b):
        out_s[:, block(b)] = _nn(wdownT[...], g_s[:, block(b)])

    def out_norm(b):
        for c in cuts(b):
            out, r3_s[0:1, c] = _norm(h_s[:, c].astype(F32) + out_s[:, c])
            out_s[:, c] = out
            hi_s[:, c], lo_s[:, c] = _split(out)

    def readout(b):
        hot = hot_ref[b]
        at = block(b)
        lr = _nn(hi_s[:, at], hot) + _nn(lo_s[:, at], hot)
        rl = pltpu.roll(lr, n_pairs, 1) * wcol[...]
        preds = jnp.sum(lr * rl, axis=0, keepdims=True)
        tgt = targets_ref[b : b + 1, :]
        diff = preds - jnp.concatenate([tgt, tgt], axis=1)
        preds_ref[b : b + 1, :] = preds[:, 0:n_pairs]
        obj_s[0:1, 0:n_pairs] += diff[:, 0:n_pairs] * diff[:, 0:n_pairs]
        hi, lo = _split((diff * (2.0 / n_all)) * rl)
        dout_s[:, at] = _nt(hi, hot) + _nt(lo, hot)

    def out_back(b):
        for c in cuts(b):
            do_s[:, c] = _norm_back(dout_s[:, c], out_s[:, c], r3_s[0:1, c]).astype(BF)

    def down_back(b):
        dup_s[:, block(b)] = _nn(wdown[...], do_s[:, block(b)]).astype(BF)

    def gate_back(b):
        for c in cuts(b):
            dup_s[:, c] = (up_s[:, c] * dup_s[:, c].astype(F32)).astype(BF)

    def up_back(b):
        da_s[:, block(b)] = _nn(wup[...], dup_s[:, block(b)]).astype(BF)

    def norms_back(b):
        for c in cuts(b):
            w = c.start % nodes
            dl = (do_s[:, c].astype(F32) + da_s[:, c].astype(F32)).astype(BF).astype(F32)
            d1 = _norm_back(dl, n1_s[:, c], r1_s[0:1, c])
            d1 = jnp.where(agg_s[:, c] > 0.0, d1, 0.0) * deg[b : b + 1, w : w + nodes]
            hi_s[:, c] = d1.astype(BF)
            da_s[:, c] = _norm_back(dl, n2_s[:, c], r2_s[0:1, c]).astype(BF)

    def branches_back(b):
        at = block(b)
        datt_s[:, at] = _nn(wo[...], da_s[:, at]).astype(BF)
        dagg = hi_s[:, at]
        dxw = _nt(dagg, adjT[b]).astype(BF)
        dy_s[msg, at] = (dxw.astype(F32) + dagg.astype(F32)).astype(BF)

    stages = (
        branches, branch_norms, raise_up, gate, lower_down, out_norm, readout, out_back,
        down_back, gate_back, up_back, norms_back, branches_back,
    )
    _wave(subs, MID_SKEW, stages)

    def attend_back(b):
        at = lanes(b)
        def score(h):
            ds_s[h] = _tn(y_s[head(2, h), at], datt_s[head(0, h), at]).astype(BF)

        def soften(h):
            pf = pf_s[b, h]
            t = ds_s[h].astype(F32) * pf
            ds_s[h] = ((t - pf * jnp.sum(t, axis=0, keepdims=True)) * scale).astype(BF)

        def blend(h):
            dy_s[head(2, h), at] = _nt(datt_s[head(0, h), at], p_s[b, h]).astype(BF)
            dy_s[head(0, h), at] = _nn(y_s[head(1, h), at], ds_s[h]).astype(BF)
            dy_s[head(1, h), at] = _nt(y_s[head(0, h), at], ds_s[h]).astype(BF)

        _wave(HEADS, BWD_SKEW, (score, soften, blend))

    _over(subs, BWD_GROUP, attend_back)

    gq_s[:, 4 * feats :] = _nt(att_s[...], da_s[...]).astype(BF)
    gu_s[...] = _nt(h_s[...], dup_s[...]).astype(BF)
    gd_s[...] = _nt(g_s[...], do_s[...]).astype(BF)
    gq_s[:, 0 : 4 * feats] = _nt(x_s[...], dy_s[...]).astype(BF)
    obj = jnp.sum(obj_s[0:1, :], axis=1, keepdims=True) / n_all
    if packed:
        slabs, cut, _ = outs[0].shape
        rows = feats // (2 * slabs)
        core = lax.axis_index("store") % 2
        obj_block = _spread(obj, TAIL)
        per = hidden // feats
        for first, second, side in ((outs[0], outs[1], core), (outs[2], outs[3], 1 - core)):
            for j in range(slabs):
                d = 2 * j + side
                r = pl.ds(pl.multiple_of(d * rows, rows), rows)
                pieces = [gq_s[r, c : c + LANES] for c in range(0, 5 * feats, LANES)]
                pieces += [gu_s[r, c : c + LANES] for c in range(0, hidden, LANES)]
                for i in range(per):
                    r = pl.ds(pl.multiple_of(d * (rows * per) + i * rows, rows), rows)
                    pieces += [gd_s[r, c : c + LANES] for c in range(0, feats, LANES)]
                whole = cut // rows
                for i, piece in enumerate(pieces[:whole]):
                    first[j, i * rows : (i + 1) * rows, :] = piece
                for i, piece in enumerate(pieces[whole:]):
                    second[j, i * rows : (i + 1) * rows, :] = piece
                second[j, (len(pieces) - whole) * rows :, :] = obj_block
    else:
        obj_ref, gqkv_ref, go_ref, gmsg_ref, gup_ref, gdown_ref = outs
        obj_ref[...] = jnp.broadcast_to(obj, obj_ref.shape)
        gqkv_ref[...] = gq_s[:, 0 : 3 * feats]
        gmsg_ref[...] = gq_s[:, 3 * feats : 4 * feats]
        go_ref[...] = gq_s[:, 4 * feats :]
        gup_ref[...] = gu_s[...]
        gdown_ref[...] = gd_s[...]


def _weights(rows):
    shape = (rows, LANES)
    at = lax.broadcasted_iota(jnp.int32, shape, 0) * LANES + lax.broadcasted_iota(jnp.int32, shape, 1)
    return 1.0 + at.astype(F32) / (rows * LANES)


def _spread(value, rows):
    return (value * _weights(rows)).astype(BF)


def _gather_terms(block):
    w = _weights(block.shape[0])
    return jnp.sum(block * w) / jnp.sum(w * w)


TAIL = 8


def _pair_kernel(a_ref, b_ref, o_ref):
    o_ref[...] = a_ref[...].astype(F32) + b_ref[...].astype(F32)


def _halving(halves, groups):
    idx = lax.axis_index("store")
    bits = groups.bit_length() - 2
    orders = [list(range(1, bits + 1)) for _ in halves]
    if bits > 1:
        orders[1][:2] = [2, 1]
    halves = [h.reshape((2,) * bits + h.shape[1:]) for h in halves]
    for step in range(bits):
        kept, got = [], []
        for h, order in zip(halves, orders):
            axis = bits - order[step]
            bit = (idx >> order[step]) & 1
            perm = [(i, i ^ (1 << order[step])) for i in range(groups)]
            send = lax.dynamic_slice_in_dim(h, 1 - bit, 1, axis).astype(BF)
            got.append(lax.ppermute(send, "store", perm))
            kept.append(lax.dynamic_slice_in_dim(h, bit, 1, axis))
        halves = [k + g.astype(F32) for k, g in zip(kept, got)]
    return [h.reshape(h.shape[-2:]) for h in halves]


def _final_kernel(groups, first_ref, second_ref, loss_ref, gqkv, go, gmsg, gup, gdown):
    total = jnp.concatenate([first_ref[...], second_ref[...]], axis=0)
    height = total.shape[0]
    rows, feats = go.shape
    hidden = gup.shape[1]
    places = [(gqkv, 0, c) for c in range(0, 3 * feats, LANES)]
    places += [(gmsg, 0, c) for c in range(0, feats, LANES)]
    places += [(go, 0, c) for c in range(0, feats, LANES)]
    places += [(gup, 0, c) for c in range(0, hidden, LANES)]
    for i in range(hidden // feats):
        places += [(gdown, i * rows, c) for c in range(0, feats, LANES)]
    for i, (ref, r, c) in enumerate(places):
        ref[r : r + rows, c : c + LANES] = total[i * rows : (i + 1) * rows, :]
    loss_ref[0] = _gather_terms(total[height - TAIL :, :]) / groups


def _vmem(n):
    return [pl.BlockSpec(memory_space=pltpu.VMEM)] * n


def local_step(prep, fetched, targets, weights, groups):
    feats, hidden = weights[1].shape
    subs, nodes = prep[3].shape
    n_pairs = targets.shape[1]
    total = subs * nodes
    sources = (*prep[2:], targets, *weights)
    rows = feats // groups
    packed = groups % 2 == 0 and feats % groups == 0 and hidden % feats == 0 and rows % 16 == 0
    packed = packed and feats % LANES == 0 and groups & (groups - 1) == 0
    out = [((subs, n_pairs), F32)]
    if packed:
        height = rows * (5 * feats + 2 * hidden) // LANES
        cut = height // (2 * rows) * rows
        sizes = (cut, height - cut + TAIL)
        out += [((groups // 2, h, LANES), BF) for h in sizes + sizes]
    else:
        out += [
            ((8, LANES), F32), ((feats, 3 * feats), BF), ((feats, feats), BF), ((feats, feats), BF),
            ((feats, hidden), BF), ((hidden, feats), BF),
        ]
    res = pl.pallas_call(
        lambda *refs: _step_kernel(packed, *refs),
        in_specs=_vmem(3) + [pl.BlockSpec(memory_space=pltpu.HBM)] * len(sources),
        out_specs=_vmem(len(out)),
        out_shape=[jax.ShapeDtypeStruct(s, d) for s, d in out],
        scratch_shapes=[pltpu.VMEM(v.shape, v.dtype) for v in sources]
        + [
            pltpu.VMEM((feats, total), BF),
            pltpu.VMEM((4 * feats, total), BF),
            pltpu.VMEM((4 * feats, total), BF),
            pltpu.VMEM((feats, total), BF),
            pltpu.VMEM((feats, total), BF),
            pltpu.VMEM((feats, total), BF),
            pltpu.VMEM((hidden, total), BF),
            pltpu.VMEM((feats, total), BF),
            pltpu.VMEM((hidden, total), BF),
            pltpu.VMEM((feats, total), BF),
            pltpu.VMEM((subs, HEADS, nodes, nodes), F32),
            pltpu.VMEM((subs, HEADS, nodes, nodes), BF),
            pltpu.VMEM((HEADS, nodes, nodes), BF),
            pltpu.VMEM((8, LANES), F32),
            pltpu.VMEM((feats, 5 * feats), BF),
            pltpu.VMEM((feats, hidden), BF),
            pltpu.VMEM((hidden, feats), BF),
            pltpu.VMEM((feats, total), F32),
            pltpu.VMEM((feats, total), F32),
            pltpu.VMEM((feats, total), F32),
            pltpu.VMEM((hidden, total), F32),
            pltpu.VMEM((feats, total), F32),
            pltpu.VMEM((feats, total), F32),
            pltpu.VMEM((feats, total), BF),
            pltpu.VMEM((feats, total), BF),
            pltpu.VMEM((8, total), F32),
            pltpu.VMEM((8, total), F32),
            pltpu.VMEM((8, total), F32),
            pltpu.SemaphoreType.DMA((len(sources),)),
        ],
        compiler_params=pltpu.CompilerParams(vmem_limit_bytes=40 << 20),
        name="graph_step",
    )(fetched, *prep[:2], *_hbm(*sources))
    return packed, res


def shards(
    store_feats, requests, node_slots, edges, pairs, targets,
    w_qkv, w_o, w_msg, w_up, w_down, w_read,
):
    feats = store_feats.shape[1]
    hidden = w_up.shape[1]
    groups = lax.axis_size("store")
    wanted = lax.all_to_all(
        requests.reshape(groups, 1, -1), "store", split_axis=0, concat_axis=0, tiled=True
    )
    *prep, store = _prep(
        w_qkv, w_o, w_msg, w_up, w_down, edges, pairs, node_slots, w_read, store_feats,
        wanted.size,
    )
    picked = pl.pallas_call(
        _serve_kernel,
        in_specs=_vmem(2),
        out_specs=pl.BlockSpec(memory_space=pltpu.VMEM),
        out_shape=jax.ShapeDtypeStruct((wanted.size, feats), store_feats.dtype),
        scratch_shapes=[pltpu.VMEM((wanted.size, 1), jnp.int32)],
        compiler_params=pltpu.CompilerParams(vmem_limit_bytes=16 << 20),
        name="serve",
    )(wanted, store)
    picked = picked.reshape(groups, -1, feats)
    fetched = lax.all_to_all(picked, "store", split_axis=0, concat_axis=0, tiled=True)
    fetched = fetched.reshape(-1, feats)
    packed, (preds, *terms) = local_step(prep, fetched, targets, (w_o, w_up, w_down), groups)
    if packed:
        rows = feats // groups
        paired = []
        for keep, send in zip(terms[:2], terms[2:]):
            got = lax.ppermute(send, "store", [(i, i ^ 1) for i in range(groups)])
            paired.append(
                pl.pallas_call(
                    _pair_kernel,
                    in_specs=_vmem(2),
                    out_specs=pl.BlockSpec(memory_space=pltpu.VMEM),
                    out_shape=jax.ShapeDtypeStruct(keep.shape, F32),
                    compiler_params=pltpu.CompilerParams(vmem_limit_bytes=8 << 20),
                    name="pair_sum",
                )(keep, got)
            )
        shared = _halving(paired, groups)
        loss, *shares = pl.pallas_call(
            lambda *refs: _final_kernel(groups, *refs),
            in_specs=_vmem(2),
            out_specs=[pl.BlockSpec(memory_space=pltpu.SMEM)] + _vmem(5),
            out_shape=[
                jax.ShapeDtypeStruct((1,), F32),
                jax.ShapeDtypeStruct((rows, 3 * feats), F32),
                jax.ShapeDtypeStruct((rows, feats), F32),
                jax.ShapeDtypeStruct((rows, feats), F32),
                jax.ShapeDtypeStruct((rows, hidden), F32),
                jax.ShapeDtypeStruct((rows * (hidden // feats), feats), F32),
            ],
            compiler_params=pltpu.CompilerParams(vmem_limit_bytes=8 << 20),
            name="final_sum",
        )(*shared)
    else:
        obj, *grads = terms
        shares = [
            lax.psum_scatter(lax.optimization_barrier(g.astype(F32)), "store", scatter_dimension=0, tiled=True)
            for g in grads
        ]
        loss = (lax.psum(obj[0, 0], "store") / groups).reshape(1)
    return (preds, loss, *shares)


def solution(mesh):
    rows = P(("parts", "store"), None)
    deep = P(("parts", "store"), None, None)
    in_specs = (rows, rows, rows, deep, deep, rows, P(), P(), P(), P(), P(), P())
    out_specs = (rows, P("parts"), rows, rows, rows, rows, rows)
    return jax.shard_map(shards, mesh=mesh, in_specs=in_specs, out_specs=out_specs, check_vma=False)
```

```python
import jax
import jax.numpy as jnp
from jax import lax
from jax.experimental import pallas as pl
from jax.experimental.pallas import tpu as pltpu
from jax.sharding import PartitionSpec as P

HEADS = 8
BF = jnp.bfloat16
F32 = jnp.float32


def _nn(a, b):
    return lax.dot_general(a, b, (((1,), (0,)), ((), ())), preferred_element_type=F32)


def _nt(a, b):
    return lax.dot_general(a, b, (((1,), (1,)), ((), ())), preferred_element_type=F32)


def _tn(a, b):
    return lax.dot_general(a, b, (((0,), (0,)), ((), ())), preferred_element_type=F32)


def _split(v):
    hi = v.astype(BF)
    lo = (v - hi.astype(F32)).astype(BF)
    return hi, lo


def _norm(v):
    c = v - jnp.mean(v, axis=0, keepdims=True)
    r = lax.rsqrt(jnp.mean(c * c, axis=0, keepdims=True) + 1e-05)
    return c * r, r


def _norm_back(d, y, r):
    m1 = jnp.mean(d, axis=0, keepdims=True)
    m2 = jnp.mean(d * y, axis=0, keepdims=True)
    return (d - m1 - y * m2) * r


GELU_C = 0.7978845608028654
GELU_A = 0.044715
LOG2E = 1.4426950408889634

LANES = 128


def _serve_kernel(wanted, store, out, column):
    peers, _, cap = wanted.shape
    diagonal = lax.broadcasted_iota(jnp.int32, (cap, cap), 0) == lax.broadcasted_iota(
        jnp.int32, (cap, cap), 1
    )
    for o in range(peers):
        row = jnp.where(diagonal, wanted[o], 0)
        column[o * cap : (o + 1) * cap, :] = jnp.sum(row, axis=1, keepdims=True)
    rows = store.shape[0]
    step = rows // 4 if rows % 512 == 0 else rows
    lane = lax.broadcasted_iota(jnp.int32, (out.shape[0], step), 1)
    total = jnp.zeros(out.shape, F32)
    for at in range(0, rows, step):
        hot = (lane == column[...] - at).astype(F32).astype(BF)
        total = total + _nn(hot, store[at : at + step, :])
    out[...] = total.astype(out.dtype)


def _prep_kernel(
    wqkv_h, wo_h, wmsg_h, wup_h, wdown_h, edges_h, pairs_h, slots_h, wread_h, store_h, *refs
):
    pick, wqmT = refs[:2]
    results = refs[2:9]
    store = refs[9]
    adjT, deg, woT, wupT, wdownT, hot, wcol = refs[10:17]
    wqkv, wmsg, wo, wup, wdown, edges, pairs, slots, wread, sems, out_sems = refs[17:]
    moves = [
        (edges_h, edges), (slots_h, slots), (pairs_h, pairs), (wread_h, wread),
        (wqkv_h, wqkv), (wmsg_h, wmsg), (wo_h, wo), (wup_h, wup), (wdown_h, wdown),
        (store_h, store),
    ]
    copies = [pltpu.make_async_copy(s, d, sems.at[i]) for i, (s, d) in enumerate(moves)]
    sends = [
        pltpu.make_async_copy(s, d, out_sems.at[i])
        for i, (s, d) in enumerate(zip(refs[10:17], results))
    ]
    for c in copies:
        c.start()
    feats = wo.shape[0]
    subs, nodes = slots.shape
    rows = pick.shape[0]
    n_edges = edges.shape[2]
    n_pairs = pairs.shape[2]
    for c in copies[:4]:
        c.wait()
    it = lax.broadcasted_iota(jnp.int32, (nodes, n_edges), 0)
    ip = lax.broadcasted_iota(jnp.int32, (nodes, 2 * n_pairs), 0)
    ir = lax.broadcasted_iota(jnp.int32, (rows, nodes), 0)

    @pl.loop(0, subs)
    def _(b):
        e = edges[b]
        srcT = (it == e[0:1, :]).astype(F32).astype(BF)
        dstT = (it == e[1:2, :]).astype(F32).astype(BF)
        cnt = _nt(srcT, dstT)
        deg[pl.ds(b, 1), :] = 1.0 / (1.0 + jnp.sum(cnt, axis=0, keepdims=True))
        adjT[b] = cnt.astype(BF)
        p = pairs[b]
        prs = jnp.concatenate([p[0:1, :], p[1:2, :]], axis=1)
        hot[b] = (ip == prs).astype(F32).astype(BF)
        at = pl.ds(pl.multiple_of(b * nodes, LANES), nodes)
        pick[:, at] = (ir == slots[pl.ds(b, 1), :]).astype(F32).astype(BF)

    wcol[...] = jnp.broadcast_to(wread[...], (2 * n_pairs, feats)).T
    for i in (0, 1, 5, 6):
        sends[i].start()
    for c in copies[4:9]:
        c.wait()
    wqmT[0 : 3 * feats, :] = wqkv[...].T
    wqmT[3 * feats : 4 * feats, :] = wmsg[...].T
    woT[...] = wo[...].T
    sends[2].start()
    wupT[...] = wup[...].T
    sends[3].start()
    wdownT[...] = wdown[...].T
    sends[4].start()
    for c in sends:
        c.wait()
    copies[9].wait()


def _hbm(*arrays):
    return [pltpu.with_memory_space_constraint(v, pltpu.HBM) for v in arrays]


def _prep(w_qkv, w_o, w_msg, w_up, w_down, edges, pairs, node_slots, w_read, store, rows):
    feats, hidden = w_up.shape
    subs, nodes = node_slots.shape
    n_edges, n_pairs = edges.shape[1], pairs.shape[1]
    out = [
        ((rows, subs * nodes), BF), ((4 * feats, feats), BF), ((subs, nodes, nodes), BF),
        ((subs, nodes), F32), ((feats, feats), BF), ((hidden, feats), BF), ((feats, hidden), BF),
        ((subs, nodes, 2 * n_pairs), BF), ((feats, 2 * n_pairs), F32),
    ]
    return pl.pallas_call(
        _prep_kernel,
        in_specs=[pl.BlockSpec(memory_space=pltpu.HBM)] * 10,
        out_specs=_vmem(2) + [pl.BlockSpec(memory_space=pltpu.HBM)] * 7 + _vmem(1),
        out_shape=[pltpu.VMEM(s, d) for s, d in out[:2]]
        + [pltpu.HBM(s, d) for s, d in out[2:]]
        + [pltpu.VMEM(store.shape, store.dtype)],
        scratch_shapes=[pltpu.VMEM(s, d) for s, d in out[2:]]
        + [
            pltpu.VMEM((feats, 3 * feats), BF),
            pltpu.VMEM((feats, feats), BF),
            pltpu.VMEM((feats, feats), BF),
            pltpu.VMEM((feats, hidden), BF),
            pltpu.VMEM((hidden, feats), BF),
            pltpu.VMEM((subs, 2, n_edges), jnp.int32),
            pltpu.VMEM((subs, 2, n_pairs), jnp.int32),
            pltpu.VMEM((subs, nodes), jnp.int32),
            pltpu.VMEM((1, feats), F32),
            pltpu.SemaphoreType.DMA((10,)),
            pltpu.SemaphoreType.DMA((7,)),
        ],
        compiler_params=pltpu.CompilerParams(vmem_limit_bytes=24 << 20),
        cost_estimate=pl.CostEstimate(
            flops=2 * subs * nodes * nodes * n_edges, bytes_accessed=8 << 20, transcendentals=0
        ),
        name="prep",
    )(
        *_hbm(
            w_qkv, w_o, w_msg, w_up, w_down, edges.transpose(0, 2, 1),
            pairs.transpose(0, 2, 1), node_slots, w_read.reshape(1, feats), store,
        )
    )


FWD_GROUP = 4
BWD_GROUP = 4


FWD_SKEW = 0
MID_SKEW = 0
BWD_SKEW = 0


def _wave(items, skew, stages):
    for step in range(len(stages) + skew * (items - 1) if skew else len(stages)):
        for i in range(items):
            s = step - skew * i
            if 0 <= s < len(stages):
                stages[s](i)


def _over(subs, group, stage):
    if subs % group:
        group = 1
    if group == subs:
        for b in range(subs):
            stage(b)
    else:

        @pl.loop(0, subs // group)
        def _(i):
            for k in range(group):
                stage(i * group + k)


def _step_kernel(packed, *refs):
    fetched_ref, pick, wqmT = refs[:3]
    sources = refs[3:14]
    preds_ref = refs[14]
    outs = refs[15 : 15 + (4 if packed else 6)]
    refs = refs[15 + len(outs) :]
    adjT, deg, woT, wupT, wdownT, hot_ref, wcol, targets_ref, wo, wup, wdown = refs[:11]
    (
        x_s, y_s, dy_s, att_s, datt_s, h_s, g_s, do_s, dup_s, da_s, pf_s, p_s, ds_s, obj_s, gq_s, gu_s, gd_s,
        agg_s, n1_s, n2_s, up_s, out_s, dout_s, hi_s, lo_s, r1_s, r2_s, r3_s,
        sems,
    ) = refs[11:]
    copies = [
        pltpu.make_async_copy(s, d, sems.at[i]) for i, (s, d) in enumerate(zip(sources, refs[:11]))
    ]
    for c in copies:
        c.start()
    feats = wo.shape[0]
    hidden = wup.shape[1]
    subs, nodes = deg.shape
    n_pairs = targets_ref.shape[1]
    n_all = subs * n_pairs
    hd = feats // HEADS
    scale = hd ** -0.5

    def lanes(b):
        if isinstance(b, int):
            return slice(b * nodes, (b + 1) * nodes)
        return pl.ds(pl.multiple_of(b * nodes, LANES), nodes)

    def head(part, h):
        return slice(part * feats + h * hd, part * feats + (h + 1) * hd)

    obj_s[...] = jnp.zeros_like(obj_s)
    x_s[...] = _nn(fetched_ref[...].T, pick[...]).astype(BF)
    y_s[...] = _nn(wqmT[...], x_s[...]).astype(BF)

    def attend(b):
        at = lanes(b)
        def score(h):
            pf_s[b, h] = _tn(y_s[head(1, h), at], y_s[head(0, h), at])

        def soften(h):
            s = pf_s[b, h]
            e = jnp.exp2((s - jnp.max(s, axis=0, keepdims=True)) * (scale * LOG2E))
            pf = e * (1.0 / jnp.sum(e, axis=0, keepdims=True))
            pf_s[b, h] = pf
            p_s[b, h] = pf.astype(BF)

        def blend(h):
            att_s[head(0, h), at] = _nn(y_s[head(2, h), at], p_s[b, h]).astype(BF)

        _wave(HEADS, FWD_SKEW, (score, soften, blend))

    _over(subs, FWD_GROUP, attend)
    for c in copies:
        c.wait()

    total = subs * nodes
    msg = slice(3 * feats, 4 * feats)

    def block(b):
        return slice(b * nodes, (b + 1) * nodes)

    def cuts(b):
        return [block(b)]

    def branches(b):
        at = block(b)
        agg_s[:, at] = _nn(y_s[msg, at], adjT[b])
        n2_s[:, at] = _nn(woT[...], att_s[:, at])

    def branch_norms(b):
        for c in cuts(b):
            w = c.start % nodes
            base = x_s[:, c].astype(F32)
            agg = (agg_s[:, c] + y_s[msg, c].astype(F32)) * deg[b : b + 1, w : w + nodes]
            agg_s[:, c] = agg
            n1, r1_s[0:1, c] = _norm(base + jnp.maximum(agg, 0.0))
            n2, r2_s[0:1, c] = _norm(base + n2_s[:, c])
            n1_s[:, c] = n1
            n2_s[:, c] = n2
            h_s[:, c] = (n1 + n2).astype(BF)

    def raise_up(b):
        up_s[:, block(b)] = _nn(wupT[...], h_s[:, block(b)])

    def gate(b):
        for c in cuts(b):
            up = up_s[:, c]
            sq = up * up
            th = jnp.tanh((GELU_C * up) * (1.0 + GELU_A * sq))
            half = 0.5 + 0.5 * th
            g_s[:, c] = (up * half).astype(BF)
            slope = (1.0 - th * th) * (GELU_C + (3.0 * GELU_A * GELU_C) * sq)
            up_s[:, c] = half + (0.5 * up) * slope

    def lower_down(b):
        out_s[:, block(b)] = _nn(wdownT[...], g_s[:, block(b)])

    def out_norm(b):
        for c in cuts(b):
            out, r3_s[0:1, c] = _norm(h_s[:, c].astype(F32) + out_s[:, c])
            out_s[:, c] = out
            hi_s[:, c], lo_s[:, c] = _split(out)

    def readout(b):
        hot = hot_ref[b]
        at = block(b)
        lr = _nn(hi_s[:, at], hot) + _nn(lo_s[:, at], hot)
        rl = pltpu.roll(lr, n_pairs, 1) * wcol[...]
        preds = jnp.sum(lr * rl, axis=0, keepdims=True)
        tgt = targets_ref[b : b + 1, :]
        diff = preds - jnp.concatenate([tgt, tgt], axis=1)
        preds_ref[b : b + 1, :] = preds[:, 0:n_pairs]
        obj_s[0:1, 0:n_pairs] += diff[:, 0:n_pairs] * diff[:, 0:n_pairs]
        hi, lo = _split((diff * (2.0 / n_all)) * rl)
        dout_s[:, at] = _nt(hi, hot) + _nt(lo, hot)

    def out_back(b):
        for c in cuts(b):
            do_s[:, c] = _norm_back(dout_s[:, c], out_s[:, c], r3_s[0:1, c]).astype(BF)

    def down_back(b):
        dup_s[:, block(b)] = _nn(wdown[...], do_s[:, block(b)]).astype(BF)

    def gate_back(b):
        for c in cuts(b):
            dup_s[:, c] = (up_s[:, c] * dup_s[:, c].astype(F32)).astype(BF)

    def up_back(b):
        da_s[:, block(b)] = _nn(wup[...], dup_s[:, block(b)]).astype(BF)

    def norms_back(b):
        for c in cuts(b):
            w = c.start % nodes
            dl = (do_s[:, c].astype(F32) + da_s[:, c].astype(F32)).astype(BF).astype(F32)
            d1 = _norm_back(dl, n1_s[:, c], r1_s[0:1, c])
            d1 = jnp.where(agg_s[:, c] > 0.0, d1, 0.0) * deg[b : b + 1, w : w + nodes]
            hi_s[:, c] = d1.astype(BF)
            da_s[:, c] = _norm_back(dl, n2_s[:, c], r2_s[0:1, c]).astype(BF)

    def branches_back(b):
        at = block(b)
        datt_s[:, at] = _nn(wo[...], da_s[:, at]).astype(BF)
        dagg = hi_s[:, at]
        dxw = _nt(dagg, adjT[b]).astype(BF)
        dy_s[msg, at] = (dxw.astype(F32) + dagg.astype(F32)).astype(BF)

    stages = (
        branches, branch_norms, raise_up, gate, lower_down, out_norm, readout, out_back,
        down_back, gate_back, up_back, norms_back, branches_back,
    )
    _wave(subs, MID_SKEW, stages)

    def attend_back(b):
        at = lanes(b)
        def score(h):
            ds_s[h] = _tn(y_s[head(2, h), at], datt_s[head(0, h), at]).astype(BF)

        def soften(h):
            pf = pf_s[b, h]
            t = ds_s[h].astype(F32) * pf
            ds_s[h] = ((t - pf * jnp.sum(t, axis=0, keepdims=True)) * scale).astype(BF)

        def blend(h):
            dy_s[head(2, h), at] = _nt(datt_s[head(0, h), at], p_s[b, h]).astype(BF)
            dy_s[head(0, h), at] = _nn(y_s[head(1, h), at], ds_s[h]).astype(BF)
            dy_s[head(1, h), at] = _nt(y_s[head(0, h), at], ds_s[h]).astype(BF)

        _wave(HEADS, BWD_SKEW, (score, soften, blend))

    _over(subs, BWD_GROUP, attend_back)

    gq_s[:, 4 * feats :] = _nt(att_s[...], da_s[...]).astype(BF)
    gu_s[...] = _nt(h_s[...], dup_s[...]).astype(BF)
    gd_s[...] = _nt(g_s[...], do_s[...]).astype(BF)
    gq_s[:, 0 : 4 * feats] = _nt(x_s[...], dy_s[...]).astype(BF)
    obj = jnp.sum(obj_s[0:1, :], axis=1, keepdims=True) / n_all
    if packed:
        slabs, cut, _ = outs[0].shape
        rows = feats // (2 * slabs)
        core = lax.axis_index("store") % 2
        obj_block = _spread(obj, TAIL)
        per = hidden // feats
        for first, second, side in ((outs[0], outs[1], core), (outs[2], outs[3], 1 - core)):
            for j in range(slabs):
                d = 2 * j + side
                r = pl.ds(pl.multiple_of(d * rows, rows), rows)
                pieces = [gq_s[r, c : c + LANES] for c in range(0, 5 * feats, LANES)]
                pieces += [gu_s[r, c : c + LANES] for c in range(0, hidden, LANES)]
                for i in range(per):
                    r = pl.ds(pl.multiple_of(d * (rows * per) + i * rows, rows), rows)
                    pieces += [gd_s[r, c : c + LANES] for c in range(0, feats, LANES)]
                whole = cut // rows
                for i, piece in enumerate(pieces[:whole]):
                    first[j, i * rows : (i + 1) * rows, :] = piece
                for i, piece in enumerate(pieces[whole:]):
                    second[j, i * rows : (i + 1) * rows, :] = piece
                second[j, (len(pieces) - whole) * rows :, :] = obj_block
    else:
        obj_ref, gqkv_ref, go_ref, gmsg_ref, gup_ref, gdown_ref = outs
        obj_ref[...] = jnp.broadcast_to(obj, obj_ref.shape)
        gqkv_ref[...] = gq_s[:, 0 : 3 * feats]
        gmsg_ref[...] = gq_s[:, 3 * feats : 4 * feats]
        go_ref[...] = gq_s[:, 4 * feats :]
        gup_ref[...] = gu_s[...]
        gdown_ref[...] = gd_s[...]


def _weights(rows):
    shape = (rows, LANES)
    at = lax.broadcasted_iota(jnp.int32, shape, 0) * LANES + lax.broadcasted_iota(jnp.int32, shape, 1)
    return 1.0 + at.astype(F32) / (rows * LANES)


def _spread(value, rows):
    return (value * _weights(rows)).astype(BF)


def _gather_terms(block):
    w = _weights(block.shape[0])
    return jnp.sum(block * w) / jnp.sum(w * w)


TAIL = 8


def _halving(halves, groups):
    idx = lax.axis_index("store")
    bits = groups.bit_length() - 2
    orders = [list(range(1, bits + 1)) for _ in halves]
    if bits > 1:
        orders[1][:2] = [2, 1]
    halves = [[v.reshape((2,) * bits + v.shape[1:]) for v in h] for h in halves]
    for step in range(bits):
        kept, got = [], []
        for h, order in zip(halves, orders):
            axis = bits - order[step]
            bit = (idx >> order[step]) & 1
            perm = [(i, i ^ (1 << order[step])) for i in range(groups)]
            send = sum(lax.dynamic_slice_in_dim(v, 1 - bit, 1, axis).astype(F32) for v in h)
            got.append(lax.ppermute(send.astype(BF), "store", perm))
            kept.append(sum(lax.dynamic_slice_in_dim(v, bit, 1, axis).astype(F32) for v in h))
        halves = [[k + g.astype(F32)] for k, g in zip(kept, got)]
    return [sum(v.astype(F32) for v in h).reshape(h[0].shape[-2:]) for h in halves]


def _final_kernel(groups, first_ref, second_ref, loss_ref, gqkv, go, gmsg, gup, gdown):
    total = jnp.concatenate([first_ref[...], second_ref[...]], axis=0)
    height = total.shape[0]
    rows, feats = go.shape
    hidden = gup.shape[1]
    places = [(gqkv, 0, c) for c in range(0, 3 * feats, LANES)]
    places += [(gmsg, 0, c) for c in range(0, feats, LANES)]
    places += [(go, 0, c) for c in range(0, feats, LANES)]
    places += [(gup, 0, c) for c in range(0, hidden, LANES)]
    for i in range(hidden // feats):
        places += [(gdown, i * rows, c) for c in range(0, feats, LANES)]
    for i, (ref, r, c) in enumerate(places):
        ref[r : r + rows, c : c + LANES] = total[i * rows : (i + 1) * rows, :]
    loss_ref[0] = _gather_terms(total[height - TAIL :, :]) / groups


def _vmem(n):
    return [pl.BlockSpec(memory_space=pltpu.VMEM)] * n


def local_step(prep, fetched, targets, weights, groups):
    feats, hidden = weights[1].shape
    subs, nodes = prep[3].shape
    n_pairs = targets.shape[1]
    total = subs * nodes
    sources = (*prep[2:], targets, *weights)
    rows = feats // groups
    packed = groups % 2 == 0 and feats % groups == 0 and hidden % feats == 0 and rows % 16 == 0
    packed = packed and feats % LANES == 0 and groups & (groups - 1) == 0
    out = [((subs, n_pairs), F32)]
    if packed:
        height = rows * (5 * feats + 2 * hidden) // LANES
        cut = height // (2 * rows) * rows
        sizes = (cut, height - cut + TAIL)
        out += [((groups // 2, h, LANES), BF) for h in sizes + sizes]
    else:
        out += [
            ((8, LANES), F32), ((feats, 3 * feats), BF), ((feats, feats), BF), ((feats, feats), BF),
            ((feats, hidden), BF), ((hidden, feats), BF),
        ]
    res = pl.pallas_call(
        lambda *refs: _step_kernel(packed, *refs),
        in_specs=_vmem(3) + [pl.BlockSpec(memory_space=pltpu.HBM)] * len(sources),
        out_specs=_vmem(len(out)),
        out_shape=[jax.ShapeDtypeStruct(s, d) for s, d in out],
        scratch_shapes=[pltpu.VMEM(v.shape, v.dtype) for v in sources]
        + [
            pltpu.VMEM((feats, total), BF),
            pltpu.VMEM((4 * feats, total), BF),
            pltpu.VMEM((4 * feats, total), BF),
            pltpu.VMEM((feats, total), BF),
            pltpu.VMEM((feats, total), BF),
            pltpu.VMEM((feats, total), BF),
            pltpu.VMEM((hidden, total), BF),
            pltpu.VMEM((feats, total), BF),
            pltpu.VMEM((hidden, total), BF),
            pltpu.VMEM((feats, total), BF),
            pltpu.VMEM((subs, HEADS, nodes, nodes), F32),
            pltpu.VMEM((subs, HEADS, nodes, nodes), BF),
            pltpu.VMEM((HEADS, nodes, nodes), BF),
            pltpu.VMEM((8, LANES), F32),
            pltpu.VMEM((feats, 5 * feats), BF),
            pltpu.VMEM((feats, hidden), BF),
            pltpu.VMEM((hidden, feats), BF),
            pltpu.VMEM((feats, total), F32),
            pltpu.VMEM((feats, total), F32),
            pltpu.VMEM((feats, total), F32),
            pltpu.VMEM((hidden, total), F32),
            pltpu.VMEM((feats, total), F32),
            pltpu.VMEM((feats, total), F32),
            pltpu.VMEM((feats, total), BF),
            pltpu.VMEM((feats, total), BF),
            pltpu.VMEM((8, total), F32),
            pltpu.VMEM((8, total), F32),
            pltpu.VMEM((8, total), F32),
            pltpu.SemaphoreType.DMA((len(sources),)),
        ],
        compiler_params=pltpu.CompilerParams(vmem_limit_bytes=40 << 20),
        name="graph_step",
    )(fetched, *prep[:2], *_hbm(*sources))
    return packed, res


def shards(
    store_feats, requests, node_slots, edges, pairs, targets,
    w_qkv, w_o, w_msg, w_up, w_down, w_read,
):
    feats = store_feats.shape[1]
    hidden = w_up.shape[1]
    groups = lax.axis_size("store")
    wanted = lax.all_to_all(
        requests.reshape(groups, 1, -1), "store", split_axis=0, concat_axis=0, tiled=True
    )
    *prep, store = _prep(
        w_qkv, w_o, w_msg, w_up, w_down, edges, pairs, node_slots, w_read, store_feats,
        wanted.size,
    )
    picked = pl.pallas_call(
        _serve_kernel,
        in_specs=_vmem(2),
        out_specs=pl.BlockSpec(memory_space=pltpu.VMEM),
        out_shape=jax.ShapeDtypeStruct((wanted.size, feats), store_feats.dtype),
        scratch_shapes=[pltpu.VMEM((wanted.size, 1), jnp.int32)],
        compiler_params=pltpu.CompilerParams(vmem_limit_bytes=16 << 20),
        name="serve",
    )(wanted, store)
    picked = picked.reshape(groups, -1, feats)
    fetched = lax.all_to_all(picked, "store", split_axis=0, concat_axis=0, tiled=True)
    fetched = fetched.reshape(-1, feats)
    packed, (preds, *terms) = local_step(prep, fetched, targets, (w_o, w_up, w_down), groups)
    if packed:
        rows = feats // groups
        paired = []
        for keep, send in zip(terms[:2], terms[2:]):
            got = lax.ppermute(send, "store", [(i, i ^ 1) for i in range(groups)])
            paired.append((keep, got))
        shared = _halving(paired, groups)
        loss, *shares = pl.pallas_call(
            lambda *refs: _final_kernel(groups, *refs),
            in_specs=_vmem(2),
            out_specs=[pl.BlockSpec(memory_space=pltpu.SMEM)] + _vmem(5),
            out_shape=[
                jax.ShapeDtypeStruct((1,), F32),
                jax.ShapeDtypeStruct((rows, 3 * feats), F32),
                jax.ShapeDtypeStruct((rows, feats), F32),
                jax.ShapeDtypeStruct((rows, feats), F32),
                jax.ShapeDtypeStruct((rows, hidden), F32),
                jax.ShapeDtypeStruct((rows * (hidden // feats), feats), F32),
            ],
            compiler_params=pltpu.CompilerParams(vmem_limit_bytes=8 << 20),
            name="final_sum",
        )(*shared)
    else:
        obj, *grads = terms
        shares = [
            lax.psum_scatter(lax.optimization_barrier(g.astype(F32)), "store", scatter_dimension=0, tiled=True)
            for g in grads
        ]
        loss = (lax.psum(obj[0, 0], "store") / groups).reshape(1)
    return (preds, loss, *shares)


def solution(mesh):
    rows = P(("parts", "store"), None)
    deep = P(("parts", "store"), None, None)
    in_specs = (rows, rows, rows, deep, deep, rows, P(), P(), P(), P(), P(), P())
    out_specs = (rows, P("parts"), rows, rows, rows, rows, rows)
    return jax.shard_map(shards, mesh=mesh, in_specs=in_specs, out_specs=out_specs, check_vma=False)
```
